256 devices in a mesh: group: 32 (over x, z), expert: 8 (over y, core).
Axes of the slice: x: 4, y: 4, z: 8, core: 2. Of those that a mesh axis runs over, the one named last changes fastest.
Arguments:
- hidden_in: bfloat16 [16384, 2048], P(('group', 'expert')), may hold values from -6 to 6
- cache_len: int32 [32], replicated, may hold values from 1 to 2048, 32768 in all
- page_table: int32 [32, 128], replicated, may hold values from 0 to 4095, as said below
- pool: bfloat16 [4096, 2, 16, 2048], P('group', None, None, 'expert'), may hold values from -200 to 200
- attn_gain: float32 [2048], replicated, may hold values from 0.1 to 1.9
- w_qkv: bfloat16 [2048, 3, 2048], P(None, None, 'expert'), may hold values from -0.125 to 0.125
- w_out: bfloat16 [2048, 2048], P('expert'), may hold values from -0.125 to 0.125
- moe_gain: float32 [2048], replicated, may hold values from 0.1 to 1.9
- w_gate: bfloat16 [8, 2048, 512], P('expert'), may hold values from -0.125 to 0.125
- w_up: bfloat16 [8, 2048, 512], P('expert'), may hold values from -0.125 to 0.125
- w_down: bfloat16 [8, 512, 2048], P('expert'), may hold values from -0.25 to 0.25
- expert_ids: int32 [16384, 2], P(('group', 'expert')), may hold values from 0 to 7, all different within a row; in each aligned block of 64 rows (0 to 63, 64 to 127, ...) at most 32 rows name the same one
- gate_weights: float32 [16384, 2], P(('group', 'expert')), may hold values from 0.05 to 0.8
Outputs:
- hidden_out: float32 [16384, 2048], P(('group', 'expert'))
The draws below stay inside these ranges and needn't reach their ends.
Inputs may be any that keep to these rules, and one draw needn't show every extreme that they name: `cache_len`: the longest request holds exactly 2048 cached tokens. `page_table`: every pool page is named exactly once; rows g * 128 to (g + 1) * 128 - 1 of the pool form group g's part, and each group's part that holds pages of a request holds exactly 8 of them. `expert_ids`: a token names 2 different experts; within the rows of one device no expert is named more than 32 times.
All inputs are finite; a program needn't handle non-finite values.
Results may differ from the reference program's by a relative error of at most 0.012.
The reference program's roundings to bfloat16 on the way count: a program that leaves them out, or rounds other values in their place, can miss the bound.
Values may be sent and summed in bfloat16 or wider, within the bound.
A program may use at most 128 MiB of HBM per device.

```python
import math
import jax
import jax.numpy as jnp
import numpy as np
from jax import lax

D = 2048
HEADS = 16
HEAD_DIM = 128
FFE = 512
TOPK = 2
PAGE = 16
NEW = 512
CTX = 2048
REQS = 32
EXPERTS = 8
HH = 2048
TOKENS = 16384
TOK_DEV = 64
PPR = 128
POOL = 4096
MOST = 8
CAP = 32
N_GROUP = 32
N_EXPERT = 8


def draw_page_table(key, part):
    streams = jax.random.split(jax.random.fold_in(key, 11), 5)
    row_perm = jax.random.permutation(streams[0], REQS)
    owner_perm = jax.random.permutation(streams[1], REQS)
    offset_perm = jax.random.permutation(streams[2], REQS)
    page_perms = jax.vmap(lambda stream: jax.random.permutation(stream, PPR))(jax.random.split(streams[3], REQS))
    block_index = page_perms // MOST
    owner_group = owner_perm[(row_perm[:, None] + offset_perm[block_index]) % REQS]
    slot_perms = jax.vmap(lambda stream: jax.random.permutation(stream, PPR))(jax.random.split(streams[4], REQS))
    slot_index = slot_perms[owner_group, page_perms]
    return (owner_group * PPR + slot_index).astype(jnp.int32)


def draw_pool(key, part):
    streams = jax.random.split(jax.random.fold_in(key, 23), 1)
    base_draw = jax.random.normal(streams[0], (POOL, 2, PAGE, HH), jnp.float32)
    key_part = jnp.clip(base_draw[:, 0:1] * 3.0, -12.0, 12.0)
    value_part = jnp.clip(base_draw[:, 1:2], -4.0, 4.0)
    return jnp.concatenate([key_part, value_part], axis=1).astype(jnp.bfloat16)


def block_scale(stream_key, extent, cuts, least, top_value):
    gain = 1.0
    for dim, blocks in cuts:
        draws = jax.random.uniform(jax.random.fold_in(jax.random.fold_in(stream_key, 6), dim), (blocks,), jnp.float32, least / len(cuts), top_value / len(cuts))
        gain = gain * jnp.repeat(jnp.exp(draws), extent[dim] // blocks).reshape((-1,) + (1,) * (len(extent) - 1 - dim))
    return gain


def profile(amount, total, reach, lean):
    weights = [(1 << 20) // math.isqrt(rank ** lean) + 1 for rank in range(2, amount + 1)]
    surplus, counts = total - reach - (amount - 1), [1] * (amount - 1)
    while surplus > 0:
        free = [i for i in range(amount - 1) if counts[i] < reach]
        whole, remaining = sum([weights[i] for i in free]), surplus
        for i in free:
            more = min(reach - counts[i], max(1, remaining * weights[i] // whole), surplus)
            counts[i] = counts[i] + more
            surplus = surplus - more
    return np.array([reach] + counts)


def ragged_sizes(stream_key, number_of, total, reach, skew):
    if number_of == 2:
        one = jax.random.randint(stream_key, (), max(1, total - reach), min(reach, total - 1) + 1)
        return jnp.stack([one, total - one])
    sizes = jnp.asarray(profile(number_of, total, reach, skew), jnp.int32)
    pairs = (number_of - 1) // 2
    donor, taker = sizes[1:1 + 2 * pairs:2], sizes[2:2 + 2 * pairs:2]
    margin = jnp.minimum(donor - 1, reach - taker)
    shifted = jax.random.randint(jax.random.fold_in(stream_key, 1), (pairs,), 0, 1 << 20) % (margin + 1)
    sizes = sizes.at[1:1 + 2 * pairs:2].set(donor - shifted).at[2:2 + 2 * pairs:2].set(taker + shifted)
    return sizes[jax.random.permutation(jax.random.fold_in(stream_key, 2), number_of)]


def routed_block(rng, own, number, rows, amount, top, most, slope):
    ranking = jax.random.permutation(rng, amount)
    packed, common = shares(amount, rows * top, most, slope, True), shares(amount, rows * top, most, slope, False)
    places = jnp.arange(amount)

    def named(sizes, rotation):
        used = int((sizes > 0).sum())
        fixed = max(1, used // 4)
        passed = fixed + (places - fixed + rotation * (used - fixed)) % max(1, amount - fixed)
        return jnp.zeros((amount,), jnp.int32).at[ranking[jnp.where(places < fixed, places, passed)]].set(jnp.asarray(sizes, jnp.int32))

    sizes = jnp.where(number % 4 == 0, named(packed, number // 4), named(common, number - number // 4 - 1))
    mixed = jax.random.permutation(jax.random.fold_in(own, 3), amount)
    donor, sink = mixed[0:amount // 2 * 2:2], mixed[1:amount // 2 * 2:2]
    margin = jnp.minimum(sizes[donor] - 1, most - sizes[sink]) // 2
    margin = jnp.where((donor == ranking[0]) | (sink == ranking[0]) | (sizes[sink] == 0), 0, jnp.maximum(margin, 0))
    passed = jax.random.randint(jax.random.fold_in(own, 4), (amount // 2,), 0, 1 << 20) % (margin + 1)
    sizes = sizes.at[donor].add(-passed).at[sink].add(passed)
    members = jnp.searchsorted(jnp.cumsum(sizes), jnp.arange(rows * top), side="right").astype(jnp.int32)
    grid = members.reshape(top, rows).T
    grid = grid[jax.random.permutation(jax.random.fold_in(own, 1), rows)]
    rotation = jax.random.randint(jax.random.fold_in(own, 2), (rows, 1), 0, top)
    return jnp.take_along_axis(grid, (jnp.arange(top)[None, :] + rotation) % top, axis=1)


def shares(number_of, total, limit, slope, full):
    weights = [(1 << 20) // math.isqrt(grade ** slope) + 1 for grade in range(1, number_of + 1)]
    largest = limit if full else min(limit, max(-(-total // number_of), total * weights[0] // sum(weights)))
    least = 1 if total - largest >= number_of - 1 else 0
    counts, rest = [largest] + [least] * (number_of - 1), total - largest - least * (number_of - 1)
    while rest > 0:
        movable = [i for i in range(1, number_of) if counts[i] < largest] or [i for i in range(1, number_of) if counts[i] < limit]
        whole, budget = sum([weights[i] for i in movable]), rest
        for i in movable:
            more = min(limit - counts[i], max(1, budget * weights[i] // whole), rest)
            counts[i] = counts[i] + more
            rest = rest - more
    return np.array(counts)


def centred(stream_key, dims, width, reach, cuts=(), dtype=jnp.bfloat16):
    result = width * jax.random.normal(stream_key, dims, jnp.float32)
    if cuts:
        result = result * block_scale(stream_key, dims, cuts, -0.22, 0.18)
    return jnp.clip(result, -reach, reach).astype(dtype)


def setup_inputs(seed: int = 0) -> dict:
    seeds = jax.random.split(jax.random.key(seed), 14)
    hidden_in = centred(seeds[0], (TOKENS, D), 1.0, 6.0, ((0, 256),))
    cache_len = ragged_sizes(seeds[1], REQS, REQS * CTX // 2, CTX, 2).astype(jnp.int32)
    page_table = draw_page_table(jax.random.fold_in(seeds[13], 71), 0)
    pool = draw_pool(jax.random.fold_in(seeds[13], 71), 0)
    attn_gain = jnp.clip(1.0 + 0.18 * jax.random.normal(seeds[4], (D,), jnp.float32), 0.1, 1.9)
    w_qkv = centred(seeds[5], (D, 3, HH), D ** -0.5, 0.125, ((2, 8),))
    w_out = centred(seeds[6], (HH, D), HH ** -0.5, 0.125, ((0, 8),))
    moe_gain = jnp.clip(1.0 + 0.18 * jax.random.normal(seeds[7], (D,), jnp.float32), 0.1, 1.9)
    w_gate = centred(seeds[8], (EXPERTS, D, FFE), D ** -0.5, 0.125, ((0, 8),))
    w_up = centred(seeds[9], (EXPERTS, D, FFE), D ** -0.5, 0.125, ((0, 8),))
    w_down = centred(seeds[10], (EXPERTS, FFE, D), FFE ** -0.5, 0.25, ((0, 8),))
    expert_ids_keys = jax.random.split(jax.random.fold_in(seeds[11], 1), TOKENS // TOK_DEV)
    expert_ids_turns = jax.random.permutation(jax.random.fold_in(seeds[11], 3), TOKENS // TOK_DEV)
    expert_ids = jax.vmap(lambda own, number: routed_block(jax.random.fold_in(seeds[11], 2), own, number, TOK_DEV, EXPERTS, TOPK, CAP, 2))(expert_ids_keys, expert_ids_turns).reshape((TOKENS, TOPK))
    gate_weights = jnp.clip(jnp.exp(math.log(0.8) - 2.7725887 * jax.random.uniform(seeds[12], (TOKENS, TOPK), jnp.float32) ** block_scale(seeds[12], (TOKENS, TOPK), ((0, 256),), -0.2, 0.2)), 0.05, 0.8)
    return {"hidden_in": hidden_in, "cache_len": cache_len, "page_table": page_table, "pool": pool, "attn_gain": attn_gain, "w_qkv": w_qkv, "w_out": w_out, "moe_gain": moe_gain, "w_gate": w_gate, "w_up": w_up, "w_down": w_down, "expert_ids": expert_ids, "gate_weights": gate_weights}


def norm_rows(inputs, gain_vector):
    values = inputs.astype(jnp.float32)
    factor = lax.rsqrt(lax.optimization_barrier(jnp.mean(values * values, axis=-1, keepdims=True)) + 1e-05)
    return (values * factor * gain_vector.astype(jnp.float32)).astype(jnp.bfloat16)

def rotate(vectors, positions):
    half_dim = vectors.shape[-1] // 2
    frequency = 10000.0 ** (-jnp.arange(half_dim).astype(jnp.float32) / half_dim)
    angles = positions[:, None] * frequency[None, :]
    cosine = jnp.cos(angles)[:, None, :]
    sine_part = jnp.sin(angles)[:, None, :]
    first_half = vectors[..., :half_dim]
    second_half = vectors[..., half_dim:]
    return jnp.concatenate([first_half * cosine - second_half * sine_part, first_half * sine_part + second_half * cosine], axis=-1)

def reference(hidden_in, cache_len, page_table, pool, attn_gain, w_qkv, w_out, moe_gain, w_gate, w_up, w_down, expert_ids, gate_weights):
    head_width = HEADS * HEAD_DIM
    score_scale = HEAD_DIM ** (-0.5)
    projection = w_qkv.reshape(D, 3 * head_width)
    group_width = head_width // N_EXPERT

    def one_request(request_item):
        token_rows, length, page_list = request_item
        normed = norm_rows(token_rows, attn_gain)
        projected = jnp.dot(normed, projection, preferred_element_type=jnp.float32).reshape(NEW, 3, HEADS, HEAD_DIM)
        positions = (length + jnp.arange(NEW).astype(jnp.int32)).astype(jnp.float32)
        queries = rotate(projected[:, 0], positions).astype(jnp.bfloat16)
        new_keys = rotate(projected[:, 1], positions).astype(jnp.bfloat16)
        new_values = projected[:, 2].astype(jnp.bfloat16)
        page_data = pool[page_list]
        all_keys = jnp.concatenate([page_data[:, 0].reshape(CTX, HEADS, HEAD_DIM), new_keys], axis=0)
        all_values = jnp.concatenate([page_data[:, 1].reshape(CTX, HEADS, HEAD_DIM), new_values], axis=0)
        scores = jnp.einsum('qhd,khd->hqk', queries.astype(jnp.float32), all_keys.astype(jnp.float32)) * score_scale
        column = jnp.arange(CTX + NEW).astype(jnp.int32)
        row_index = jnp.arange(NEW).astype(jnp.int32)
        key_valid = jnp.where(column[None, :] < CTX, column[None, :] < length, column[None, :] - CTX <= row_index[:, None])
        scores = jnp.where(key_valid[None], scores, -1e+30)
        row_peak = lax.optimization_barrier(jnp.max(scores, axis=-1, keepdims=True))
        weights = jnp.exp(scores - row_peak)
        row_total = lax.optimization_barrier(jnp.sum(weights, axis=-1))
        probs = lax.optimization_barrier(weights.astype(jnp.bfloat16))
        mixed = jnp.einsum('hqk,khd->qhd', probs.astype(jnp.float32), all_values.astype(jnp.float32))
        attended = (mixed / jnp.transpose(row_total)[:, :, None]).astype(jnp.bfloat16).reshape(NEW, head_width)
        head_parts = jnp.einsum('tec,ecd->ted', attended.reshape(NEW, N_EXPERT, group_width).astype(jnp.float32), w_out.reshape(N_EXPERT, group_width, D).astype(jnp.float32))
        head_parts = lax.optimization_barrier(head_parts.astype(jnp.bfloat16))
        head_sum = lax.optimization_barrier(jnp.sum(head_parts.astype(jnp.float32), axis=1))
        return token_rows.astype(jnp.float32) + head_sum
    residual = lax.map(one_request, (hidden_in.reshape(REQS, NEW, D), cache_len, page_table)).reshape(TOKENS, D)
    moe_in = norm_rows(residual, moe_gain)
    rows_bound = CAP * N_GROUP * N_EXPERT

    def one_expert(combined, expert_item):
        gate_matrix, up_matrix, down_matrix, number = expert_item
        hits = expert_ids == number
        chosen = jnp.any(hits, axis=1)
        weight = lax.optimization_barrier(jnp.sum(jnp.where(hits, gate_weights, 0.0), axis=1))
        picked = jnp.nonzero(chosen, size=rows_bound, fill_value=0)[0].astype(jnp.int32)
        live_rows = jnp.arange(rows_bound).astype(jnp.int32) < jnp.sum(chosen.astype(jnp.int32))
        inputs = moe_in[picked]
        gate_part = jnp.dot(inputs, gate_matrix, preferred_element_type=jnp.float32)
        up_part = jnp.dot(inputs, up_matrix, preferred_element_type=jnp.float32)
        hidden = (jax.nn.silu(gate_part) * up_part).astype(jnp.bfloat16)
        expert_out = jnp.dot(hidden, down_matrix, preferred_element_type=jnp.float32).astype(jnp.bfloat16)
        contribution = jnp.where(live_rows, weight[picked], 0.0)[:, None] * expert_out.astype(jnp.float32)
        return (combined.at[picked].add(contribution), None)
    combined, unused = lax.scan(one_expert, jnp.zeros((TOKENS, D), jnp.float32), (w_gate, w_up, w_down, jnp.arange(EXPERTS).astype(jnp.int32)))
    return residual + combined
```

```python
import jax
import jax.numpy as jnp
from jax import lax
from jax.sharding import PartitionSpec as P

HEAD_DIM = 128
NBLK = 8
CTX = 2048


def norm_rows(inputs, gain_vector):
    values = inputs.astype(jnp.float32)
    factor = lax.rsqrt(jnp.mean(values * values, axis=-1, keepdims=True) + 1e-05)
    return (values * factor * gain_vector).astype(jnp.bfloat16)


def rotate(vectors, positions):
    half_dim = vectors.shape[-1] // 2
    frequency = 10000.0 ** (-jnp.arange(half_dim).astype(jnp.float32) / half_dim)
    angles = positions[:, None] * frequency[None, :]
    cosine = jnp.cos(angles)[:, None, :]
    sine_part = jnp.sin(angles)[:, None, :]
    first_half = vectors[..., :half_dim]
    second_half = vectors[..., half_dim:]
    return jnp.concatenate(
        [
            first_half * cosine - second_half * sine_part,
            first_half * sine_part + second_half * cosine,
        ],
        axis=-1,
    )


def attend_block(softmax_state, queries, key_block, value_block, key_valid):
    old_peak, old_total, old_mixed = softmax_state
    score_scale = queries.shape[-1] ** (-0.5)
    scores = (
        jnp.einsum("qhd,khd->hqk", queries, key_block, preferred_element_type=jnp.float32)
        * score_scale
    )
    scores = jnp.where(key_valid[None], scores, -1e30)
    new_peak = jnp.maximum(old_peak, jnp.max(scores, axis=-1))
    weights = jnp.exp(scores - new_peak[..., None])
    factor = jnp.exp(old_peak - new_peak)
    new_total = old_total * factor + jnp.sum(weights, axis=-1)
    new_mixed = old_mixed * factor[..., None] + jnp.einsum(
        "hqk,khd->hqd",
        weights.astype(jnp.bfloat16),
        value_block,
        preferred_element_type=jnp.float32,
    )
    return (new_peak, new_total, new_mixed)


def cache_pass(
    softmax_state,
    queries,
    all_keys,
    all_values,
    length,
    turn_count,
    array_step,
    array_first,
    position_step,
    position_first,
    block_len,
):

    def step_once(turn_index, running):
        array_start = (array_first + array_step * turn_index) * block_len
        position_start = (position_first + position_step * turn_index) * block_len
        key_block = lax.dynamic_slice_in_dim(all_keys, array_start, block_len, 0)
        value_block = lax.dynamic_slice_in_dim(all_values, array_start, block_len, 0)
        key_valid = (position_start + jnp.arange(block_len, dtype=jnp.int32) < length)[None, :]
        return attend_block(running, queries, key_block, value_block, key_valid)

    return lax.fori_loop(0, turn_count, step_once, softmax_state)


def shards(
    hidden_in,
    cache_len,
    page_table,
    pool,
    attn_gain,
    w_qkv,
    w_out,
    moe_gain,
    w_gate,
    w_up,
    w_down,
    expert_ids,
    gate_weights,
):
    groups = lax.axis_size("group")
    expert_lanes = lax.axis_size("expert")
    group_index = lax.axis_index("group")
    tok_rows = hidden_in.shape[0]
    model_width = hidden_in.shape[1]
    local_width = w_out.shape[0]
    head_size = HEAD_DIM
    local_heads = local_width // head_size
    new_count = tok_rows * expert_lanes
    block_len = CTX // NBLK
    length = cache_len[group_index]
    normed = norm_rows(hidden_in, attn_gain)
    projection = w_qkv.reshape(model_width, 3 * local_width)
    projected = jnp.dot(
        lax.all_gather(normed, "expert", axis=0, tiled=True),
        projection,
        preferred_element_type=jnp.float32,
    )
    projected = projected.reshape(new_count, 3, local_heads, head_size)
    positions = (length + jnp.arange(new_count, dtype=jnp.int32)).astype(jnp.float32)
    queries = rotate(projected[:, 0], positions).astype(jnp.bfloat16)
    new_keys = rotate(projected[:, 1], positions).astype(jnp.bfloat16)
    new_values = projected[:, 2].astype(jnp.bfloat16)
    pages_per = page_table.shape[1]
    page_most = max(1, pages_per // min(groups, 16))
    owner_group = page_table // pages_per
    local_slot = page_table % pages_per
    page_order = jnp.arange(pages_per, dtype=jnp.int32)
    mine = (owner_group == group_index).astype(jnp.int32)
    mine_rank = jnp.cumsum(mine, axis=1) - mine
    slot_ids = jnp.arange(page_most, dtype=jnp.int32)
    pick = (mine[:, None, :] > 0) & (mine_rank[:, None, :] == slot_ids[None, :, None])
    send_index = jnp.sum(jnp.where(pick, local_slot[:, None, :], 0), axis=-1)
    outgoing = pool[send_index]
    arrived = lax.all_to_all(outgoing, "group", split_axis=0, concat_axis=0, tiled=True)
    arrived = arrived.reshape((groups * page_most,) + pool.shape[1:])
    my_owner = owner_group[group_index]
    before = page_order[None, :] < page_order[:, None]
    my_rank = jnp.sum(jnp.logical_and(my_owner[:, None] == my_owner[None, :], before), axis=-1)
    cache_pages = arrived[my_owner * page_most + my_rank]
    cache_keys = cache_pages[:, 0].reshape(CTX, local_heads, head_size)
    cache_values = cache_pages[:, 1].reshape(CTX, local_heads, head_size)
    row_order = jnp.arange(new_count, dtype=jnp.int32)
    causal = row_order[None, :] <= row_order[:, None]
    start_state = (
        jnp.full((local_heads, new_count), -1e30, jnp.float32),
        jnp.zeros((local_heads, new_count), jnp.float32),
        jnp.zeros((local_heads, new_count, head_size), jnp.float32),
    )
    softmax_state = attend_block(start_state, queries, new_keys, new_values, causal)
    block_count = (length + block_len - 1) // block_len
    softmax_state = cache_pass(
        softmax_state, queries, cache_keys, cache_values, length, block_count, 1, 0, 1, 0, block_len
    )
    row_total = softmax_state[1]
    row_mixed = softmax_state[2]
    attended = (
        jnp.transpose(row_mixed / row_total[..., None], (1, 0, 2))
        .reshape(new_count, local_width)
        .astype(jnp.bfloat16)
    )
    rows_piece = attended
    head_sum = lax.psum_scatter(
        jnp.dot(rows_piece, w_out, preferred_element_type=jnp.float32).astype(jnp.bfloat16),
        "expert",
        scatter_dimension=0,
        tiled=True,
    ).astype(jnp.float32)
    residual = hidden_in.astype(jnp.float32) + head_sum
    moe_in = norm_rows(residual, moe_gain)
    route_count = expert_ids.shape[1]
    capacity = 2 * tok_rows * route_count // expert_lanes
    flat_expert = expert_ids.reshape(-1)
    assign_index = jnp.arange(flat_expert.shape[0], dtype=jnp.int32)
    earlier = assign_index[None, :] < assign_index[:, None]
    slot_index = jnp.sum(
        jnp.logical_and(flat_expert[:, None] == flat_expert[None, :], earlier), axis=-1
    )
    token_of = assign_index // route_count
    slot_of = flat_expert * capacity + slot_index
    dest_ids = jnp.arange(expert_lanes * capacity, dtype=jnp.int32)
    token_ids = jnp.arange(tok_rows, dtype=jnp.int32)
    hit = (slot_of[None, :] == dest_ids[:, None])
    source_token = jnp.sum(jnp.where(hit, token_of[None, :], 0), axis=-1)
    has_source = jnp.any(hit, axis=-1)
    select = ((source_token[:, None] == token_ids[None, :]) & has_source[:, None]).astype(jnp.bfloat16)
    outgoing_rows = (
        jnp.dot(select, moe_in, preferred_element_type=jnp.float32)
        .astype(jnp.bfloat16)
        .reshape(expert_lanes, capacity, model_width)
    )
    rows_piece = lax.all_to_all(outgoing_rows, "expert", split_axis=0, concat_axis=0, tiled=True)
    flat_rows = rows_piece.reshape(-1, rows_piece.shape[-1])
    gate_part = jnp.dot(flat_rows, w_gate[0], preferred_element_type=jnp.float32)
    up_part = jnp.dot(flat_rows, w_up[0], preferred_element_type=jnp.float32)
    hidden = (jax.nn.silu(gate_part) * up_part).astype(jnp.bfloat16)
    result = (
        jnp.dot(hidden, w_down[0], preferred_element_type=jnp.float32)
        .astype(jnp.bfloat16)
        .reshape(rows_piece.shape)
    )
    returned = lax.all_to_all(result, "expert", split_axis=0, concat_axis=0, tiled=True)
    picked = returned.reshape(expert_lanes * capacity, model_width)[
        flat_expert * capacity + slot_index
    ]
    weighted = jnp.sum(
        picked.reshape(tok_rows, route_count, model_width).astype(jnp.float32)
        * gate_weights[..., None],
        axis=1,
    )
    return residual + weighted


def solution(mesh):
    placed = (
        P(("group", "expert"), None),
        P(),
        P(),
        P("group", None, None, "expert"),
        P(),
        P(None, None, "expert"),
        P("expert", None),
        P(),
        P("expert", None, None),
        P("expert", None, None),
        P("expert", None, None),
        P(("group", "expert"), None),
        P(("group", "expert"), None),
    )
    return jax.shard_map(
        shards, mesh=mesh, in_specs=placed, out_specs=P(("group", "expert"), None), check_vma=False
    )
```

```python
import jax
import jax.numpy as jnp
from jax import lax
from jax.experimental import pallas as pl
from jax.experimental.pallas import tpu as pltpu
from jax.sharding import PartitionSpec as P

HEAD_DIM = 128
NBLK = 8
CTX = 2048


def norm_rows(inputs, gain_vector):
    values = inputs.astype(jnp.float32)
    factor = lax.rsqrt(jnp.mean(values * values, axis=-1, keepdims=True) + 1e-05)
    return (values * factor * gain_vector).astype(jnp.bfloat16)


def rotate(vectors, positions):
    half_dim = vectors.shape[-1] // 2
    frequency = 10000.0 ** (-jnp.arange(half_dim).astype(jnp.float32) / half_dim)
    angles = positions[:, None] * frequency[None, :]
    cosine = jnp.cos(angles)[:, None, :]
    sine_part = jnp.sin(angles)[:, None, :]
    first_half = vectors[..., :half_dim]
    second_half = vectors[..., half_dim:]
    return jnp.concatenate(
        [
            first_half * cosine - second_half * sine_part,
            first_half * sine_part + second_half * cosine,
        ],
        axis=-1,
    )


def attend_block(softmax_state, queries, key_block, value_block, key_valid):
    old_peak, old_total, old_mixed = softmax_state
    score_scale = queries.shape[-1] ** (-0.5)
    scores = (
        jnp.einsum("qhd,khd->hqk", queries, key_block, preferred_element_type=jnp.float32)
        * score_scale
    )
    scores = jnp.where(key_valid[None], scores, -1e30)
    new_peak = jnp.maximum(old_peak, jnp.max(scores, axis=-1))
    weights = jnp.exp(scores - new_peak[..., None])
    factor = jnp.exp(old_peak - new_peak)
    new_total = old_total * factor + jnp.sum(weights, axis=-1)
    new_mixed = old_mixed * factor[..., None] + jnp.einsum(
        "hqk,khd->hqd",
        weights.astype(jnp.bfloat16),
        value_block,
        preferred_element_type=jnp.float32,
    )
    return (new_peak, new_total, new_mixed)


def cache_pass(
    softmax_state,
    queries,
    all_keys,
    all_values,
    length,
    turn_count,
    array_step,
    array_first,
    position_step,
    position_first,
    block_len,
):

    def step_once(turn_index, running):
        array_start = (array_first + array_step * turn_index) * block_len
        position_start = (position_first + position_step * turn_index) * block_len
        key_block = lax.dynamic_slice_in_dim(all_keys, array_start, block_len, 0)
        value_block = lax.dynamic_slice_in_dim(all_values, array_start, block_len, 0)
        key_valid = (position_start + jnp.arange(block_len, dtype=jnp.int32) < length)[None, :]
        return attend_block(running, queries, key_block, value_block, key_valid)

    return lax.fori_loop(0, turn_count, step_once, softmax_state)


def attention_kernel(
    slots_ref, len_ref, q_ref, nk_ref, nv_ref, arr_ref, o_ref, kbuf, vbuf, m_sc, l_sc, acc_sc
):
    head = pl.program_id(0)
    rows, width = q_ref.shape
    page = arr_ref.shape[2]
    block_len = kbuf.shape[0]
    pages_per_block = block_len // page
    score_scale = width ** (-0.5)
    lanes = pl.ds(pl.multiple_of(head * width, width), width)
    q = q_ref[...]
    dims = (((1,), (1,)), ((), ()))
    scores = lax.dot_general(q, nk_ref[...], dims, preferred_element_type=jnp.float32) * score_scale
    row_i = lax.broadcasted_iota(jnp.int32, (rows, rows), 0)
    col_i = lax.broadcasted_iota(jnp.int32, (rows, rows), 1)
    scores = jnp.where(col_i <= row_i, scores, -1e30)
    peak = jnp.max(scores, axis=-1, keepdims=True)
    weights = jnp.exp(scores - peak)
    m_sc[...] = peak
    l_sc[...] = jnp.sum(weights, axis=-1, keepdims=True)
    acc_sc[...] = jnp.dot(weights.astype(jnp.bfloat16), nv_ref[...], preferred_element_type=jnp.float32)
    length = len_ref[0]
    block_count = (length + block_len - 1) // block_len

    def one_block(b, carry):
        for i in range(pages_per_block):
            slot = slots_ref[b * pages_per_block + i]
            kbuf[pl.ds(i * page, page), :] = arr_ref[slot, 0, :, lanes]
            vbuf[pl.ds(i * page, page), :] = arr_ref[slot, 1, :, lanes]
        block_scores = (
            lax.dot_general(q, kbuf[...], dims, preferred_element_type=jnp.float32) * score_scale
        )
        position = b * block_len + lax.broadcasted_iota(jnp.int32, (rows, block_len), 1)
        block_scores = jnp.where(position < length, block_scores, -1e30)
        old_peak = m_sc[...]
        new_peak = jnp.maximum(old_peak, jnp.max(block_scores, axis=-1, keepdims=True))
        block_weights = jnp.exp(block_scores - new_peak)
        factor = jnp.exp(old_peak - new_peak)
        l_sc[...] = l_sc[...] * factor + jnp.sum(block_weights, axis=-1, keepdims=True)
        acc_sc[...] = acc_sc[...] * factor + jnp.dot(
            block_weights.astype(jnp.bfloat16), vbuf[...], preferred_element_type=jnp.float32
        )
        m_sc[...] = new_peak
        return carry

    lax.fori_loop(0, block_count, one_block, 0)
    o_ref[...] = (acc_sc[...] / l_sc[...]).astype(o_ref.dtype)


def paged_attention(slots, length, queries, new_keys, new_values, arrived, block_len):
    rows, local_width = queries.shape
    heads = local_width // HEAD_DIM
    slot_count, _, page, _ = arrived.shape
    column = lambda h, *_: (0, h)
    spec = pl.BlockSpec((rows, HEAD_DIM), column)
    cost = pl.CostEstimate(
        flops=4 * rows * (rows + CTX) * local_width,
        transcendentals=rows * (rows + CTX) * heads,
        bytes_accessed=arrived.size * 2 + 4 * rows * local_width * 2,
    )
    return pl.pallas_call(
        attention_kernel,
        out_shape=jax.ShapeDtypeStruct((rows, local_width), jnp.bfloat16),
        grid_spec=pltpu.PrefetchScalarGridSpec(
            num_scalar_prefetch=2,
            grid=(heads,),
            in_specs=[
                spec,
                spec,
                spec,
                pl.BlockSpec(arrived.shape, lambda h, *_: (0, 0, 0, 0)),
            ],
            out_specs=spec,
            scratch_shapes=[
                pltpu.VMEM((block_len, HEAD_DIM), jnp.bfloat16),
                pltpu.VMEM((block_len, HEAD_DIM), jnp.bfloat16),
                pltpu.VMEM((rows, 1), jnp.float32),
                pltpu.VMEM((rows, 1), jnp.float32),
                pltpu.VMEM((rows, HEAD_DIM), jnp.float32),
            ],
        ),
        compiler_params=pltpu.CompilerParams(vmem_limit_bytes=48 * 1024 * 1024),
        cost_estimate=cost,
    )(slots, length, queries, new_keys, new_values, arrived)


def shards(
    hidden_in,
    cache_len,
    page_table,
    pool,
    attn_gain,
    w_qkv,
    w_out,
    moe_gain,
    w_gate,
    w_up,
    w_down,
    expert_ids,
    gate_weights,
):
    groups = lax.axis_size("group")
    expert_lanes = lax.axis_size("expert")
    group_index = lax.axis_index("group")
    tok_rows = hidden_in.shape[0]
    model_width = hidden_in.shape[1]
    local_width = w_out.shape[0]
    head_size = HEAD_DIM
    local_heads = local_width // head_size
    new_count = tok_rows * expert_lanes
    block_len = CTX // NBLK
    length = cache_len[group_index]
    normed = norm_rows(hidden_in, attn_gain)
    projection = w_qkv.reshape(model_width, 3 * local_width)
    projected = jnp.dot(
        lax.all_gather(normed, "expert", axis=0, tiled=True),
        projection,
        preferred_element_type=jnp.float32,
    )
    projected = projected.reshape(new_count, 3, local_heads, head_size)
    positions = (length + jnp.arange(new_count, dtype=jnp.int32)).astype(jnp.float32)
    queries = rotate(projected[:, 0], positions).astype(jnp.bfloat16)
    new_keys = rotate(projected[:, 1], positions).astype(jnp.bfloat16)
    new_values = projected[:, 2].astype(jnp.bfloat16)
    pages_per = page_table.shape[1]
    page_most = max(1, pages_per // min(groups, 16))
    owner_group = page_table // pages_per
    local_slot = page_table % pages_per
    page_order = jnp.arange(pages_per, dtype=jnp.int32)
    mine = (owner_group == group_index).astype(jnp.int32)
    mine_rank = jnp.cumsum(mine, axis=1) - mine
    slot_ids = jnp.arange(page_most, dtype=jnp.int32)
    pick = (mine[:, None, :] > 0) & (mine_rank[:, None, :] == slot_ids[None, :, None])
    send_index = jnp.sum(jnp.where(pick, local_slot[:, None, :], 0), axis=-1)
    outgoing = pool[send_index]
    arrived = lax.all_to_all(outgoing, "group", split_axis=0, concat_axis=0, tiled=True)
    arrived = arrived.reshape((groups * page_most,) + pool.shape[1:])
    my_owner = owner_group[group_index]
    before = page_order[None, :] < page_order[:, None]
    my_rank = jnp.sum(jnp.logical_and(my_owner[:, None] == my_owner[None, :], before), axis=-1)
    slots = (my_owner * page_most + my_rank).astype(jnp.int32)
    attended = paged_attention(
        slots,
        jnp.reshape(length, (1,)).astype(jnp.int32),
        queries.reshape(new_count, local_width),
        new_keys.reshape(new_count, local_width),
        new_values.reshape(new_count, local_width),
        arrived,
        block_len,
    )
    rows_piece = attended
    head_sum = lax.psum_scatter(
        jnp.dot(rows_piece, w_out, preferred_element_type=jnp.float32).astype(jnp.bfloat16),
        "expert",
        scatter_dimension=0,
        tiled=True,
    ).astype(jnp.float32)
    residual = hidden_in.astype(jnp.float32) + head_sum
    moe_in = norm_rows(residual, moe_gain)
    route_count = expert_ids.shape[1]
    capacity = 2 * tok_rows * route_count // expert_lanes
    flat_expert = expert_ids.reshape(-1)
    assign_index = jnp.arange(flat_expert.shape[0], dtype=jnp.int32)
    earlier = assign_index[None, :] < assign_index[:, None]
    slot_index = jnp.sum(
        jnp.logical_and(flat_expert[:, None] == flat_expert[None, :], earlier), axis=-1
    )
    token_of = assign_index // route_count
    slot_of = flat_expert * capacity + slot_index
    dest_ids = jnp.arange(expert_lanes * capacity, dtype=jnp.int32)
    token_ids = jnp.arange(tok_rows, dtype=jnp.int32)
    hit = (slot_of[None, :] == dest_ids[:, None])
    source_token = jnp.sum(jnp.where(hit, token_of[None, :], 0), axis=-1)
    has_source = jnp.any(hit, axis=-1)
    select = ((source_token[:, None] == token_ids[None, :]) & has_source[:, None]).astype(jnp.bfloat16)
    outgoing_rows = (
        jnp.dot(select, moe_in, preferred_element_type=jnp.float32)
        .astype(jnp.bfloat16)
        .reshape(expert_lanes, capacity, model_width)
    )
    rows_piece = lax.all_to_all(outgoing_rows, "expert", split_axis=0, concat_axis=0, tiled=True)
    flat_rows = rows_piece.reshape(-1, rows_piece.shape[-1])
    gate_part = jnp.dot(flat_rows, w_gate[0], preferred_element_type=jnp.float32)
    up_part = jnp.dot(flat_rows, w_up[0], preferred_element_type=jnp.float32)
    hidden = (jax.nn.silu(gate_part) * up_part).astype(jnp.bfloat16)
    result = (
        jnp.dot(hidden, w_down[0], preferred_element_type=jnp.float32)
        .astype(jnp.bfloat16)
        .reshape(rows_piece.shape)
    )
    returned = lax.all_to_all(result, "expert", split_axis=0, concat_axis=0, tiled=True)
    picked = returned.reshape(expert_lanes * capacity, model_width)[
        flat_expert * capacity + slot_index
    ]
    weighted = jnp.sum(
        picked.reshape(tok_rows, route_count, model_width).astype(jnp.float32)
        * gate_weights[..., None],
        axis=1,
    )
    return residual + weighted


def solution(mesh):
    placed = (
        P(("group", "expert"), None),
        P(),
        P(),
        P("group", None, None, "expert"),
        P(),
        P(None, None, "expert"),
        P("expert", None),
        P(),
        P("expert", None, None),
        P("expert", None, None),
        P("expert", None, None),
        P(("group", "expert"), None),
        P(("group", "expert"), None),
    )
    return jax.shard_map(
        shards, mesh=mesh, in_specs=placed, out_specs=P(("group", "expert"), None), check_vma=False
    )
```

```python
import jax
import jax.numpy as jnp
from jax import lax
from jax.experimental import pallas as pl
from jax.experimental.pallas import tpu as pltpu
from jax.sharding import PartitionSpec as P

HEAD_DIM = 128
EXPERT = ("ey", "ec")
NBLK = 8
CTX = 2048


def norm_rows(inputs, gain_vector):
    values = inputs.astype(jnp.float32)
    factor = lax.rsqrt(jnp.mean(values * values, axis=-1, keepdims=True) + 1e-05)
    return (values * factor * gain_vector).astype(jnp.bfloat16)


def rotate(vectors, positions):
    half_dim = vectors.shape[-1] // 2
    frequency = 10000.0 ** (-jnp.arange(half_dim).astype(jnp.float32) / half_dim)
    angles = positions[:, None] * frequency[None, :]
    cosine = jnp.cos(angles)[:, None, :]
    sine_part = jnp.sin(angles)[:, None, :]
    first_half = vectors[..., :half_dim]
    second_half = vectors[..., half_dim:]
    return jnp.concatenate(
        [
            first_half * cosine - second_half * sine_part,
            first_half * sine_part + second_half * cosine,
        ],
        axis=-1,
    )


def attend_block(softmax_state, queries, key_block, value_block, key_valid):
    old_peak, old_total, old_mixed = softmax_state
    score_scale = queries.shape[-1] ** (-0.5)
    scores = (
        jnp.einsum("qhd,khd->hqk", queries, key_block, preferred_element_type=jnp.float32)
        * score_scale
    )
    scores = jnp.where(key_valid[None], scores, -1e30)
    new_peak = jnp.maximum(old_peak, jnp.max(scores, axis=-1))
    weights = jnp.exp(scores - new_peak[..., None])
    factor = jnp.exp(old_peak - new_peak)
    new_total = old_total * factor + jnp.sum(weights, axis=-1)
    new_mixed = old_mixed * factor[..., None] + jnp.einsum(
        "hqk,khd->hqd",
        weights.astype(jnp.bfloat16),
        value_block,
        preferred_element_type=jnp.float32,
    )
    return (new_peak, new_total, new_mixed)


def cache_pass(
    softmax_state,
    queries,
    all_keys,
    all_values,
    length,
    turn_count,
    array_step,
    array_first,
    position_step,
    position_first,
    block_len,
):

    def step_once(turn_index, running):
        array_start = (array_first + array_step * turn_index) * block_len
        position_start = (position_first + position_step * turn_index) * block_len
        key_block = lax.dynamic_slice_in_dim(all_keys, array_start, block_len, 0)
        value_block = lax.dynamic_slice_in_dim(all_values, array_start, block_len, 0)
        key_valid = (position_start + jnp.arange(block_len, dtype=jnp.int32) < length)[None, :]
        return attend_block(running, queries, key_block, value_block, key_valid)

    return lax.fori_loop(0, turn_count, step_once, softmax_state)


def attention_kernel(
    slots_ref, len_ref, q_ref, nk_ref, nv_ref, arr_ref, o_ref, kbuf, vbuf, m_sc, l_sc, acc_sc
):
    head = pl.program_id(0)
    rows, width = q_ref.shape
    page = arr_ref.shape[2]
    block_len = kbuf.shape[0]
    pages_per_block = block_len // page
    score_scale = width ** (-0.5)
    lanes = pl.ds(pl.multiple_of(head * width, width), width)
    q = q_ref[...]
    dims = (((1,), (1,)), ((), ()))
    scores = lax.dot_general(q, nk_ref[...], dims, preferred_element_type=jnp.float32) * score_scale
    row_i = lax.broadcasted_iota(jnp.int32, (rows, rows), 0)
    col_i = lax.broadcasted_iota(jnp.int32, (rows, rows), 1)
    scores = jnp.where(col_i <= row_i, scores, -1e30)
    peak = jnp.max(scores, axis=-1, keepdims=True)
    weights = jnp.exp(scores - peak)
    m_sc[...] = peak
    l_sc[...] = jnp.sum(weights, axis=-1, keepdims=True)
    acc_sc[...] = jnp.dot(weights.astype(jnp.bfloat16), nv_ref[...], preferred_element_type=jnp.float32)
    length = len_ref[0]
    block_count = (length + block_len - 1) // block_len

    def one_block(b, carry):
        for i in range(pages_per_block):
            slot = slots_ref[b * pages_per_block + i]
            kbuf[pl.ds(i * page, page), :] = arr_ref[slot, 0, :, lanes]
            vbuf[pl.ds(i * page, page), :] = arr_ref[slot, 1, :, lanes]
        block_scores = (
            lax.dot_general(q, kbuf[...], dims, preferred_element_type=jnp.float32) * score_scale
        )
        position = b * block_len + lax.broadcasted_iota(jnp.int32, (rows, block_len), 1)
        block_scores = jnp.where(position < length, block_scores, -1e30)
        old_peak = m_sc[...]
        new_peak = jnp.maximum(old_peak, jnp.max(block_scores, axis=-1, keepdims=True))
        block_weights = jnp.exp(block_scores - new_peak)
        factor = jnp.exp(old_peak - new_peak)
        l_sc[...] = l_sc[...] * factor + jnp.sum(block_weights, axis=-1, keepdims=True)
        acc_sc[...] = acc_sc[...] * factor + jnp.dot(
            block_weights.astype(jnp.bfloat16), vbuf[...], preferred_element_type=jnp.float32
        )
        m_sc[...] = new_peak
        return carry

    lax.fori_loop(0, block_count, one_block, 0)
    o_ref[...] = (acc_sc[...] / l_sc[...]).astype(o_ref.dtype)


def paged_attention(slots, length, queries, new_keys, new_values, arrived, block_len):
    rows, local_width = queries.shape
    heads = local_width // HEAD_DIM
    slot_count, _, page, _ = arrived.shape
    column = lambda h, *_: (0, h)
    spec = pl.BlockSpec((rows, HEAD_DIM), column)
    cost = pl.CostEstimate(
        flops=4 * rows * (rows + CTX) * local_width,
        transcendentals=rows * (rows + CTX) * heads,
        bytes_accessed=arrived.size * 2 + 4 * rows * local_width * 2,
    )
    return pl.pallas_call(
        attention_kernel,
        out_shape=jax.ShapeDtypeStruct((rows, local_width), jnp.bfloat16),
        grid_spec=pltpu.PrefetchScalarGridSpec(
            num_scalar_prefetch=2,
            grid=(heads,),
            in_specs=[
                spec,
                spec,
                spec,
                pl.BlockSpec(arrived.shape, lambda h, *_: (0, 0, 0, 0)),
            ],
            out_specs=spec,
            scratch_shapes=[
                pltpu.VMEM((block_len, HEAD_DIM), jnp.bfloat16),
                pltpu.VMEM((block_len, HEAD_DIM), jnp.bfloat16),
                pltpu.VMEM((rows, 1), jnp.float32),
                pltpu.VMEM((rows, 1), jnp.float32),
                pltpu.VMEM((rows, HEAD_DIM), jnp.float32),
            ],
        ),
        compiler_params=pltpu.CompilerParams(vmem_limit_bytes=48 * 1024 * 1024),
        cost_estimate=cost,
    )(slots, length, queries, new_keys, new_values, arrived)


def shards(
    hidden_in,
    cache_len,
    page_table,
    pool,
    attn_gain,
    w_qkv,
    w_out,
    moe_gain,
    w_gate,
    w_up,
    w_down,
    expert_ids,
    gate_weights,
):
    groups = lax.axis_size("group")
    expert_lanes = lax.axis_size(EXPERT)
    group_index = lax.axis_index("group")
    tok_rows = hidden_in.shape[0]
    model_width = hidden_in.shape[1]
    local_width = w_out.shape[0]
    head_size = HEAD_DIM
    local_heads = local_width // head_size
    new_count = tok_rows * expert_lanes
    block_len = CTX // NBLK
    length = cache_len[group_index]
    normed = norm_rows(hidden_in, attn_gain)
    projection = w_qkv.reshape(model_width, 3 * local_width)
    projected = jnp.dot(
        lax.all_gather(normed, EXPERT, axis=0, tiled=True),
        projection,
        preferred_element_type=jnp.float32,
    )
    projected = projected.reshape(new_count, 3, local_heads, head_size)
    positions = (length + jnp.arange(new_count, dtype=jnp.int32)).astype(jnp.float32)
    queries = rotate(projected[:, 0], positions).astype(jnp.bfloat16)
    new_keys = rotate(projected[:, 1], positions).astype(jnp.bfloat16)
    new_values = projected[:, 2].astype(jnp.bfloat16)
    pages_per = page_table.shape[1]
    page_most = max(1, pages_per // min(groups, 16))
    owner_group = page_table // pages_per
    local_slot = page_table % pages_per
    page_order = jnp.arange(pages_per, dtype=jnp.int32)
    mine = (owner_group == group_index).astype(jnp.int32)
    mine_rank = jnp.cumsum(mine, axis=1) - mine
    slot_ids = jnp.arange(page_most, dtype=jnp.int32)
    pick = (mine[:, None, :] > 0) & (mine_rank[:, None, :] == slot_ids[None, :, None])
    send_index = jnp.sum(jnp.where(pick, local_slot[:, None, :], 0), axis=-1)
    outgoing = pool[send_index]
    arrived = lax.all_to_all(outgoing, "group", split_axis=0, concat_axis=0, tiled=True)
    arrived = arrived.reshape((groups * page_most,) + pool.shape[1:])
    my_owner = owner_group[group_index]
    before = page_order[None, :] < page_order[:, None]
    my_rank = jnp.sum(jnp.logical_and(my_owner[:, None] == my_owner[None, :], before), axis=-1)
    slots = (my_owner * page_most + my_rank).astype(jnp.int32)
    attended = paged_attention(
        slots,
        jnp.reshape(length, (1,)).astype(jnp.int32),
        queries.reshape(new_count, local_width),
        new_keys.reshape(new_count, local_width),
        new_values.reshape(new_count, local_width),
        arrived,
        block_len,
    )
    rows_piece = attended
    head_parts = jnp.dot(rows_piece, w_out, preferred_element_type=jnp.float32).astype(jnp.bfloat16)
    chips = lax.axis_size("ey")
    cores = lax.axis_size("ec")
    head_parts = head_parts.reshape(chips, cores, tok_rows, model_width)
    head_parts = lax.all_to_all(head_parts, "ec", split_axis=1, concat_axis=1, tiled=True)
    head_parts = jnp.sum(head_parts.astype(jnp.float32), axis=1).astype(jnp.bfloat16)
    head_parts = lax.all_to_all(head_parts, "ey", split_axis=0, concat_axis=0, tiled=True)
    head_sum = jnp.sum(head_parts.astype(jnp.float32), axis=0)
    residual = hidden_in.astype(jnp.float32) + head_sum
    moe_in = norm_rows(residual, moe_gain)
    route_count = expert_ids.shape[1]
    capacity = 2 * tok_rows * route_count // expert_lanes
    flat_expert = expert_ids.reshape(-1)
    assign_index = jnp.arange(flat_expert.shape[0], dtype=jnp.int32)
    earlier = assign_index[None, :] < assign_index[:, None]
    slot_index = jnp.sum(
        jnp.logical_and(flat_expert[:, None] == flat_expert[None, :], earlier), axis=-1
    )
    token_of = assign_index // route_count
    slot_of = flat_expert * capacity + slot_index
    dest_ids = jnp.arange(expert_lanes * capacity, dtype=jnp.int32)
    token_ids = jnp.arange(tok_rows, dtype=jnp.int32)
    hit = (slot_of[None, :] == dest_ids[:, None])
    source_token = jnp.sum(jnp.where(hit, token_of[None, :], 0), axis=-1)
    has_source = jnp.any(hit, axis=-1)
    select = ((source_token[:, None] == token_ids[None, :]) & has_source[:, None]).astype(jnp.bfloat16)
    outgoing_rows = (
        jnp.dot(select, moe_in, preferred_element_type=jnp.float32)
        .astype(jnp.bfloat16)
        .reshape(expert_lanes, capacity, model_width)
    )
    rows_piece = lax.all_to_all(outgoing_rows, EXPERT, split_axis=0, concat_axis=0, tiled=True)
    flat_rows = rows_piece.reshape(-1, rows_piece.shape[-1])
    gate_part = jnp.dot(flat_rows, w_gate[0], preferred_element_type=jnp.float32)
    up_part = jnp.dot(flat_rows, w_up[0], preferred_element_type=jnp.float32)
    hidden = (jax.nn.silu(gate_part) * up_part).astype(jnp.bfloat16)
    result = (
        jnp.dot(hidden, w_down[0], preferred_element_type=jnp.float32)
        .astype(jnp.bfloat16)
        .reshape(rows_piece.shape)
    )
    returned = lax.all_to_all(result, EXPERT, split_axis=0, concat_axis=0, tiled=True)
    picked = returned.reshape(expert_lanes * capacity, model_width)[
        flat_expert * capacity + slot_index
    ]
    weighted = jnp.sum(
        picked.reshape(tok_rows, route_count, model_width).astype(jnp.float32)
        * gate_weights[..., None],
        axis=1,
    )
    return residual + weighted


def solution(mesh):
    lanes = mesh.shape["expert"]
    cores = 2 if lanes % 2 == 0 else 1
    split = jax.sharding.Mesh(
        mesh.devices.reshape(mesh.shape["group"], lanes // cores, cores), ("group",) + EXPERT
    )
    rows = ("group",) + EXPERT
    placed = (
        P(rows, None),
        P(),
        P(),
        P("group", None, None, EXPERT),
        P(),
        P(None, None, EXPERT),
        P(EXPERT, None),
        P(),
        P(EXPERT, None, None),
        P(EXPERT, None, None),
        P(EXPERT, None, None),
        P(rows, None),
        P(rows, None),
    )
    return jax.shard_map(
        shards, mesh=split, in_specs=placed, out_specs=P(rows, None), check_vma=False
    )
```

```python
import functools

import jax
import jax.numpy as jnp
from jax import lax
from jax.experimental import pallas as pl
from jax.experimental.pallas import tpu as pltpu
from jax.sharding import PartitionSpec as P

HEAD_DIM = 128
EXPERT = ("ey", "ec")
MESH_AXES = ("group", "ey", "ec")
MESH_IDS = pl.DeviceIdType.MESH
NBLK = 8
CTX = 2048


def norm_rows(inputs, gain_vector):
    values = inputs.astype(jnp.float32)
    factor = lax.rsqrt(jnp.mean(values * values, axis=-1, keepdims=True) + 1e-05)
    return (values * factor * gain_vector).astype(jnp.bfloat16)


def rotate(vectors, positions):
    half_dim = vectors.shape[-1] // 2
    frequency = 10000.0 ** (-jnp.arange(half_dim).astype(jnp.float32) / half_dim)
    angles = positions[:, None] * frequency[None, :]
    cosine = jnp.cos(angles)[:, None, :]
    sine_part = jnp.sin(angles)[:, None, :]
    first_half = vectors[..., :half_dim]
    second_half = vectors[..., half_dim:]
    return jnp.concatenate(
        [
            first_half * cosine - second_half * sine_part,
            first_half * sine_part + second_half * cosine,
        ],
        axis=-1,
    )


def attend_block(softmax_state, queries, key_block, value_block, key_valid):
    old_peak, old_total, old_mixed = softmax_state
    score_scale = queries.shape[-1] ** (-0.5)
    scores = (
        jnp.einsum("qhd,khd->hqk", queries, key_block, preferred_element_type=jnp.float32)
        * score_scale
    )
    scores = jnp.where(key_valid[None], scores, -1e30)
    new_peak = jnp.maximum(old_peak, jnp.max(scores, axis=-1))
    weights = jnp.exp(scores - new_peak[..., None])
    factor = jnp.exp(old_peak - new_peak)
    new_total = old_total * factor + jnp.sum(weights, axis=-1)
    new_mixed = old_mixed * factor[..., None] + jnp.einsum(
        "hqk,khd->hqd",
        weights.astype(jnp.bfloat16),
        value_block,
        preferred_element_type=jnp.float32,
    )
    return (new_peak, new_total, new_mixed)


def cache_pass(
    softmax_state,
    queries,
    all_keys,
    all_values,
    length,
    turn_count,
    array_step,
    array_first,
    position_step,
    position_first,
    block_len,
):

    def step_once(turn_index, running):
        array_start = (array_first + array_step * turn_index) * block_len
        position_start = (position_first + position_step * turn_index) * block_len
        key_block = lax.dynamic_slice_in_dim(all_keys, array_start, block_len, 0)
        value_block = lax.dynamic_slice_in_dim(all_values, array_start, block_len, 0)
        key_valid = (position_start + jnp.arange(block_len, dtype=jnp.int32) < length)[None, :]
        return attend_block(running, queries, key_block, value_block, key_valid)

    return lax.fori_loop(0, turn_count, step_once, softmax_state)


def exchange_kernel(axes, x_ref, o_ref, send_sems, recv_sems, own_sem):
    sizes = [lax.axis_size(a) for a in axes]
    count = 1
    for size in sizes:
        count *= size
    me = 0
    for a, size in zip(axes, sizes):
        me = me * size + lax.axis_index(a)

    def device_of(peer):
        coords = {}
        rest = peer
        for a, size in reversed(list(zip(axes, sizes))):
            coords[a] = rest % size
            rest = rest // size
        return tuple(coords.get(a, lax.axis_index(a)) for a in MESH_AXES)

    barrier = pltpu.get_barrier_semaphore()
    for k in range(1, count):
        pl.semaphore_signal(
            barrier, inc=1, device_id=device_of((me + k) % count), device_id_type=MESH_IDS
        )
    pl.semaphore_wait(barrier, count - 1)
    own = pltpu.make_async_copy(x_ref.at[me], o_ref.at[me], own_sem)
    own.start()
    copies = []
    for k in range(1, count):
        peer = (me + k) % count
        copy = pltpu.make_async_remote_copy(
            src_ref=x_ref.at[peer],
            dst_ref=o_ref.at[me],
            send_sem=send_sems.at[k],
            recv_sem=recv_sems.at[k],
            device_id=device_of(peer),
            device_id_type=MESH_IDS,
        )
        copy.start()
        copies.append(copy)
    own.wait()
    for copy in copies:
        copy.wait()


def exchange(x, axes, ident):
    count = x.shape[0]
    return pl.pallas_call(
        functools.partial(exchange_kernel, axes),
        out_shape=jax.ShapeDtypeStruct(x.shape, x.dtype),
        in_specs=[pl.BlockSpec(memory_space=pl.ANY)],
        out_specs=pl.BlockSpec(memory_space=pl.ANY),
        scratch_shapes=[
            pltpu.SemaphoreType.DMA((count,)),
            pltpu.SemaphoreType.DMA((count,)),
            pltpu.SemaphoreType.DMA(()),
        ],
        compiler_params=pltpu.CompilerParams(collective_id=ident, has_side_effects=True),
    )(x)


def attention_kernel(
    slots_ref, len_ref, q_ref, nk_ref, nv_ref, arr_ref, o_ref, kbuf, vbuf, m_sc, l_sc, acc_sc
):
    head = pl.program_id(0)
    rows, width = q_ref.shape
    page = arr_ref.shape[2]
    block_len = kbuf.shape[0]
    pages_per_block = block_len // page
    score_scale = width ** (-0.5)
    lanes = pl.ds(pl.multiple_of(head * width, width), width)
    q = q_ref[...]
    dims = (((1,), (1,)), ((), ()))
    scores = lax.dot_general(q, nk_ref[...], dims, preferred_element_type=jnp.float32) * score_scale
    row_i = lax.broadcasted_iota(jnp.int32, (rows, rows), 0)
    col_i = lax.broadcasted_iota(jnp.int32, (rows, rows), 1)
    scores = jnp.where(col_i <= row_i, scores, -1e30)
    peak = jnp.max(scores, axis=-1, keepdims=True)
    weights = jnp.exp(scores - peak)
    m_sc[...] = peak
    l_sc[...] = jnp.sum(weights, axis=-1, keepdims=True)
    acc_sc[...] = jnp.dot(weights.astype(jnp.bfloat16), nv_ref[...], preferred_element_type=jnp.float32)
    length = len_ref[0]
    block_count = (length + block_len - 1) // block_len

    def one_block(b, carry):
        for i in range(pages_per_block):
            slot = slots_ref[b * pages_per_block + i]
            kbuf[pl.ds(i * page, page), :] = arr_ref[slot, 0, :, lanes]
            vbuf[pl.ds(i * page, page), :] = arr_ref[slot, 1, :, lanes]
        block_scores = (
            lax.dot_general(q, kbuf[...], dims, preferred_element_type=jnp.float32) * score_scale
        )
        position = b * block_len + lax.broadcasted_iota(jnp.int32, (rows, block_len), 1)
        block_scores = jnp.where(position < length, block_scores, -1e30)
        old_peak = m_sc[...]
        new_peak = jnp.maximum(old_peak, jnp.max(block_scores, axis=-1, keepdims=True))
        block_weights = jnp.exp(block_scores - new_peak)
        factor = jnp.exp(old_peak - new_peak)
        l_sc[...] = l_sc[...] * factor + jnp.sum(block_weights, axis=-1, keepdims=True)
        acc_sc[...] = acc_sc[...] * factor + jnp.dot(
            block_weights.astype(jnp.bfloat16), vbuf[...], preferred_element_type=jnp.float32
        )
        m_sc[...] = new_peak
        return carry

    lax.fori_loop(0, block_count, one_block, 0)
    o_ref[...] = (acc_sc[...] / l_sc[...]).astype(o_ref.dtype)


def paged_attention(slots, length, queries, new_keys, new_values, arrived, block_len):
    rows, local_width = queries.shape
    heads = local_width // HEAD_DIM
    slot_count, _, page, _ = arrived.shape
    column = lambda h, *_: (0, h)
    spec = pl.BlockSpec((rows, HEAD_DIM), column)
    cost = pl.CostEstimate(
        flops=4 * rows * (rows + CTX) * local_width,
        transcendentals=rows * (rows + CTX) * heads,
        bytes_accessed=arrived.size * 2 + 4 * rows * local_width * 2,
    )
    return pl.pallas_call(
        attention_kernel,
        out_shape=jax.ShapeDtypeStruct((rows, local_width), jnp.bfloat16),
        grid_spec=pltpu.PrefetchScalarGridSpec(
            num_scalar_prefetch=2,
            grid=(heads,),
            in_specs=[
                spec,
                spec,
                spec,
                pl.BlockSpec(arrived.shape, lambda h, *_: (0, 0, 0, 0)),
            ],
            out_specs=spec,
            scratch_shapes=[
                pltpu.VMEM((block_len, HEAD_DIM), jnp.bfloat16),
                pltpu.VMEM((block_len, HEAD_DIM), jnp.bfloat16),
                pltpu.VMEM((rows, 1), jnp.float32),
                pltpu.VMEM((rows, 1), jnp.float32),
                pltpu.VMEM((rows, HEAD_DIM), jnp.float32),
            ],
        ),
        compiler_params=pltpu.CompilerParams(vmem_limit_bytes=48 * 1024 * 1024),
        cost_estimate=cost,
    )(slots, length, queries, new_keys, new_values, arrived)


def shards(
    hidden_in,
    cache_len,
    page_table,
    pool,
    attn_gain,
    w_qkv,
    w_out,
    moe_gain,
    w_gate,
    w_up,
    w_down,
    expert_ids,
    gate_weights,
):
    groups = lax.axis_size("group")
    expert_lanes = lax.axis_size(EXPERT)
    group_index = lax.axis_index("group")
    tok_rows = hidden_in.shape[0]
    model_width = hidden_in.shape[1]
    local_width = w_out.shape[0]
    head_size = HEAD_DIM
    local_heads = local_width // head_size
    new_count = tok_rows * expert_lanes
    block_len = CTX // NBLK
    length = cache_len[group_index]
    normed = norm_rows(hidden_in, attn_gain)
    projection = w_qkv.reshape(model_width, 3 * local_width)
    projected = jnp.dot(
        lax.all_gather(normed, EXPERT, axis=0, tiled=True),
        projection,
        preferred_element_type=jnp.float32,
    )
    projected = projected.reshape(new_count, 3, local_heads, head_size)
    positions = (length + jnp.arange(new_count, dtype=jnp.int32)).astype(jnp.float32)
    queries = rotate(projected[:, 0], positions).astype(jnp.bfloat16)
    new_keys = rotate(projected[:, 1], positions).astype(jnp.bfloat16)
    new_values = projected[:, 2].astype(jnp.bfloat16)
    pages_per = page_table.shape[1]
    page_most = max(1, pages_per // min(groups, 16))
    owner_group = page_table // pages_per
    local_slot = page_table % pages_per
    page_order = jnp.arange(pages_per, dtype=jnp.int32)
    mine = (owner_group == group_index).astype(jnp.int32)
    mine_rank = jnp.cumsum(mine, axis=1) - mine
    slot_ids = jnp.arange(page_most, dtype=jnp.int32)
    pick = (mine[:, None, :] > 0) & (mine_rank[:, None, :] == slot_ids[None, :, None])
    send_index = jnp.sum(jnp.where(pick, local_slot[:, None, :], 0), axis=-1)
    outgoing = pool[send_index]
    arrived = lax.all_to_all(outgoing, "group", split_axis=0, concat_axis=0, tiled=True)
    arrived = arrived.reshape((groups * page_most,) + pool.shape[1:])
    my_owner = owner_group[group_index]
    before = page_order[None, :] < page_order[:, None]
    my_rank = jnp.sum(jnp.logical_and(my_owner[:, None] == my_owner[None, :], before), axis=-1)
    slots = (my_owner * page_most + my_rank).astype(jnp.int32)
    attended = paged_attention(
        slots,
        jnp.reshape(length, (1,)).astype(jnp.int32),
        queries.reshape(new_count, local_width),
        new_keys.reshape(new_count, local_width),
        new_values.reshape(new_count, local_width),
        arrived,
        block_len,
    )
    rows_piece = attended
    head_parts = jnp.dot(rows_piece, w_out, preferred_element_type=jnp.float32).astype(jnp.bfloat16)
    chips = lax.axis_size("ey")
    cores = lax.axis_size("ec")
    head_parts = head_parts.reshape(chips, cores, tok_rows, model_width)
    head_parts = lax.all_to_all(head_parts, "ec", split_axis=1, concat_axis=1, tiled=True)
    head_parts = jnp.sum(head_parts.astype(jnp.float32), axis=1).astype(jnp.bfloat16)
    head_parts = lax.all_to_all(head_parts, "ey", split_axis=0, concat_axis=0, tiled=True)
    head_sum = jnp.sum(head_parts.astype(jnp.float32), axis=0)
    residual = hidden_in.astype(jnp.float32) + head_sum
    moe_in = norm_rows(residual, moe_gain)
    route_count = expert_ids.shape[1]
    capacity = 2 * tok_rows * route_count // expert_lanes
    flat_expert = expert_ids.reshape(-1)
    assign_index = jnp.arange(flat_expert.shape[0], dtype=jnp.int32)
    earlier = assign_index[None, :] < assign_index[:, None]
    slot_index = jnp.sum(
        jnp.logical_and(flat_expert[:, None] == flat_expert[None, :], earlier), axis=-1
    )
    token_of = assign_index // route_count
    slot_of = flat_expert * capacity + slot_index
    dest_ids = jnp.arange(expert_lanes * capacity, dtype=jnp.int32)
    token_ids = jnp.arange(tok_rows, dtype=jnp.int32)
    hit = (slot_of[None, :] == dest_ids[:, None])
    source_token = jnp.sum(jnp.where(hit, token_of[None, :], 0), axis=-1)
    has_source = jnp.any(hit, axis=-1)
    select = ((source_token[:, None] == token_ids[None, :]) & has_source[:, None]).astype(jnp.bfloat16)
    outgoing_rows = (
        jnp.dot(select, moe_in, preferred_element_type=jnp.float32)
        .astype(jnp.bfloat16)
        .reshape(expert_lanes, capacity, model_width)
    )
    rows_piece = exchange(outgoing_rows, EXPERT, 0)
    flat_rows = rows_piece.reshape(-1, rows_piece.shape[-1])
    gate_part = jnp.dot(flat_rows, w_gate[0], preferred_element_type=jnp.float32)
    up_part = jnp.dot(flat_rows, w_up[0], preferred_element_type=jnp.float32)
    hidden = (jax.nn.silu(gate_part) * up_part).astype(jnp.bfloat16)
    result = (
        jnp.dot(hidden, w_down[0], preferred_element_type=jnp.float32)
        .astype(jnp.bfloat16)
        .reshape(rows_piece.shape)
    )
    returned = exchange(result, EXPERT, 1)
    picked = returned.reshape(expert_lanes * capacity, model_width)[
        flat_expert * capacity + slot_index
    ]
    weighted = jnp.sum(
        picked.reshape(tok_rows, route_count, model_width).astype(jnp.float32)
        * gate_weights[..., None],
        axis=1,
    )
    return residual + weighted


def solution(mesh):
    lanes = mesh.shape["expert"]
    cores = 2 if lanes % 2 == 0 else 1
    split = jax.sharding.Mesh(
        mesh.devices.reshape(mesh.shape["group"], lanes // cores, cores), ("group",) + EXPERT
    )
    rows = ("group",) + EXPERT
    placed = (
        P(rows, None),
        P(),
        P(),
        P("group", None, None, EXPERT),
        P(),
        P(None, None, EXPERT),
        P(EXPERT, None),
        P(),
        P(EXPERT, None, None),
        P(EXPERT, None, None),
        P(EXPERT, None, None),
        P(rows, None),
        P(rows, None),
    )
    return jax.shard_map(
        shards, mesh=split, in_specs=placed, out_specs=P(rows, None), check_vma=False
    )
```

```python
import functools

import jax
import jax.numpy as jnp
from jax import lax
from jax.experimental import pallas as pl
from jax.experimental.pallas import tpu as pltpu
from jax.sharding import PartitionSpec as P

HEAD_DIM = 128
EXPERT = ("ey", "ec")
MESH_AXES = ("group", "ey", "ec")
MESH_IDS = pl.DeviceIdType.MESH
NBLK = 8
CTX = 2048


def norm_rows(inputs, gain_vector):
    values = inputs.astype(jnp.float32)
    factor = lax.rsqrt(jnp.mean(values * values, axis=-1, keepdims=True) + 1e-05)
    return (values * factor * gain_vector).astype(jnp.bfloat16)


def rotate(vectors, positions):
    half_dim = vectors.shape[-1] // 2
    frequency = 10000.0 ** (-jnp.arange(half_dim).astype(jnp.float32) / half_dim)
    angles = positions[:, None] * frequency[None, :]
    cosine = jnp.cos(angles)[:, None, :]
    sine_part = jnp.sin(angles)[:, None, :]
    first_half = vectors[..., :half_dim]
    second_half = vectors[..., half_dim:]
    return jnp.concatenate(
        [
            first_half * cosine - second_half * sine_part,
            first_half * sine_part + second_half * cosine,
        ],
        axis=-1,
    )


def attend_block(softmax_state, queries, key_block, value_block, key_valid):
    old_peak, old_total, old_mixed = softmax_state
    score_scale = queries.shape[-1] ** (-0.5)
    scores = (
        jnp.einsum("qhd,khd->hqk", queries, key_block, preferred_element_type=jnp.float32)
        * score_scale
    )
    scores = jnp.where(key_valid[None], scores, -1e30)
    new_peak = jnp.maximum(old_peak, jnp.max(scores, axis=-1))
    weights = jnp.exp(scores - new_peak[..., None])
    factor = jnp.exp(old_peak - new_peak)
    new_total = old_total * factor + jnp.sum(weights, axis=-1)
    new_mixed = old_mixed * factor[..., None] + jnp.einsum(
        "hqk,khd->hqd",
        weights.astype(jnp.bfloat16),
        value_block,
        preferred_element_type=jnp.float32,
    )
    return (new_peak, new_total, new_mixed)


def cache_pass(
    softmax_state,
    queries,
    all_keys,
    all_values,
    length,
    turn_count,
    array_step,
    array_first,
    position_step,
    position_first,
    block_len,
):

    def step_once(turn_index, running):
        array_start = (array_first + array_step * turn_index) * block_len
        position_start = (position_first + position_step * turn_index) * block_len
        key_block = lax.dynamic_slice_in_dim(all_keys, array_start, block_len, 0)
        value_block = lax.dynamic_slice_in_dim(all_values, array_start, block_len, 0)
        key_valid = (position_start + jnp.arange(block_len, dtype=jnp.int32) < length)[None, :]
        return attend_block(running, queries, key_block, value_block, key_valid)

    return lax.fori_loop(0, turn_count, step_once, softmax_state)


def exchange_kernel(axes, split, x_ref, o_ref, send_sems, recv_sems, own_sem):
    sizes = [lax.axis_size(a) for a in axes]
    count = 1
    for size in sizes:
        count *= size
    me = 0
    for a, size in zip(axes, sizes):
        me = me * size + lax.axis_index(a)

    def device_of(peer):
        coords = {}
        rest = peer
        for a, size in reversed(list(zip(axes, sizes))):
            coords[a] = rest % size
            rest = rest // size
        return tuple(coords.get(a, lax.axis_index(a)) for a in MESH_AXES)

    barrier = pltpu.get_barrier_semaphore()
    for k in range(1, count):
        pl.semaphore_signal(
            barrier, inc=1, device_id=device_of((me + k) % count), device_id_type=MESH_IDS
        )
    pl.semaphore_wait(barrier, count - 1)
    def block(ref, index):
        return ref.at[index] if split == 0 else ref.at[:, index]

    own = pltpu.make_async_copy(block(x_ref, me), block(o_ref, me), own_sem)
    own.start()
    copies = []
    for k in range(1, count):
        peer = (me + k) % count
        copy = pltpu.make_async_remote_copy(
            src_ref=block(x_ref, peer),
            dst_ref=block(o_ref, me),
            send_sem=send_sems.at[k],
            recv_sem=recv_sems.at[k],
            device_id=device_of(peer),
            device_id_type=MESH_IDS,
        )
        copy.start()
        copies.append(copy)
    own.wait()
    for copy in copies:
        copy.wait()


def exchange(x, axes, ident, split=0):
    count = x.shape[split]
    return pl.pallas_call(
        functools.partial(exchange_kernel, axes, split),
        out_shape=jax.ShapeDtypeStruct(x.shape, x.dtype),
        in_specs=[pl.BlockSpec(memory_space=pl.ANY)],
        out_specs=pl.BlockSpec(memory_space=pl.ANY),
        scratch_shapes=[
            pltpu.SemaphoreType.DMA((count,)),
            pltpu.SemaphoreType.DMA((count,)),
            pltpu.SemaphoreType.DMA(()),
        ],
        compiler_params=pltpu.CompilerParams(collective_id=ident, has_side_effects=True),
    )(x)


def attention_kernel(
    slots_ref, len_ref, q_ref, nk_ref, nv_ref, arr_ref, o_ref, kbuf, vbuf, m_sc, l_sc, acc_sc
):
    head = pl.program_id(0)
    rows, width = q_ref.shape
    page = arr_ref.shape[2]
    block_len = kbuf.shape[0]
    pages_per_block = block_len // page
    score_scale = width ** (-0.5)
    lanes = pl.ds(pl.multiple_of(head * width, width), width)
    q = q_ref[...]
    dims = (((1,), (1,)), ((), ()))
    scores = lax.dot_general(q, nk_ref[...], dims, preferred_element_type=jnp.float32) * score_scale
    row_i = lax.broadcasted_iota(jnp.int32, (rows, rows), 0)
    col_i = lax.broadcasted_iota(jnp.int32, (rows, rows), 1)
    scores = jnp.where(col_i <= row_i, scores, -1e30)
    peak = jnp.max(scores, axis=-1, keepdims=True)
    weights = jnp.exp(scores - peak)
    m_sc[...] = peak
    l_sc[...] = jnp.sum(weights, axis=-1, keepdims=True)
    acc_sc[...] = jnp.dot(weights.astype(jnp.bfloat16), nv_ref[...], preferred_element_type=jnp.float32)
    length = len_ref[0]
    block_count = (length + block_len - 1) // block_len

    def one_block(b, carry):
        for i in range(pages_per_block):
            slot = slots_ref[b * pages_per_block + i]
            kbuf[pl.ds(i * page, page), :] = arr_ref[slot, 0, :, lanes]
            vbuf[pl.ds(i * page, page), :] = arr_ref[slot, 1, :, lanes]
        block_scores = (
            lax.dot_general(q, kbuf[...], dims, preferred_element_type=jnp.float32) * score_scale
        )
        position = b * block_len + lax.broadcasted_iota(jnp.int32, (rows, block_len), 1)
        block_scores = jnp.where(position < length, block_scores, -1e30)
        old_peak = m_sc[...]
        new_peak = jnp.maximum(old_peak, jnp.max(block_scores, axis=-1, keepdims=True))
        block_weights = jnp.exp(block_scores - new_peak)
        factor = jnp.exp(old_peak - new_peak)
        l_sc[...] = l_sc[...] * factor + jnp.sum(block_weights, axis=-1, keepdims=True)
        acc_sc[...] = acc_sc[...] * factor + jnp.dot(
            block_weights.astype(jnp.bfloat16), vbuf[...], preferred_element_type=jnp.float32
        )
        m_sc[...] = new_peak
        return carry

    lax.fori_loop(0, block_count, one_block, 0)
    o_ref[...] = (acc_sc[...] / l_sc[...]).astype(o_ref.dtype)


def paged_attention(slots, length, queries, new_keys, new_values, arrived, block_len):
    rows, local_width = queries.shape
    heads = local_width // HEAD_DIM
    slot_count, _, page, _ = arrived.shape
    column = lambda h, *_: (0, h)
    spec = pl.BlockSpec((rows, HEAD_DIM), column)
    cost = pl.CostEstimate(
        flops=4 * rows * (rows + CTX) * local_width,
        transcendentals=rows * (rows + CTX) * heads,
        bytes_accessed=arrived.size * 2 + 4 * rows * local_width * 2,
    )
    return pl.pallas_call(
        attention_kernel,
        out_shape=jax.ShapeDtypeStruct((rows, local_width), jnp.bfloat16),
        grid_spec=pltpu.PrefetchScalarGridSpec(
            num_scalar_prefetch=2,
            grid=(heads,),
            in_specs=[
                spec,
                spec,
                spec,
                pl.BlockSpec(arrived.shape, lambda h, *_: (0, 0, 0, 0)),
            ],
            out_specs=spec,
            scratch_shapes=[
                pltpu.VMEM((block_len, HEAD_DIM), jnp.bfloat16),
                pltpu.VMEM((block_len, HEAD_DIM), jnp.bfloat16),
                pltpu.VMEM((rows, 1), jnp.float32),
                pltpu.VMEM((rows, 1), jnp.float32),
                pltpu.VMEM((rows, HEAD_DIM), jnp.float32),
            ],
        ),
        compiler_params=pltpu.CompilerParams(vmem_limit_bytes=48 * 1024 * 1024),
        cost_estimate=cost,
    )(slots, length, queries, new_keys, new_values, arrived)


def shards(
    hidden_in,
    cache_len,
    page_table,
    pool,
    attn_gain,
    w_qkv,
    w_out,
    moe_gain,
    w_gate,
    w_up,
    w_down,
    expert_ids,
    gate_weights,
):
    groups = lax.axis_size("group")
    expert_lanes = lax.axis_size(EXPERT)
    group_index = lax.axis_index("group")
    tok_rows = hidden_in.shape[0]
    model_width = hidden_in.shape[1]
    local_width = w_out.shape[0]
    head_size = HEAD_DIM
    local_heads = local_width // head_size
    new_count = tok_rows * expert_lanes
    block_len = CTX // NBLK
    length = cache_len[group_index]
    normed = norm_rows(hidden_in, attn_gain)
    projection = w_qkv.reshape(model_width, 3 * local_width)
    projected = jnp.dot(
        lax.all_gather(normed, EXPERT, axis=0, tiled=True),
        projection,
        preferred_element_type=jnp.float32,
    )
    projected = projected.reshape(new_count, 3, local_heads, head_size)
    positions = (length + jnp.arange(new_count, dtype=jnp.int32)).astype(jnp.float32)
    queries = rotate(projected[:, 0], positions).astype(jnp.bfloat16)
    new_keys = rotate(projected[:, 1], positions).astype(jnp.bfloat16)
    new_values = projected[:, 2].astype(jnp.bfloat16)
    pages_per = page_table.shape[1]
    page_most = max(1, pages_per // min(groups, 16))
    owner_group = page_table // pages_per
    local_slot = page_table % pages_per
    page_order = jnp.arange(pages_per, dtype=jnp.int32)
    mine = (owner_group == group_index).astype(jnp.int32)
    mine_rank = jnp.cumsum(mine, axis=1) - mine
    slot_ids = jnp.arange(page_most, dtype=jnp.int32)
    pick = (mine[:, None, :] > 0) & (mine_rank[:, None, :] == slot_ids[None, :, None])
    send_index = jnp.sum(jnp.where(pick, local_slot[:, None, :], 0), axis=-1)
    outgoing = pool[send_index]
    arrived = lax.all_to_all(outgoing, "group", split_axis=0, concat_axis=0, tiled=True)
    arrived = arrived.reshape((groups * page_most,) + pool.shape[1:])
    my_owner = owner_group[group_index]
    before = page_order[None, :] < page_order[:, None]
    my_rank = jnp.sum(jnp.logical_and(my_owner[:, None] == my_owner[None, :], before), axis=-1)
    slots = (my_owner * page_most + my_rank).astype(jnp.int32)
    attended = paged_attention(
        slots,
        jnp.reshape(length, (1,)).astype(jnp.int32),
        queries.reshape(new_count, local_width),
        new_keys.reshape(new_count, local_width),
        new_values.reshape(new_count, local_width),
        arrived,
        block_len,
    )
    rows_piece = attended
    head_parts = jnp.dot(rows_piece, w_out, preferred_element_type=jnp.float32).astype(jnp.bfloat16)
    chips = lax.axis_size("ey")
    cores = lax.axis_size("ec")
    head_parts = head_parts.reshape(chips, cores, tok_rows, model_width)
    head_parts = exchange(head_parts, ("ec",), 2, split=1)
    head_parts = jnp.sum(head_parts.astype(jnp.float32), axis=1).astype(jnp.bfloat16)
    head_parts = exchange(head_parts, ("ey",), 3)
    head_sum = jnp.sum(head_parts.astype(jnp.float32), axis=0)
    residual = hidden_in.astype(jnp.float32) + head_sum
    moe_in = norm_rows(residual, moe_gain)
    route_count = expert_ids.shape[1]
    capacity = 2 * tok_rows * route_count // expert_lanes
    flat_expert = expert_ids.reshape(-1)
    assign_index = jnp.arange(flat_expert.shape[0], dtype=jnp.int32)
    earlier = assign_index[None, :] < assign_index[:, None]
    slot_index = jnp.sum(
        jnp.logical_and(flat_expert[:, None] == flat_expert[None, :], earlier), axis=-1
    )
    token_of = assign_index // route_count
    slot_of = flat_expert * capacity + slot_index
    dest_ids = jnp.arange(expert_lanes * capacity, dtype=jnp.int32)
    token_ids = jnp.arange(tok_rows, dtype=jnp.int32)
    hit = (slot_of[None, :] == dest_ids[:, None])
    source_token = jnp.sum(jnp.where(hit, token_of[None, :], 0), axis=-1)
    has_source = jnp.any(hit, axis=-1)
    select = ((source_token[:, None] == token_ids[None, :]) & has_source[:, None]).astype(jnp.bfloat16)
    outgoing_rows = (
        jnp.dot(select, moe_in, preferred_element_type=jnp.float32)
        .astype(jnp.bfloat16)
        .reshape(expert_lanes, capacity, model_width)
    )
    rows_piece = exchange(outgoing_rows, EXPERT, 0)
    flat_rows = rows_piece.reshape(-1, rows_piece.shape[-1])
    gate_part = jnp.dot(flat_rows, w_gate[0], preferred_element_type=jnp.float32)
    up_part = jnp.dot(flat_rows, w_up[0], preferred_element_type=jnp.float32)
    hidden = (jax.nn.silu(gate_part) * up_part).astype(jnp.bfloat16)
    result = (
        jnp.dot(hidden, w_down[0], preferred_element_type=jnp.float32)
        .astype(jnp.bfloat16)
        .reshape(rows_piece.shape)
    )
    returned = exchange(result, EXPERT, 1)
    picked = returned.reshape(expert_lanes * capacity, model_width)[
        flat_expert * capacity + slot_index
    ]
    weighted = jnp.sum(
        picked.reshape(tok_rows, route_count, model_width).astype(jnp.float32)
        * gate_weights[..., None],
        axis=1,
    )
    return residual + weighted


def solution(mesh):
    lanes = mesh.shape["expert"]
    cores = 2 if lanes % 2 == 0 else 1
    split = jax.sharding.Mesh(
        mesh.devices.reshape(mesh.shape["group"], lanes // cores, cores), ("group",) + EXPERT
    )
    rows = ("group",) + EXPERT
    placed = (
        P(rows, None),
        P(),
        P(),
        P("group", None, None, EXPERT),
        P(),
        P(None, None, EXPERT),
        P(EXPERT, None),
        P(),
        P(EXPERT, None, None),
        P(EXPERT, None, None),
        P(EXPERT, None, None),
        P(rows, None),
        P(rows, None),
    )
    return jax.shard_map(
        shards, mesh=split, in_specs=placed, out_specs=P(rows, None), check_vma=False
    )
```

```python
import functools

import jax
import jax.numpy as jnp
from jax import lax
from jax.experimental import pallas as pl
from jax.experimental.pallas import tpu as pltpu
from jax.sharding import PartitionSpec as P

HEAD_DIM = 128
EXPERT = ("ey", "ec")
MESH_AXES = ("group", "ey", "ec")
MESH_IDS = pl.DeviceIdType.MESH
NBLK = 8
CTX = 2048


def norm_rows(inputs, gain_vector):
    values = inputs.astype(jnp.float32)
    factor = lax.rsqrt(jnp.mean(values * values, axis=-1, keepdims=True) + 1e-05)
    return (values * factor * gain_vector).astype(jnp.bfloat16)


def rotate(vectors, positions):
    half_dim = vectors.shape[-1] // 2
    frequency = 10000.0 ** (-jnp.arange(half_dim).astype(jnp.float32) / half_dim)
    angles = positions[:, None] * frequency[None, :]
    cosine = jnp.cos(angles)[:, None, :]
    sine_part = jnp.sin(angles)[:, None, :]
    first_half = vectors[..., :half_dim]
    second_half = vectors[..., half_dim:]
    return jnp.concatenate(
        [
            first_half * cosine - second_half * sine_part,
            first_half * sine_part + second_half * cosine,
        ],
        axis=-1,
    )


def attend_block(softmax_state, queries, key_block, value_block, key_valid):
    old_peak, old_total, old_mixed = softmax_state
    score_scale = queries.shape[-1] ** (-0.5)
    scores = (
        jnp.einsum("qhd,khd->hqk", queries, key_block, preferred_element_type=jnp.float32)
        * score_scale
    )
    scores = jnp.where(key_valid[None], scores, -1e30)
    new_peak = jnp.maximum(old_peak, jnp.max(scores, axis=-1))
    weights = jnp.exp(scores - new_peak[..., None])
    factor = jnp.exp(old_peak - new_peak)
    new_total = old_total * factor + jnp.sum(weights, axis=-1)
    new_mixed = old_mixed * factor[..., None] + jnp.einsum(
        "hqk,khd->hqd",
        weights.astype(jnp.bfloat16),
        value_block,
        preferred_element_type=jnp.float32,
    )
    return (new_peak, new_total, new_mixed)


def cache_pass(
    softmax_state,
    queries,
    all_keys,
    all_values,
    length,
    turn_count,
    array_step,
    array_first,
    position_step,
    position_first,
    block_len,
):

    def step_once(turn_index, running):
        array_start = (array_first + array_step * turn_index) * block_len
        position_start = (position_first + position_step * turn_index) * block_len
        key_block = lax.dynamic_slice_in_dim(all_keys, array_start, block_len, 0)
        value_block = lax.dynamic_slice_in_dim(all_values, array_start, block_len, 0)
        key_valid = (position_start + jnp.arange(block_len, dtype=jnp.int32) < length)[None, :]
        return attend_block(running, queries, key_block, value_block, key_valid)

    return lax.fori_loop(0, turn_count, step_once, softmax_state)


def exchange_kernel(axes, split, x_ref, o_ref, send_sems, recv_sems, own_sem):
    sizes = [lax.axis_size(a) for a in axes]
    count = 1
    for size in sizes:
        count *= size
    me = 0
    for a, size in zip(axes, sizes):
        me = me * size + lax.axis_index(a)

    def device_of(peer):
        coords = {}
        rest = peer
        for a, size in reversed(list(zip(axes, sizes))):
            coords[a] = rest % size
            rest = rest // size
        return tuple(coords.get(a, lax.axis_index(a)) for a in MESH_AXES)

    barrier = pltpu.get_barrier_semaphore()
    for k in range(1, count):
        pl.semaphore_signal(
            barrier, inc=1, device_id=device_of((me + k) % count), device_id_type=MESH_IDS
        )
    pl.semaphore_wait(barrier, count - 1)
    def block(ref, index):
        return ref.at[index] if split == 0 else ref.at[:, index]

    own = pltpu.make_async_copy(block(x_ref, me), block(o_ref, me), own_sem)
    own.start()
    copies = []
    for k in range(1, count):
        peer = (me + k) % count
        copy = pltpu.make_async_remote_copy(
            src_ref=block(x_ref, peer),
            dst_ref=block(o_ref, me),
            send_sem=send_sems.at[k],
            recv_sem=recv_sems.at[k],
            device_id=device_of(peer),
            device_id_type=MESH_IDS,
        )
        copy.start()
        copies.append(copy)
    own.wait()
    for copy in copies:
        copy.wait()


def exchange(x, axes, ident, split=0):
    count = x.shape[split]
    return pl.pallas_call(
        functools.partial(exchange_kernel, axes, split),
        out_shape=jax.ShapeDtypeStruct(x.shape, x.dtype),
        in_specs=[pl.BlockSpec(memory_space=pl.ANY)],
        out_specs=pl.BlockSpec(memory_space=pl.ANY),
        scratch_shapes=[
            pltpu.SemaphoreType.DMA((count,)),
            pltpu.SemaphoreType.DMA((count,)),
            pltpu.SemaphoreType.DMA(()),
        ],
        compiler_params=pltpu.CompilerParams(collective_id=ident, has_side_effects=True),
    )(x)


def attention_kernel(
    slots_ref, len_ref, q_ref, nk_ref, nv_ref, arr_ref, o_ref, kbuf, vbuf, m_sc, l_sc, acc_sc
):
    head = pl.program_id(0)
    rows, width = q_ref.shape
    page = arr_ref.shape[2]
    block_len = kbuf.shape[0]
    pages_per_block = block_len // page
    score_scale = width ** (-0.5)
    lanes = pl.ds(pl.multiple_of(head * width, width), width)
    q = q_ref[...]
    dims = (((1,), (1,)), ((), ()))
    scores = lax.dot_general(q, nk_ref[...], dims, preferred_element_type=jnp.float32) * score_scale
    row_i = lax.broadcasted_iota(jnp.int32, (rows, rows), 0)
    col_i = lax.broadcasted_iota(jnp.int32, (rows, rows), 1)
    scores = jnp.where(col_i <= row_i, scores, -1e30)
    peak = jnp.max(scores, axis=-1, keepdims=True)
    weights = jnp.exp(scores - peak)
    m_sc[...] = peak
    l_sc[...] = jnp.sum(weights, axis=-1, keepdims=True)
    acc_sc[...] = jnp.dot(weights.astype(jnp.bfloat16), nv_ref[...], preferred_element_type=jnp.float32)
    length = len_ref[0]
    block_count = (length + block_len - 1) // block_len

    def one_block(b, carry):
        for i in range(pages_per_block):
            slot = slots_ref[b * pages_per_block + i]
            kbuf[pl.ds(i * page, page), :] = arr_ref[slot, 0, :, lanes]
            vbuf[pl.ds(i * page, page), :] = arr_ref[slot, 1, :, lanes]
        block_scores = (
            lax.dot_general(q, kbuf[...], dims, preferred_element_type=jnp.float32) * score_scale
        )
        position = b * block_len + lax.broadcasted_iota(jnp.int32, (rows, block_len), 1)
        block_scores = jnp.where(position < length, block_scores, -1e30)
        old_peak = m_sc[...]
        new_peak = jnp.maximum(old_peak, jnp.max(block_scores, axis=-1, keepdims=True))
        block_weights = jnp.exp(block_scores - new_peak)
        factor = jnp.exp(old_peak - new_peak)
        l_sc[...] = l_sc[...] * factor + jnp.sum(block_weights, axis=-1, keepdims=True)
        acc_sc[...] = acc_sc[...] * factor + jnp.dot(
            block_weights.astype(jnp.bfloat16), vbuf[...], preferred_element_type=jnp.float32
        )
        m_sc[...] = new_peak
        return carry

    lax.fori_loop(0, block_count, one_block, 0)
    o_ref[...] = (acc_sc[...] / l_sc[...]).astype(o_ref.dtype)


def paged_attention(slots, length, queries, new_keys, new_values, arrived, block_len):
    rows, local_width = queries.shape
    heads = local_width // HEAD_DIM
    slot_count, _, page, _ = arrived.shape
    column = lambda h, *_: (0, h)
    spec = pl.BlockSpec((rows, HEAD_DIM), column)
    cost = pl.CostEstimate(
        flops=4 * rows * (rows + CTX) * local_width,
        transcendentals=rows * (rows + CTX) * heads,
        bytes_accessed=arrived.size * 2 + 4 * rows * local_width * 2,
    )
    return pl.pallas_call(
        attention_kernel,
        out_shape=jax.ShapeDtypeStruct((rows, local_width), jnp.bfloat16),
        grid_spec=pltpu.PrefetchScalarGridSpec(
            num_scalar_prefetch=2,
            grid=(heads,),
            in_specs=[
                spec,
                spec,
                spec,
                pl.BlockSpec(arrived.shape, lambda h, *_: (0, 0, 0, 0)),
            ],
            out_specs=spec,
            scratch_shapes=[
                pltpu.VMEM((block_len, HEAD_DIM), jnp.bfloat16),
                pltpu.VMEM((block_len, HEAD_DIM), jnp.bfloat16),
                pltpu.VMEM((rows, 1), jnp.float32),
                pltpu.VMEM((rows, 1), jnp.float32),
                pltpu.VMEM((rows, HEAD_DIM), jnp.float32),
            ],
        ),
        compiler_params=pltpu.CompilerParams(vmem_limit_bytes=48 * 1024 * 1024),
        cost_estimate=cost,
    )(slots, length, queries, new_keys, new_values, arrived)


def shards(
    hidden_in,
    cache_len,
    page_table,
    pool,
    attn_gain,
    w_qkv,
    w_out,
    moe_gain,
    w_gate,
    w_up,
    w_down,
    expert_ids,
    gate_weights,
):
    groups = lax.axis_size("group")
    expert_lanes = lax.axis_size(EXPERT)
    group_index = lax.axis_index("group")
    tok_rows = hidden_in.shape[0]
    model_width = hidden_in.shape[1]
    local_width = w_out.shape[0]
    head_size = HEAD_DIM
    local_heads = local_width // head_size
    new_count = tok_rows * expert_lanes
    block_len = CTX // NBLK
    length = cache_len[group_index]
    normed = norm_rows(hidden_in, attn_gain)
    projection = w_qkv.reshape(model_width, 3 * local_width)
    projected = jnp.dot(
        lax.all_gather(normed, EXPERT, axis=0, tiled=True),
        projection,
        preferred_element_type=jnp.float32,
    )
    projected = projected.reshape(new_count, 3, local_heads, head_size)
    positions = (length + jnp.arange(new_count, dtype=jnp.int32)).astype(jnp.float32)
    queries = rotate(projected[:, 0], positions).astype(jnp.bfloat16)
    new_keys = rotate(projected[:, 1], positions).astype(jnp.bfloat16)
    new_values = projected[:, 2].astype(jnp.bfloat16)
    pages_per = page_table.shape[1]
    page_most = max(1, pages_per // min(groups, 16))
    owner_group = page_table // pages_per
    local_slot = page_table % pages_per
    page_order = jnp.arange(pages_per, dtype=jnp.int32)
    mine = (owner_group == group_index).astype(jnp.int32)
    mine_rank = jnp.cumsum(mine, axis=1) - mine
    slot_ids = jnp.arange(page_most, dtype=jnp.int32)
    pick = (mine[:, None, :] > 0) & (mine_rank[:, None, :] == slot_ids[None, :, None])
    send_index = jnp.sum(jnp.where(pick, local_slot[:, None, :], 0), axis=-1)
    outgoing = pool[send_index]
    arrived = lax.all_to_all(outgoing, "group", split_axis=0, concat_axis=0, tiled=True)
    arrived = arrived.reshape((groups * page_most,) + pool.shape[1:])
    my_owner = owner_group[group_index]
    before = page_order[None, :] < page_order[:, None]
    my_rank = jnp.sum(jnp.logical_and(my_owner[:, None] == my_owner[None, :], before), axis=-1)
    slots = (my_owner * page_most + my_rank).astype(jnp.int32)
    attended = paged_attention(
        slots,
        jnp.reshape(length, (1,)).astype(jnp.int32),
        queries.reshape(new_count, local_width),
        new_keys.reshape(new_count, local_width),
        new_values.reshape(new_count, local_width),
        arrived,
        block_len,
    )
    chips = lax.axis_size("ey")
    cores = lax.axis_size("ec")
    rows_piece = jnp.transpose(
        attended.reshape(chips, cores, tok_rows, local_width), (1, 0, 2, 3)
    ).reshape(new_count, local_width)
    head_parts = jnp.dot(rows_piece, w_out, preferred_element_type=jnp.float32).astype(jnp.bfloat16)
    head_parts = head_parts.reshape(cores, chips, tok_rows, model_width)
    head_parts = exchange(head_parts, ("ec",), 2)
    head_parts = jnp.sum(head_parts.astype(jnp.float32), axis=0).astype(jnp.bfloat16)
    head_parts = exchange(head_parts, ("ey",), 3)
    head_sum = jnp.sum(head_parts.astype(jnp.float32), axis=0)
    residual = hidden_in.astype(jnp.float32) + head_sum
    moe_in = norm_rows(residual, moe_gain)
    route_count = expert_ids.shape[1]
    capacity = 2 * tok_rows * route_count // expert_lanes
    flat_expert = expert_ids.reshape(-1)
    assign_index = jnp.arange(flat_expert.shape[0], dtype=jnp.int32)
    earlier = assign_index[None, :] < assign_index[:, None]
    slot_index = jnp.sum(
        jnp.logical_and(flat_expert[:, None] == flat_expert[None, :], earlier), axis=-1
    )
    token_of = assign_index // route_count
    slot_of = flat_expert * capacity + slot_index
    dest_ids = jnp.arange(expert_lanes * capacity, dtype=jnp.int32)
    token_ids = jnp.arange(tok_rows, dtype=jnp.int32)
    hit = (slot_of[None, :] == dest_ids[:, None])
    source_token = jnp.sum(jnp.where(hit, token_of[None, :], 0), axis=-1)
    has_source = jnp.any(hit, axis=-1)
    select = ((source_token[:, None] == token_ids[None, :]) & has_source[:, None]).astype(jnp.bfloat16)
    outgoing_rows = (
        jnp.dot(select, moe_in, preferred_element_type=jnp.float32)
        .astype(jnp.bfloat16)
        .reshape(expert_lanes, capacity, model_width)
    )
    rows_piece = exchange(outgoing_rows, EXPERT, 0)
    flat_rows = rows_piece.reshape(-1, rows_piece.shape[-1])
    gate_part = jnp.dot(flat_rows, w_gate[0], preferred_element_type=jnp.float32)
    up_part = jnp.dot(flat_rows, w_up[0], preferred_element_type=jnp.float32)
    hidden = (jax.nn.silu(gate_part) * up_part).astype(jnp.bfloat16)
    result = (
        jnp.dot(hidden, w_down[0], preferred_element_type=jnp.float32)
        .astype(jnp.bfloat16)
        .reshape(rows_piece.shape)
    )
    returned = exchange(result, EXPERT, 1)
    picked = returned.reshape(expert_lanes * capacity, model_width)[
        flat_expert * capacity + slot_index
    ]
    weighted = jnp.sum(
        picked.reshape(tok_rows, route_count, model_width).astype(jnp.float32)
        * gate_weights[..., None],
        axis=1,
    )
    return residual + weighted


def solution(mesh):
    lanes = mesh.shape["expert"]
    cores = 2 if lanes % 2 == 0 else 1
    split = jax.sharding.Mesh(
        mesh.devices.reshape(mesh.shape["group"], lanes // cores, cores), ("group",) + EXPERT
    )
    rows = ("group",) + EXPERT
    placed = (
        P(rows, None),
        P(),
        P(),
        P("group", None, None, EXPERT),
        P(),
        P(None, None, EXPERT),
        P(EXPERT, None),
        P(),
        P(EXPERT, None, None),
        P(EXPERT, None, None),
        P(EXPERT, None, None),
        P(rows, None),
        P(rows, None),
    )
    return jax.shard_map(
        shards, mesh=split, in_specs=placed, out_specs=P(rows, None), check_vma=False
    )
```

```python
import functools

import jax
import jax.numpy as jnp
from jax import lax
from jax.experimental import pallas as pl
from jax.experimental.pallas import tpu as pltpu
from jax.sharding import PartitionSpec as P

HEAD_DIM = 128
EXPERT = ("ey", "ec")
MESH_AXES = ("group", "ey", "ec")
MESH_IDS = pl.DeviceIdType.MESH
NBLK = 8
CTX = 2048


def norm_rows(inputs, gain_vector):
    values = inputs.astype(jnp.float32)
    factor = lax.rsqrt(jnp.mean(values * values, axis=-1, keepdims=True) + 1e-05)
    return (values * factor * gain_vector).astype(jnp.bfloat16)


def rotate(vectors, positions):
    half_dim = vectors.shape[-1] // 2
    frequency = 10000.0 ** (-jnp.arange(half_dim).astype(jnp.float32) / half_dim)
    angles = positions[:, None] * frequency[None, :]
    cosine = jnp.cos(angles)[:, None, :]
    sine_part = jnp.sin(angles)[:, None, :]
    first_half = vectors[..., :half_dim]
    second_half = vectors[..., half_dim:]
    return jnp.concatenate(
        [
            first_half * cosine - second_half * sine_part,
            first_half * sine_part + second_half * cosine,
        ],
        axis=-1,
    )


def attend_block(softmax_state, queries, key_block, value_block, key_valid):
    old_peak, old_total, old_mixed = softmax_state
    score_scale = queries.shape[-1] ** (-0.5)
    scores = (
        jnp.einsum("qhd,khd->hqk", queries, key_block, preferred_element_type=jnp.float32)
        * score_scale
    )
    scores = jnp.where(key_valid[None], scores, -1e30)
    new_peak = jnp.maximum(old_peak, jnp.max(scores, axis=-1))
    weights = jnp.exp(scores - new_peak[..., None])
    factor = jnp.exp(old_peak - new_peak)
    new_total = old_total * factor + jnp.sum(weights, axis=-1)
    new_mixed = old_mixed * factor[..., None] + jnp.einsum(
        "hqk,khd->hqd",
        weights.astype(jnp.bfloat16),
        value_block,
        preferred_element_type=jnp.float32,
    )
    return (new_peak, new_total, new_mixed)


def cache_pass(
    softmax_state,
    queries,
    all_keys,
    all_values,
    length,
    turn_count,
    array_step,
    array_first,
    position_step,
    position_first,
    block_len,
):

    def step_once(turn_index, running):
        array_start = (array_first + array_step * turn_index) * block_len
        position_start = (position_first + position_step * turn_index) * block_len
        key_block = lax.dynamic_slice_in_dim(all_keys, array_start, block_len, 0)
        value_block = lax.dynamic_slice_in_dim(all_values, array_start, block_len, 0)
        key_valid = (position_start + jnp.arange(block_len, dtype=jnp.int32) < length)[None, :]
        return attend_block(running, queries, key_block, value_block, key_valid)

    return lax.fori_loop(0, turn_count, step_once, softmax_state)


def exchange_kernel(axes, split, x_ref, o_ref, send_sems, recv_sems, own_sem):
    sizes = [lax.axis_size(a) for a in axes]
    count = 1
    for size in sizes:
        count *= size
    me = 0
    for a, size in zip(axes, sizes):
        me = me * size + lax.axis_index(a)

    def device_of(peer):
        coords = {}
        rest = peer
        for a, size in reversed(list(zip(axes, sizes))):
            coords[a] = rest % size
            rest = rest // size
        return tuple(coords.get(a, lax.axis_index(a)) for a in MESH_AXES)

    barrier = pltpu.get_barrier_semaphore()
    for k in range(1, count):
        pl.semaphore_signal(
            barrier, inc=1, device_id=device_of((me + k) % count), device_id_type=MESH_IDS
        )
    pl.semaphore_wait(barrier, count - 1)
    def block(ref, index):
        return ref.at[index] if split == 0 else ref.at[:, index]

    own = pltpu.make_async_copy(block(x_ref, me), block(o_ref, me), own_sem)
    own.start()
    copies = []
    for k in range(1, count):
        peer = (me + k) % count
        copy = pltpu.make_async_remote_copy(
            src_ref=block(x_ref, peer),
            dst_ref=block(o_ref, me),
            send_sem=send_sems.at[k],
            recv_sem=recv_sems.at[k],
            device_id=device_of(peer),
            device_id_type=MESH_IDS,
        )
        copy.start()
        copies.append(copy)
    own.wait()
    for copy in copies:
        copy.wait()


def exchange(x, axes, ident, split=0):
    count = x.shape[split]
    return pl.pallas_call(
        functools.partial(exchange_kernel, axes, split),
        out_shape=jax.ShapeDtypeStruct(x.shape, x.dtype),
        in_specs=[pl.BlockSpec(memory_space=pl.ANY)],
        out_specs=pl.BlockSpec(memory_space=pl.ANY),
        scratch_shapes=[
            pltpu.SemaphoreType.DMA((count,)),
            pltpu.SemaphoreType.DMA((count,)),
            pltpu.SemaphoreType.DMA(()),
        ],
        compiler_params=pltpu.CompilerParams(collective_id=ident, has_side_effects=True),
    )(x)


def attention_kernel(
    slots_ref, len_ref, q_ref, nk_ref, nv_ref, arr_ref, o_ref, kbuf, vbuf, m_sc, l_sc, acc_sc
):
    head = pl.program_id(0)
    rows, width = q_ref.shape
    page = arr_ref.shape[2]
    block_len = kbuf.shape[0]
    pages_per_block = block_len // page
    score_scale = width ** (-0.5)
    lanes = pl.ds(pl.multiple_of(head * width, width), width)
    q = q_ref[...]
    dims = (((1,), (1,)), ((), ()))
    scores = lax.dot_general(q, nk_ref[...], dims, preferred_element_type=jnp.float32) * score_scale
    row_i = lax.broadcasted_iota(jnp.int32, (rows, rows), 0)
    col_i = lax.broadcasted_iota(jnp.int32, (rows, rows), 1)
    scores = jnp.where(col_i <= row_i, scores, -1e30)
    peak = jnp.max(scores, axis=-1, keepdims=True)
    weights = jnp.exp(scores - peak)
    m_sc[...] = peak
    l_sc[...] = jnp.sum(weights, axis=-1, keepdims=True)
    acc_sc[...] = jnp.dot(weights.astype(jnp.bfloat16), nv_ref[...], preferred_element_type=jnp.float32)
    length = len_ref[0]
    block_count = (length + block_len - 1) // block_len

    def one_block(b, carry):
        for i in range(pages_per_block):
            slot = slots_ref[b * pages_per_block + i]
            kbuf[pl.ds(i * page, page), :] = arr_ref[slot, 0, :, lanes]
            vbuf[pl.ds(i * page, page), :] = arr_ref[slot, 1, :, lanes]
        block_scores = (
            lax.dot_general(q, kbuf[...], dims, preferred_element_type=jnp.float32) * score_scale
        )
        position = b * block_len + lax.broadcasted_iota(jnp.int32, (rows, block_len), 1)
        block_scores = jnp.where(position < length, block_scores, -1e30)
        old_peak = m_sc[...]
        new_peak = jnp.maximum(old_peak, jnp.max(block_scores, axis=-1, keepdims=True))
        block_weights = jnp.exp(block_scores - new_peak)
        factor = jnp.exp(old_peak - new_peak)
        l_sc[...] = l_sc[...] * factor + jnp.sum(block_weights, axis=-1, keepdims=True)
        acc_sc[...] = acc_sc[...] * factor + jnp.dot(
            block_weights.astype(jnp.bfloat16), vbuf[...], preferred_element_type=jnp.float32
        )
        m_sc[...] = new_peak
        return carry

    lax.fori_loop(0, block_count, one_block, 0)
    o_ref[...] = (acc_sc[...] / l_sc[...]).astype(o_ref.dtype)


def paged_attention(slots, length, queries, new_keys, new_values, arrived, block_len):
    rows, local_width = queries.shape
    heads = local_width // HEAD_DIM
    slot_count, _, page, _ = arrived.shape
    column = lambda h, *_: (0, h)
    spec = pl.BlockSpec((rows, HEAD_DIM), column)
    cost = pl.CostEstimate(
        flops=4 * rows * (rows + CTX) * local_width,
        transcendentals=rows * (rows + CTX) * heads,
        bytes_accessed=arrived.size * 2 + 4 * rows * local_width * 2,
    )
    return pl.pallas_call(
        attention_kernel,
        out_shape=jax.ShapeDtypeStruct((rows, local_width), jnp.bfloat16),
        grid_spec=pltpu.PrefetchScalarGridSpec(
            num_scalar_prefetch=2,
            grid=(heads,),
            in_specs=[
                spec,
                spec,
                spec,
                pl.BlockSpec(arrived.shape, lambda h, *_: (0, 0, 0, 0)),
            ],
            out_specs=spec,
            scratch_shapes=[
                pltpu.VMEM((block_len, HEAD_DIM), jnp.bfloat16),
                pltpu.VMEM((block_len, HEAD_DIM), jnp.bfloat16),
                pltpu.VMEM((rows, 1), jnp.float32),
                pltpu.VMEM((rows, 1), jnp.float32),
                pltpu.VMEM((rows, HEAD_DIM), jnp.float32),
            ],
        ),
        compiler_params=pltpu.CompilerParams(vmem_limit_bytes=48 * 1024 * 1024),
        cost_estimate=cost,
    )(slots, length, queries, new_keys, new_values, arrived)


def shards(
    hidden_in,
    cache_len,
    page_table,
    pool,
    attn_gain,
    w_qkv,
    w_out,
    moe_gain,
    w_gate,
    w_up,
    w_down,
    expert_ids,
    gate_weights,
):
    groups = lax.axis_size("group")
    expert_lanes = lax.axis_size(EXPERT)
    group_index = lax.axis_index("group")
    tok_rows = hidden_in.shape[0]
    model_width = hidden_in.shape[1]
    local_width = w_out.shape[0]
    head_size = HEAD_DIM
    local_heads = local_width // head_size
    new_count = tok_rows * expert_lanes
    block_len = CTX // NBLK
    length = cache_len[group_index]
    normed = norm_rows(hidden_in, attn_gain)
    projection = w_qkv.reshape(model_width, 3 * local_width)
    projected = jnp.dot(
        lax.all_gather(normed, EXPERT, axis=0, tiled=True),
        projection,
        preferred_element_type=jnp.float32,
    )
    projected = projected.reshape(new_count, 3, local_heads, head_size)
    positions = (length + jnp.arange(new_count, dtype=jnp.int32)).astype(jnp.float32)
    queries = rotate(projected[:, 0], positions).astype(jnp.bfloat16)
    new_keys = rotate(projected[:, 1], positions).astype(jnp.bfloat16)
    new_values = projected[:, 2].astype(jnp.bfloat16)
    pages_per = page_table.shape[1]
    page_most = max(1, pages_per // min(groups, 16))
    owner_group = page_table // pages_per
    local_slot = page_table % pages_per
    page_order = jnp.arange(pages_per, dtype=jnp.int32)
    mine = (owner_group == group_index).astype(jnp.int32)
    mine_rank = jnp.cumsum(mine, axis=1) - mine
    slot_ids = jnp.arange(page_most, dtype=jnp.int32)
    pick = (mine[:, None, :] > 0) & (mine_rank[:, None, :] == slot_ids[None, :, None])
    send_index = jnp.sum(jnp.where(pick, local_slot[:, None, :], 0), axis=-1)
    outgoing = pool[send_index]
    arrived = lax.all_to_all(outgoing, "group", split_axis=0, concat_axis=0, tiled=True)
    arrived = arrived.reshape((groups * page_most,) + pool.shape[1:])
    my_owner = owner_group[group_index]
    before = page_order[None, :] < page_order[:, None]
    my_rank = jnp.sum(jnp.logical_and(my_owner[:, None] == my_owner[None, :], before), axis=-1)
    slots = (my_owner * page_most + my_rank).astype(jnp.int32)
    attended = paged_attention(
        slots,
        jnp.reshape(length, (1,)).astype(jnp.int32),
        queries.reshape(new_count, local_width),
        new_keys.reshape(new_count, local_width),
        new_values.reshape(new_count, local_width),
        arrived,
        block_len,
    )
    rows_piece = attended
    head_parts = jnp.dot(rows_piece, w_out, preferred_element_type=jnp.float32).astype(jnp.bfloat16)
    chips = lax.axis_size("ey")
    cores = lax.axis_size("ec")
    head_parts = head_parts.reshape(chips, cores, tok_rows, model_width)
    head_parts = lax.all_to_all(head_parts, "ec", split_axis=1, concat_axis=1, tiled=True)
    head_parts = jnp.sum(head_parts.astype(jnp.float32), axis=1).astype(jnp.bfloat16)
    head_parts = exchange(head_parts, ("ey",), 2)
    head_sum = jnp.sum(head_parts.astype(jnp.float32), axis=0)
    residual = hidden_in.astype(jnp.float32) + head_sum
    moe_in = norm_rows(residual, moe_gain)
    route_count = expert_ids.shape[1]
    capacity = 2 * tok_rows * route_count // expert_lanes
    flat_expert = expert_ids.reshape(-1)
    assign_index = jnp.arange(flat_expert.shape[0], dtype=jnp.int32)
    earlier = assign_index[None, :] < assign_index[:, None]
    slot_index = jnp.sum(
        jnp.logical_and(flat_expert[:, None] == flat_expert[None, :], earlier), axis=-1
    )
    token_of = assign_index // route_count
    slot_of = flat_expert * capacity + slot_index
    dest_ids = jnp.arange(expert_lanes * capacity, dtype=jnp.int32)
    token_ids = jnp.arange(tok_rows, dtype=jnp.int32)
    hit = (slot_of[None, :] == dest_ids[:, None])
    source_token = jnp.sum(jnp.where(hit, token_of[None, :], 0), axis=-1)
    has_source = jnp.any(hit, axis=-1)
    select = ((source_token[:, None] == token_ids[None, :]) & has_source[:, None]).astype(jnp.bfloat16)
    outgoing_rows = (
        jnp.dot(select, moe_in, preferred_element_type=jnp.float32)
        .astype(jnp.bfloat16)
        .reshape(expert_lanes, capacity, model_width)
    )
    rows_piece = exchange(outgoing_rows, EXPERT, 0)
    flat_rows = rows_piece.reshape(-1, rows_piece.shape[-1])
    gate_part = jnp.dot(flat_rows, w_gate[0], preferred_element_type=jnp.float32)
    up_part = jnp.dot(flat_rows, w_up[0], preferred_element_type=jnp.float32)
    hidden = (jax.nn.silu(gate_part) * up_part).astype(jnp.bfloat16)
    result = (
        jnp.dot(hidden, w_down[0], preferred_element_type=jnp.float32)
        .astype(jnp.bfloat16)
        .reshape(rows_piece.shape)
    )
    returned = exchange(result, EXPERT, 1)
    picked = returned.reshape(expert_lanes * capacity, model_width)[
        flat_expert * capacity + slot_index
    ]
    weighted = jnp.sum(
        picked.reshape(tok_rows, route_count, model_width).astype(jnp.float32)
        * gate_weights[..., None],
        axis=1,
    )
    return residual + weighted


def solution(mesh):
    lanes = mesh.shape["expert"]
    cores = 2 if lanes % 2 == 0 else 1
    split = jax.sharding.Mesh(
        mesh.devices.reshape(mesh.shape["group"], lanes // cores, cores), ("group",) + EXPERT
    )
    rows = ("group",) + EXPERT
    placed = (
        P(rows, None),
        P(),
        P(),
        P("group", None, None, EXPERT),
        P(),
        P(None, None, EXPERT),
        P(EXPERT, None),
        P(),
        P(EXPERT, None, None),
        P(EXPERT, None, None),
        P(EXPERT, None, None),
        P(rows, None),
        P(rows, None),
    )
    return jax.shard_map(
        shards, mesh=split, in_specs=placed, out_specs=P(rows, None), check_vma=False
    )
```

```python
import functools

import jax
import jax.numpy as jnp
from jax import lax
from jax.experimental import pallas as pl
from jax.experimental.pallas import tpu as pltpu
from jax.sharding import PartitionSpec as P

HEAD_DIM = 128
EXPERT = ("ey", "ec")
MESH_AXES = ("group", "ey", "ec")
MESH_IDS = pl.DeviceIdType.MESH
NBLK = 8
CTX = 2048


def norm_rows(inputs, gain_vector):
    values = inputs.astype(jnp.float32)
    factor = lax.rsqrt(jnp.mean(values * values, axis=-1, keepdims=True) + 1e-05)
    return (values * factor * gain_vector).astype(jnp.bfloat16)


def rotate(vectors, positions):
    half_dim = vectors.shape[-1] // 2
    frequency = 10000.0 ** (-jnp.arange(half_dim).astype(jnp.float32) / half_dim)
    angles = positions[:, None] * frequency[None, :]
    cosine = jnp.cos(angles)[:, None, :]
    sine_part = jnp.sin(angles)[:, None, :]
    first_half = vectors[..., :half_dim]
    second_half = vectors[..., half_dim:]
    return jnp.concatenate(
        [
            first_half * cosine - second_half * sine_part,
            first_half * sine_part + second_half * cosine,
        ],
        axis=-1,
    )


def attend_block(softmax_state, queries, key_block, value_block, key_valid):
    old_peak, old_total, old_mixed = softmax_state
    score_scale = queries.shape[-1] ** (-0.5)
    scores = (
        jnp.einsum("qhd,khd->hqk", queries, key_block, preferred_element_type=jnp.float32)
        * score_scale
    )
    scores = jnp.where(key_valid[None], scores, -1e30)
    new_peak = jnp.maximum(old_peak, jnp.max(scores, axis=-1))
    weights = jnp.exp(scores - new_peak[..., None])
    factor = jnp.exp(old_peak - new_peak)
    new_total = old_total * factor + jnp.sum(weights, axis=-1)
    new_mixed = old_mixed * factor[..., None] + jnp.einsum(
        "hqk,khd->hqd",
        weights.astype(jnp.bfloat16),
        value_block,
        preferred_element_type=jnp.float32,
    )
    return (new_peak, new_total, new_mixed)


def cache_pass(
    softmax_state,
    queries,
    all_keys,
    all_values,
    length,
    turn_count,
    array_step,
    array_first,
    position_step,
    position_first,
    block_len,
):

    def step_once(turn_index, running):
        array_start = (array_first + array_step * turn_index) * block_len
        position_start = (position_first + position_step * turn_index) * block_len
        key_block = lax.dynamic_slice_in_dim(all_keys, array_start, block_len, 0)
        value_block = lax.dynamic_slice_in_dim(all_values, array_start, block_len, 0)
        key_valid = (position_start + jnp.arange(block_len, dtype=jnp.int32) < length)[None, :]
        return attend_block(running, queries, key_block, value_block, key_valid)

    return lax.fori_loop(0, turn_count, step_once, softmax_state)


def exchange_kernel(axes, split, x_ref, o_ref, send_sems, recv_sems, own_sem):
    sizes = [lax.axis_size(a) for a in axes]
    count = 1
    for size in sizes:
        count *= size
    me = 0
    for a, size in zip(axes, sizes):
        me = me * size + lax.axis_index(a)

    def device_of(peer):
        coords = {}
        rest = peer
        for a, size in reversed(list(zip(axes, sizes))):
            coords[a] = rest % size
            rest = rest // size
        return tuple(coords.get(a, lax.axis_index(a)) for a in MESH_AXES)

    barrier = pltpu.get_barrier_semaphore()
    for k in range(1, count):
        pl.semaphore_signal(
            barrier, inc=1, device_id=device_of((me + k) % count), device_id_type=MESH_IDS
        )
    pl.semaphore_wait(barrier, count - 1)
    def block(ref, index):
        return ref.at[index] if split == 0 else ref.at[:, index]

    own = pltpu.make_async_copy(block(x_ref, me), block(o_ref, me), own_sem)
    own.start()
    copies = []
    for k in range(1, count):
        peer = (me + k) % count
        copy = pltpu.make_async_remote_copy(
            src_ref=block(x_ref, peer),
            dst_ref=block(o_ref, me),
            send_sem=send_sems.at[k],
            recv_sem=recv_sems.at[k],
            device_id=device_of(peer),
            device_id_type=MESH_IDS,
        )
        copy.start()
        copies.append(copy)
    own.wait()
    for copy in copies:
        copy.wait()


def exchange(x, axes, ident, split=0):
    count = x.shape[split]
    return pl.pallas_call(
        functools.partial(exchange_kernel, axes, split),
        out_shape=jax.ShapeDtypeStruct(x.shape, x.dtype),
        in_specs=[pl.BlockSpec(memory_space=pl.ANY)],
        out_specs=pl.BlockSpec(memory_space=pl.ANY),
        scratch_shapes=[
            pltpu.SemaphoreType.DMA((count,)),
            pltpu.SemaphoreType.DMA((count,)),
            pltpu.SemaphoreType.DMA(()),
        ],
        compiler_params=pltpu.CompilerParams(collective_id=ident, has_side_effects=True),
    )(x)


def fresh_kernel(q_ref, nk_ref, nv_ref, m_ref, l_ref, acc_ref):
    rows, width = q_ref.shape
    score_scale = width ** (-0.5)
    dims = (((1,), (1,)), ((), ()))
    scores = (
        lax.dot_general(q_ref[...], nk_ref[...], dims, preferred_element_type=jnp.float32)
        * score_scale
    )
    row_i = lax.broadcasted_iota(jnp.int32, (rows, rows), 0)
    col_i = lax.broadcasted_iota(jnp.int32, (rows, rows), 1)
    scores = jnp.where(col_i <= row_i, scores, -1e30)
    peak = jnp.max(scores, axis=-1, keepdims=True)
    weights = jnp.exp(scores - peak)
    m_ref[...] = peak
    l_ref[...] = jnp.sum(weights, axis=-1, keepdims=True)
    acc_ref[...] = jnp.dot(
        weights.astype(jnp.bfloat16), nv_ref[...], preferred_element_type=jnp.float32
    )


def cache_kernel(
    slots_ref, len_ref, q_ref, m_in, l_in, acc_in, arr_ref, o_ref, kbuf, vbuf, m_sc, l_sc, acc_sc
):
    head = pl.program_id(0)
    rows, width = q_ref.shape
    page = arr_ref.shape[2]
    block_len = kbuf.shape[0]
    pages_per_block = block_len // page
    score_scale = width ** (-0.5)
    lanes = pl.ds(pl.multiple_of(head * width, width), width)
    q = q_ref[...]
    dims = (((1,), (1,)), ((), ()))
    m_sc[...] = m_in[...]
    l_sc[...] = l_in[...]
    acc_sc[...] = acc_in[...]
    length = len_ref[0]
    block_count = (length + block_len - 1) // block_len

    def one_block(b, carry):
        for i in range(pages_per_block):
            slot = slots_ref[b * pages_per_block + i]
            kbuf[pl.ds(i * page, page), :] = arr_ref[slot, 0, :, lanes]
            vbuf[pl.ds(i * page, page), :] = arr_ref[slot, 1, :, lanes]
        block_scores = (
            lax.dot_general(q, kbuf[...], dims, preferred_element_type=jnp.float32) * score_scale
        )
        position = b * block_len + lax.broadcasted_iota(jnp.int32, (rows, block_len), 1)
        block_scores = jnp.where(position < length, block_scores, -1e30)
        old_peak = m_sc[...]
        new_peak = jnp.maximum(old_peak, jnp.max(block_scores, axis=-1, keepdims=True))
        block_weights = jnp.exp(block_scores - new_peak)
        factor = jnp.exp(old_peak - new_peak)
        l_sc[...] = l_sc[...] * factor + jnp.sum(block_weights, axis=-1, keepdims=True)
        acc_sc[...] = acc_sc[...] * factor + jnp.dot(
            block_weights.astype(jnp.bfloat16), vbuf[...], preferred_element_type=jnp.float32
        )
        m_sc[...] = new_peak
        return carry

    lax.fori_loop(0, block_count, one_block, 0)
    o_ref[...] = (acc_sc[...] / l_sc[...]).astype(o_ref.dtype)


def fresh_attention(queries, new_keys, new_values):
    rows, local_width = queries.shape
    heads = local_width // HEAD_DIM
    spec = pl.BlockSpec((rows, HEAD_DIM), lambda h: (0, h))
    stat = pl.BlockSpec((None, rows, 1), lambda h: (h, 0, 0))
    cost = pl.CostEstimate(
        flops=4 * rows * rows * local_width,
        transcendentals=rows * rows * heads,
        bytes_accessed=3 * rows * local_width * 2 + rows * local_width * 4,
    )
    return pl.pallas_call(
        fresh_kernel,
        out_shape=(
            jax.ShapeDtypeStruct((heads, rows, 1), jnp.float32),
            jax.ShapeDtypeStruct((heads, rows, 1), jnp.float32),
            jax.ShapeDtypeStruct((rows, local_width), jnp.float32),
        ),
        grid=(heads,),
        in_specs=[spec, spec, spec],
        out_specs=(stat, stat, pl.BlockSpec((rows, HEAD_DIM), lambda h: (0, h))),
        cost_estimate=cost,
    )(queries, new_keys, new_values)


def paged_attention(slots, length, queries, new_keys, new_values, arrived, block_len):
    rows, local_width = queries.shape
    heads = local_width // HEAD_DIM
    peak, total, mixed = fresh_attention(queries, new_keys, new_values)
    spec = pl.BlockSpec((rows, HEAD_DIM), lambda h, *_: (0, h))
    stat = pl.BlockSpec((None, rows, 1), lambda h, *_: (h, 0, 0))
    cost = pl.CostEstimate(
        flops=4 * rows * CTX * local_width,
        transcendentals=rows * CTX * heads,
        bytes_accessed=arrived.size * 2 + 4 * rows * local_width * 2,
    )
    return pl.pallas_call(
        cache_kernel,
        out_shape=jax.ShapeDtypeStruct((rows, local_width), jnp.bfloat16),
        grid_spec=pltpu.PrefetchScalarGridSpec(
            num_scalar_prefetch=2,
            grid=(heads,),
            in_specs=[
                spec,
                stat,
                stat,
                pl.BlockSpec((rows, HEAD_DIM), lambda h, *_: (0, h)),
                pl.BlockSpec(arrived.shape, lambda h, *_: (0, 0, 0, 0)),
            ],
            out_specs=spec,
            scratch_shapes=[
                pltpu.VMEM((block_len, HEAD_DIM), jnp.bfloat16),
                pltpu.VMEM((block_len, HEAD_DIM), jnp.bfloat16),
                pltpu.VMEM((rows, 1), jnp.float32),
                pltpu.VMEM((rows, 1), jnp.float32),
                pltpu.VMEM((rows, HEAD_DIM), jnp.float32),
            ],
        ),
        compiler_params=pltpu.CompilerParams(vmem_limit_bytes=48 * 1024 * 1024),
        cost_estimate=cost,
    )(slots, length, queries, peak, total, mixed, arrived)


def shards(
    hidden_in,
    cache_len,
    page_table,
    pool,
    attn_gain,
    w_qkv,
    w_out,
    moe_gain,
    w_gate,
    w_up,
    w_down,
    expert_ids,
    gate_weights,
):
    groups = lax.axis_size("group")
    expert_lanes = lax.axis_size(EXPERT)
    group_index = lax.axis_index("group")
    tok_rows = hidden_in.shape[0]
    model_width = hidden_in.shape[1]
    local_width = w_out.shape[0]
    head_size = HEAD_DIM
    local_heads = local_width // head_size
    new_count = tok_rows * expert_lanes
    block_len = CTX // NBLK
    length = cache_len[group_index]
    normed = norm_rows(hidden_in, attn_gain)
    projection = w_qkv.reshape(model_width, 3 * local_width)
    projected = jnp.dot(
        lax.all_gather(normed, EXPERT, axis=0, tiled=True),
        projection,
        preferred_element_type=jnp.float32,
    )
    projected = projected.reshape(new_count, 3, local_heads, head_size)
    positions = (length + jnp.arange(new_count, dtype=jnp.int32)).astype(jnp.float32)
    queries = rotate(projected[:, 0], positions).astype(jnp.bfloat16)
    new_keys = rotate(projected[:, 1], positions).astype(jnp.bfloat16)
    new_values = projected[:, 2].astype(jnp.bfloat16)
    pages_per = page_table.shape[1]
    page_most = max(1, pages_per // min(groups, 16))
    owner_group = page_table // pages_per
    local_slot = page_table % pages_per
    page_order = jnp.arange(pages_per, dtype=jnp.int32)
    mine = (owner_group == group_index).astype(jnp.int32)
    mine_rank = jnp.cumsum(mine, axis=1) - mine
    slot_ids = jnp.arange(page_most, dtype=jnp.int32)
    pick = (mine[:, None, :] > 0) & (mine_rank[:, None, :] == slot_ids[None, :, None])
    send_index = jnp.sum(jnp.where(pick, local_slot[:, None, :], 0), axis=-1)
    outgoing = pool[send_index]
    arrived = lax.all_to_all(outgoing, "group", split_axis=0, concat_axis=0, tiled=True)
    arrived = arrived.reshape((groups * page_most,) + pool.shape[1:])
    my_owner = owner_group[group_index]
    before = page_order[None, :] < page_order[:, None]
    my_rank = jnp.sum(jnp.logical_and(my_owner[:, None] == my_owner[None, :], before), axis=-1)
    slots = (my_owner * page_most + my_rank).astype(jnp.int32)
    attended = paged_attention(
        slots,
        jnp.reshape(length, (1,)).astype(jnp.int32),
        queries.reshape(new_count, local_width),
        new_keys.reshape(new_count, local_width),
        new_values.reshape(new_count, local_width),
        arrived,
        block_len,
    )
    rows_piece = attended
    head_parts = jnp.dot(rows_piece, w_out, preferred_element_type=jnp.float32).astype(jnp.bfloat16)
    chips = lax.axis_size("ey")
    cores = lax.axis_size("ec")
    head_parts = head_parts.reshape(chips, cores, tok_rows, model_width)
    head_parts = lax.all_to_all(head_parts, "ec", split_axis=1, concat_axis=1, tiled=True)
    head_parts = jnp.sum(head_parts.astype(jnp.float32), axis=1).astype(jnp.bfloat16)
    head_parts = exchange(head_parts, ("ey",), 2)
    head_sum = jnp.sum(head_parts.astype(jnp.float32), axis=0)
    residual = hidden_in.astype(jnp.float32) + head_sum
    moe_in = norm_rows(residual, moe_gain)
    route_count = expert_ids.shape[1]
    capacity = 2 * tok_rows * route_count // expert_lanes
    flat_expert = expert_ids.reshape(-1)
    assign_index = jnp.arange(flat_expert.shape[0], dtype=jnp.int32)
    earlier = assign_index[None, :] < assign_index[:, None]
    slot_index = jnp.sum(
        jnp.logical_and(flat_expert[:, None] == flat_expert[None, :], earlier), axis=-1
    )
    token_of = assign_index // route_count
    slot_of = flat_expert * capacity + slot_index
    dest_ids = jnp.arange(expert_lanes * capacity, dtype=jnp.int32)
    token_ids = jnp.arange(tok_rows, dtype=jnp.int32)
    hit = (slot_of[None, :] == dest_ids[:, None])
    source_token = jnp.sum(jnp.where(hit, token_of[None, :], 0), axis=-1)
    has_source = jnp.any(hit, axis=-1)
    select = ((source_token[:, None] == token_ids[None, :]) & has_source[:, None]).astype(jnp.bfloat16)
    outgoing_rows = (
        jnp.dot(select, moe_in, preferred_element_type=jnp.float32)
        .astype(jnp.bfloat16)
        .reshape(expert_lanes, capacity, model_width)
    )
    rows_piece = exchange(outgoing_rows, EXPERT, 0)
    flat_rows = rows_piece.reshape(-1, rows_piece.shape[-1])
    gate_part = jnp.dot(flat_rows, w_gate[0], preferred_element_type=jnp.float32)
    up_part = jnp.dot(flat_rows, w_up[0], preferred_element_type=jnp.float32)
    hidden = (jax.nn.silu(gate_part) * up_part).astype(jnp.bfloat16)
    result = (
        jnp.dot(hidden, w_down[0], preferred_element_type=jnp.float32)
        .astype(jnp.bfloat16)
        .reshape(rows_piece.shape)
    )
    returned = exchange(result, EXPERT, 1)
    picked = returned.reshape(expert_lanes * capacity, model_width)[
        flat_expert * capacity + slot_index
    ]
    weighted = jnp.sum(
        picked.reshape(tok_rows, route_count, model_width).astype(jnp.float32)
        * gate_weights[..., None],
        axis=1,
    )
    return residual + weighted


def solution(mesh):
    lanes = mesh.shape["expert"]
    cores = 2 if lanes % 2 == 0 else 1
    split = jax.sharding.Mesh(
        mesh.devices.reshape(mesh.shape["group"], lanes // cores, cores), ("group",) + EXPERT
    )
    rows = ("group",) + EXPERT
    placed = (
        P(rows, None),
        P(),
        P(),
        P("group", None, None, EXPERT),
        P(),
        P(None, None, EXPERT),
        P(EXPERT, None),
        P(),
        P(EXPERT, None, None),
        P(EXPERT, None, None),
        P(EXPERT, None, None),
        P(rows, None),
        P(rows, None),
    )
    return jax.shard_map(
        shards, mesh=split, in_specs=placed, out_specs=P(rows, None), check_vma=False
    )
```

```python
import functools

import jax
import jax.numpy as jnp
from jax import lax
from jax.experimental import pallas as pl
from jax.experimental.pallas import tpu as pltpu
from jax.sharding import PartitionSpec as P

HEAD_DIM = 128
EXPERT = ("ey", "ec")
MESH_AXES = ("group", "ey", "ec")
MESH_IDS = pl.DeviceIdType.MESH
NBLK = 8
CTX = 2048


def norm_rows(inputs, gain_vector):
    values = inputs.astype(jnp.float32)
    factor = lax.rsqrt(jnp.mean(values * values, axis=-1, keepdims=True) + 1e-05)
    return (values * factor * gain_vector).astype(jnp.bfloat16)


def rotate(vectors, positions):
    half_dim = vectors.shape[-1] // 2
    frequency = 10000.0 ** (-jnp.arange(half_dim).astype(jnp.float32) / half_dim)
    angles = positions[:, None] * frequency[None, :]
    cosine = jnp.cos(angles)[:, None, :]
    sine_part = jnp.sin(angles)[:, None, :]
    first_half = vectors[..., :half_dim]
    second_half = vectors[..., half_dim:]
    return jnp.concatenate(
        [
            first_half * cosine - second_half * sine_part,
            first_half * sine_part + second_half * cosine,
        ],
        axis=-1,
    )


def attend_block(softmax_state, queries, key_block, value_block, key_valid):
    old_peak, old_total, old_mixed = softmax_state
    score_scale = queries.shape[-1] ** (-0.5)
    scores = (
        jnp.einsum("qhd,khd->hqk", queries, key_block, preferred_element_type=jnp.float32)
        * score_scale
    )
    scores = jnp.where(key_valid[None], scores, -1e30)
    new_peak = jnp.maximum(old_peak, jnp.max(scores, axis=-1))
    weights = jnp.exp(scores - new_peak[..., None])
    factor = jnp.exp(old_peak - new_peak)
    new_total = old_total * factor + jnp.sum(weights, axis=-1)
    new_mixed = old_mixed * factor[..., None] + jnp.einsum(
        "hqk,khd->hqd",
        weights.astype(jnp.bfloat16),
        value_block,
        preferred_element_type=jnp.float32,
    )
    return (new_peak, new_total, new_mixed)


def cache_pass(
    softmax_state,
    queries,
    all_keys,
    all_values,
    length,
    turn_count,
    array_step,
    array_first,
    position_step,
    position_first,
    block_len,
):

    def step_once(turn_index, running):
        array_start = (array_first + array_step * turn_index) * block_len
        position_start = (position_first + position_step * turn_index) * block_len
        key_block = lax.dynamic_slice_in_dim(all_keys, array_start, block_len, 0)
        value_block = lax.dynamic_slice_in_dim(all_values, array_start, block_len, 0)
        key_valid = (position_start + jnp.arange(block_len, dtype=jnp.int32) < length)[None, :]
        return attend_block(running, queries, key_block, value_block, key_valid)

    return lax.fori_loop(0, turn_count, step_once, softmax_state)


def exchange_kernel(axes, split, x_ref, o_ref, send_sems, recv_sems, own_sem):
    sizes = [lax.axis_size(a) for a in axes]
    count = 1
    for size in sizes:
        count *= size
    me = 0
    for a, size in zip(axes, sizes):
        me = me * size + lax.axis_index(a)

    def device_of(peer):
        coords = {}
        rest = peer
        for a, size in reversed(list(zip(axes, sizes))):
            coords[a] = rest % size
            rest = rest // size
        return tuple(coords.get(a, lax.axis_index(a)) for a in MESH_AXES)

    barrier = pltpu.get_barrier_semaphore()
    for k in range(1, count):
        pl.semaphore_signal(
            barrier, inc=1, device_id=device_of((me + k) % count), device_id_type=MESH_IDS
        )
    pl.semaphore_wait(barrier, count - 1)
    def block(ref, index):
        return ref.at[index] if split == 0 else ref.at[:, index]

    own = pltpu.make_async_copy(block(x_ref, me), block(o_ref, me), own_sem)
    own.start()
    copies = []
    for k in range(1, count):
        peer = (me + k) % count
        copy = pltpu.make_async_remote_copy(
            src_ref=block(x_ref, peer),
            dst_ref=block(o_ref, me),
            send_sem=send_sems.at[k],
            recv_sem=recv_sems.at[k],
            device_id=device_of(peer),
            device_id_type=MESH_IDS,
        )
        copy.start()
        copies.append(copy)
    own.wait()
    for copy in copies:
        copy.wait()


def exchange(x, axes, ident, split=0):
    count = x.shape[split]
    return pl.pallas_call(
        functools.partial(exchange_kernel, axes, split),
        out_shape=jax.ShapeDtypeStruct(x.shape, x.dtype),
        in_specs=[pl.BlockSpec(memory_space=pl.ANY)],
        out_specs=pl.BlockSpec(memory_space=pl.ANY),
        scratch_shapes=[
            pltpu.SemaphoreType.DMA((count,)),
            pltpu.SemaphoreType.DMA((count,)),
            pltpu.SemaphoreType.DMA(()),
        ],
        compiler_params=pltpu.CompilerParams(collective_id=ident, has_side_effects=True),
    )(x)


def attention_kernel(
    slots_ref, len_ref, q_ref, nk_ref, nv_ref, arr_ref, o_ref, kbuf, vbuf, m_sc, l_sc, acc_sc
):
    head = pl.program_id(0)
    rows, width = q_ref.shape
    page = arr_ref.shape[2]
    block_len = kbuf.shape[0]
    pages_per_block = block_len // page
    score_scale = width ** (-0.5)
    lanes = pl.ds(pl.multiple_of(head * width, width), width)
    q = q_ref[...]
    dims = (((1,), (1,)), ((), ()))
    scores = lax.dot_general(q, nk_ref[...], dims, preferred_element_type=jnp.float32) * score_scale
    row_i = lax.broadcasted_iota(jnp.int32, (rows, rows), 0)
    col_i = lax.broadcasted_iota(jnp.int32, (rows, rows), 1)
    scores = jnp.where(col_i <= row_i, scores, -1e30)
    peak = jnp.max(scores, axis=-1, keepdims=True)
    weights = jnp.exp(scores - peak)
    m_sc[...] = peak
    l_sc[...] = jnp.sum(weights, axis=-1, keepdims=True)
    acc_sc[...] = jnp.dot(weights.astype(jnp.bfloat16), nv_ref[...], preferred_element_type=jnp.float32)
    length = len_ref[0]
    block_count = (length + block_len - 1) // block_len

    def one_block(b, carry):
        for i in range(pages_per_block):
            slot = slots_ref[b * pages_per_block + i]
            kbuf[pl.ds(i * page, page), :] = arr_ref[slot, 0, :, lanes]
            vbuf[pl.ds(i * page, page), :] = arr_ref[slot, 1, :, lanes]
        block_scores = (
            lax.dot_general(q, kbuf[...], dims, preferred_element_type=jnp.float32) * score_scale
        )
        position = b * block_len + lax.broadcasted_iota(jnp.int32, (rows, block_len), 1)
        block_scores = jnp.where(position < length, block_scores, -1e30)
        old_peak = m_sc[...]
        new_peak = jnp.maximum(old_peak, jnp.max(block_scores, axis=-1, keepdims=True))
        block_weights = jnp.exp(block_scores - new_peak)
        factor = jnp.exp(old_peak - new_peak)
        l_sc[...] = l_sc[...] * factor + jnp.sum(block_weights, axis=-1, keepdims=True)
        acc_sc[...] = acc_sc[...] * factor + jnp.dot(
            block_weights.astype(jnp.bfloat16), vbuf[...], preferred_element_type=jnp.float32
        )
        m_sc[...] = new_peak
        return carry

    lax.fori_loop(0, block_count, one_block, 0)
    o_ref[...] = (acc_sc[...] / l_sc[...]).astype(o_ref.dtype)


def paged_attention(slots, length, queries, new_keys, new_values, arrived, block_len):
    rows, local_width = queries.shape
    heads = local_width // HEAD_DIM
    slot_count, _, page, _ = arrived.shape
    column = lambda h, *_: (0, h)
    spec = pl.BlockSpec((rows, HEAD_DIM), column)
    cost = pl.CostEstimate(
        flops=4 * rows * (rows + CTX) * local_width,
        transcendentals=rows * (rows + CTX) * heads,
        bytes_accessed=arrived.size * 2 + 4 * rows * local_width * 2,
    )
    return pl.pallas_call(
        attention_kernel,
        out_shape=jax.ShapeDtypeStruct((rows, local_width), jnp.bfloat16),
        grid_spec=pltpu.PrefetchScalarGridSpec(
            num_scalar_prefetch=2,
            grid=(heads,),
            in_specs=[
                spec,
                spec,
                spec,
                pl.BlockSpec(arrived.shape, lambda h, *_: (0, 0, 0, 0)),
            ],
            out_specs=spec,
            scratch_shapes=[
                pltpu.VMEM((block_len, HEAD_DIM), jnp.bfloat16),
                pltpu.VMEM((block_len, HEAD_DIM), jnp.bfloat16),
                pltpu.VMEM((rows, 1), jnp.float32),
                pltpu.VMEM((rows, 1), jnp.float32),
                pltpu.VMEM((rows, HEAD_DIM), jnp.float32),
            ],
        ),
        compiler_params=pltpu.CompilerParams(vmem_limit_bytes=48 * 1024 * 1024),
        cost_estimate=cost,
    )(slots, length, queries, new_keys, new_values, arrived)


def shards(
    hidden_in,
    cache_len,
    page_table,
    pool,
    attn_gain,
    w_qkv,
    w_out,
    moe_gain,
    w_gate,
    w_up,
    w_down,
    expert_ids,
    gate_weights,
):
    groups = lax.axis_size("group")
    expert_lanes = lax.axis_size(EXPERT)
    group_index = lax.axis_index("group")
    tok_rows = hidden_in.shape[0]
    model_width = hidden_in.shape[1]
    local_width = w_out.shape[0]
    head_size = HEAD_DIM
    local_heads = local_width // head_size
    new_count = tok_rows * expert_lanes
    block_len = CTX // NBLK
    length = cache_len[group_index]
    normed = norm_rows(hidden_in, attn_gain)
    projection = w_qkv.reshape(model_width, 3 * local_width)
    projected = jnp.dot(
        lax.all_gather(normed, EXPERT, axis=0, tiled=True),
        projection,
        preferred_element_type=jnp.float32,
    )
    projected = projected.reshape(new_count, 3, local_heads, head_size)
    positions = (length + jnp.arange(new_count, dtype=jnp.int32)).astype(jnp.float32)
    queries = rotate(projected[:, 0], positions).astype(jnp.bfloat16)
    new_keys = rotate(projected[:, 1], positions).astype(jnp.bfloat16)
    new_values = projected[:, 2].astype(jnp.bfloat16)
    pages_per = page_table.shape[1]
    page_most = max(1, pages_per // min(groups, 16))
    owner_group = page_table // pages_per
    local_slot = page_table % pages_per
    page_order = jnp.arange(pages_per, dtype=jnp.int32)
    mine = (owner_group == group_index).astype(jnp.int32)
    mine_rank = jnp.cumsum(mine, axis=1) - mine
    slot_ids = jnp.arange(page_most, dtype=jnp.int32)
    pick = (mine[:, None, :] > 0) & (mine_rank[:, None, :] == slot_ids[None, :, None])
    send_index = jnp.sum(jnp.where(pick, local_slot[:, None, :], 0), axis=-1)
    outgoing = pool[send_index]
    arrived = lax.all_to_all(outgoing, "group", split_axis=0, concat_axis=0, tiled=True)
    arrived = arrived.reshape((groups * page_most,) + pool.shape[1:])
    my_owner = owner_group[group_index]
    before = page_order[None, :] < page_order[:, None]
    my_rank = jnp.sum(jnp.logical_and(my_owner[:, None] == my_owner[None, :], before), axis=-1)
    slots = (my_owner * page_most + my_rank).astype(jnp.int32)
    attended = paged_attention(
        slots,
        jnp.reshape(length, (1,)).astype(jnp.int32),
        queries.reshape(new_count, local_width),
        new_keys.reshape(new_count, local_width),
        new_values.reshape(new_count, local_width),
        arrived,
        block_len,
    )
    head_weights = lax.all_gather(w_out, EXPERT, axis=0, tiled=True)
    head_weights = head_weights.reshape(expert_lanes, local_width, model_width)
    rows_piece = lax.all_to_all(
        attended.reshape(expert_lanes, tok_rows, local_width), EXPERT, 0, 0, tiled=True
    )
    head_parts = jnp.einsum(
        "gtc,gcd->gtd", rows_piece, head_weights, preferred_element_type=jnp.float32
    ).astype(jnp.bfloat16)
    head_sum = jnp.sum(head_parts.astype(jnp.float32), axis=0)
    residual = hidden_in.astype(jnp.float32) + head_sum
    moe_in = norm_rows(residual, moe_gain)
    route_count = expert_ids.shape[1]
    capacity = 2 * tok_rows * route_count // expert_lanes
    flat_expert = expert_ids.reshape(-1)
    assign_index = jnp.arange(flat_expert.shape[0], dtype=jnp.int32)
    earlier = assign_index[None, :] < assign_index[:, None]
    slot_index = jnp.sum(
        jnp.logical_and(flat_expert[:, None] == flat_expert[None, :], earlier), axis=-1
    )
    token_of = assign_index // route_count
    slot_of = flat_expert * capacity + slot_index
    dest_ids = jnp.arange(expert_lanes * capacity, dtype=jnp.int32)
    token_ids = jnp.arange(tok_rows, dtype=jnp.int32)
    hit = (slot_of[None, :] == dest_ids[:, None])
    source_token = jnp.sum(jnp.where(hit, token_of[None, :], 0), axis=-1)
    has_source = jnp.any(hit, axis=-1)
    select = ((source_token[:, None] == token_ids[None, :]) & has_source[:, None]).astype(jnp.bfloat16)
    outgoing_rows = (
        jnp.dot(select, moe_in, preferred_element_type=jnp.float32)
        .astype(jnp.bfloat16)
        .reshape(expert_lanes, capacity, model_width)
    )
    rows_piece = exchange(outgoing_rows, EXPERT, 0)
    flat_rows = rows_piece.reshape(-1, rows_piece.shape[-1])
    gate_part = jnp.dot(flat_rows, w_gate[0], preferred_element_type=jnp.float32)
    up_part = jnp.dot(flat_rows, w_up[0], preferred_element_type=jnp.float32)
    hidden = (jax.nn.silu(gate_part) * up_part).astype(jnp.bfloat16)
    result = (
        jnp.dot(hidden, w_down[0], preferred_element_type=jnp.float32)
        .astype(jnp.bfloat16)
        .reshape(rows_piece.shape)
    )
    returned = exchange(result, EXPERT, 1)
    picked = returned.reshape(expert_lanes * capacity, model_width)[
        flat_expert * capacity + slot_index
    ]
    weighted = jnp.sum(
        picked.reshape(tok_rows, route_count, model_width).astype(jnp.float32)
        * gate_weights[..., None],
        axis=1,
    )
    return residual + weighted


def solution(mesh):
    lanes = mesh.shape["expert"]
    cores = 2 if lanes % 2 == 0 else 1
    split = jax.sharding.Mesh(
        mesh.devices.reshape(mesh.shape["group"], lanes // cores, cores), ("group",) + EXPERT
    )
    rows = ("group",) + EXPERT
    placed = (
        P(rows, None),
        P(),
        P(),
        P("group", None, None, EXPERT),
        P(),
        P(None, None, EXPERT),
        P(EXPERT, None),
        P(),
        P(EXPERT, None, None),
        P(EXPERT, None, None),
        P(EXPERT, None, None),
        P(rows, None),
        P(rows, None),
    )
    return jax.shard_map(
        shards, mesh=split, in_specs=placed, out_specs=P(rows, None), check_vma=False
    )
```

```python
import functools

import jax
import jax.numpy as jnp
from jax import lax
from jax.experimental import pallas as pl
from jax.experimental.pallas import tpu as pltpu
from jax.sharding import PartitionSpec as P

HEAD_DIM = 128
EXPERT = ("ey", "ec")
MESH_AXES = ("group", "ey", "ec")
MESH_IDS = pl.DeviceIdType.MESH
NBLK = 8
CTX = 2048


def norm_rows(inputs, gain_vector):
    values = inputs.astype(jnp.float32)
    factor = lax.rsqrt(jnp.mean(values * values, axis=-1, keepdims=True) + 1e-05)
    return (values * factor * gain_vector).astype(jnp.bfloat16)


def rotate(vectors, positions):
    half_dim = vectors.shape[-1] // 2
    frequency = 10000.0 ** (-jnp.arange(half_dim).astype(jnp.float32) / half_dim)
    angles = positions[:, None] * frequency[None, :]
    cosine = jnp.cos(angles)[:, None, :]
    sine_part = jnp.sin(angles)[:, None, :]
    first_half = vectors[..., :half_dim]
    second_half = vectors[..., half_dim:]
    return jnp.concatenate(
        [
            first_half * cosine - second_half * sine_part,
            first_half * sine_part + second_half * cosine,
        ],
        axis=-1,
    )


def attend_block(softmax_state, queries, key_block, value_block, key_valid):
    old_peak, old_total, old_mixed = softmax_state
    score_scale = queries.shape[-1] ** (-0.5)
    scores = (
        jnp.einsum("qhd,khd->hqk", queries, key_block, preferred_element_type=jnp.float32)
        * score_scale
    )
    scores = jnp.where(key_valid[None], scores, -1e30)
    new_peak = jnp.maximum(old_peak, jnp.max(scores, axis=-1))
    weights = jnp.exp(scores - new_peak[..., None])
    factor = jnp.exp(old_peak - new_peak)
    new_total = old_total * factor + jnp.sum(weights, axis=-1)
    new_mixed = old_mixed * factor[..., None] + jnp.einsum(
        "hqk,khd->hqd",
        weights.astype(jnp.bfloat16),
        value_block,
        preferred_element_type=jnp.float32,
    )
    return (new_peak, new_total, new_mixed)


def cache_pass(
    softmax_state,
    queries,
    all_keys,
    all_values,
    length,
    turn_count,
    array_step,
    array_first,
    position_step,
    position_first,
    block_len,
):

    def step_once(turn_index, running):
        array_start = (array_first + array_step * turn_index) * block_len
        position_start = (position_first + position_step * turn_index) * block_len
        key_block = lax.dynamic_slice_in_dim(all_keys, array_start, block_len, 0)
        value_block = lax.dynamic_slice_in_dim(all_values, array_start, block_len, 0)
        key_valid = (position_start + jnp.arange(block_len, dtype=jnp.int32) < length)[None, :]
        return attend_block(running, queries, key_block, value_block, key_valid)

    return lax.fori_loop(0, turn_count, step_once, softmax_state)


def exchange_kernel(axes, split, x_ref, o_ref, send_sems, recv_sems, own_sem):
    sizes = [lax.axis_size(a) for a in axes]
    count = 1
    for size in sizes:
        count *= size
    me = 0
    for a, size in zip(axes, sizes):
        me = me * size + lax.axis_index(a)

    def device_of(peer):
        coords = {}
        rest = peer
        for a, size in reversed(list(zip(axes, sizes))):
            coords[a] = rest % size
            rest = rest // size
        return tuple(coords.get(a, lax.axis_index(a)) for a in MESH_AXES)

    barrier = pltpu.get_barrier_semaphore()
    for k in range(1, count):
        pl.semaphore_signal(
            barrier, inc=1, device_id=device_of((me + k) % count), device_id_type=MESH_IDS
        )
    pl.semaphore_wait(barrier, count - 1)
    def block(ref, index):
        return ref.at[index] if split == 0 else ref.at[:, index]

    own = pltpu.make_async_copy(block(x_ref, me), block(o_ref, me), own_sem)
    own.start()
    copies = []
    for k in range(1, count):
        peer = (me + k) % count
        copy = pltpu.make_async_remote_copy(
            src_ref=block(x_ref, peer),
            dst_ref=block(o_ref, me),
            send_sem=send_sems.at[k],
            recv_sem=recv_sems.at[k],
            device_id=device_of(peer),
            device_id_type=MESH_IDS,
        )
        copy.start()
        copies.append(copy)
    own.wait()
    for copy in copies:
        copy.wait()


def exchange(x, axes, ident, split=0):
    count = x.shape[split]
    return pl.pallas_call(
        functools.partial(exchange_kernel, axes, split),
        out_shape=jax.ShapeDtypeStruct(x.shape, x.dtype),
        in_specs=[pl.BlockSpec(memory_space=pl.ANY)],
        out_specs=pl.BlockSpec(memory_space=pl.ANY),
        scratch_shapes=[
            pltpu.SemaphoreType.DMA((count,)),
            pltpu.SemaphoreType.DMA((count,)),
            pltpu.SemaphoreType.DMA(()),
        ],
        compiler_params=pltpu.CompilerParams(collective_id=ident, has_side_effects=True),
    )(x)


def attention_kernel(
    slots_ref, len_ref, q_ref, nk_ref, nv_ref, arr_ref, o_ref, kbuf, vbuf, m_sc, l_sc, acc_sc
):
    head = pl.program_id(0)
    rows, width = q_ref.shape
    page = arr_ref.shape[2]
    block_len = kbuf.shape[0]
    pages_per_block = block_len // page
    score_scale = width ** (-0.5)
    lanes = pl.ds(pl.multiple_of(head * width, width), width)
    q = q_ref[...]
    dims = (((1,), (1,)), ((), ()))
    scores = lax.dot_general(q, nk_ref[...], dims, preferred_element_type=jnp.float32) * score_scale
    row_i = lax.broadcasted_iota(jnp.int32, (rows, rows), 0)
    col_i = lax.broadcasted_iota(jnp.int32, (rows, rows), 1)
    scores = jnp.where(col_i <= row_i, scores, -1e30)
    peak = jnp.max(scores, axis=-1, keepdims=True)
    weights = jnp.exp(scores - peak)
    m_sc[...] = peak
    l_sc[...] = jnp.sum(weights, axis=-1, keepdims=True)
    acc_sc[...] = jnp.dot(weights.astype(jnp.bfloat16), nv_ref[...], preferred_element_type=jnp.float32)
    length = len_ref[0]
    block_count = (length + block_len - 1) // block_len

    def one_block(b, carry):
        for i in range(pages_per_block):
            slot = slots_ref[b * pages_per_block + i]
            kbuf[pl.ds(i * page, page), :] = arr_ref[slot, 0, :, lanes]
            vbuf[pl.ds(i * page, page), :] = arr_ref[slot, 1, :, lanes]
        block_scores = (
            lax.dot_general(q, kbuf[...], dims, preferred_element_type=jnp.float32) * score_scale
        )
        position = b * block_len + lax.broadcasted_iota(jnp.int32, (rows, block_len), 1)
        block_scores = jnp.where(position < length, block_scores, -1e30)
        old_peak = m_sc[...]
        new_peak = jnp.maximum(old_peak, jnp.max(block_scores, axis=-1, keepdims=True))
        block_weights = jnp.exp(block_scores - new_peak)
        factor = jnp.exp(old_peak - new_peak)
        l_sc[...] = l_sc[...] * factor + jnp.sum(block_weights, axis=-1, keepdims=True)
        acc_sc[...] = acc_sc[...] * factor + jnp.dot(
            block_weights.astype(jnp.bfloat16), vbuf[...], preferred_element_type=jnp.float32
        )
        m_sc[...] = new_peak
        return carry

    lax.fori_loop(0, block_count, one_block, 0)
    o_ref[...] = (acc_sc[...] / l_sc[...]).astype(o_ref.dtype)


def paged_attention(slots, length, queries, new_keys, new_values, arrived, block_len):
    rows, local_width = queries.shape
    heads = local_width // HEAD_DIM
    slot_count, _, page, _ = arrived.shape
    column = lambda h, *_: (0, h)
    spec = pl.BlockSpec((rows, HEAD_DIM), column)
    cost = pl.CostEstimate(
        flops=4 * rows * (rows + CTX) * local_width,
        transcendentals=rows * (rows + CTX) * heads,
        bytes_accessed=arrived.size * 2 + 4 * rows * local_width * 2,
    )
    return pl.pallas_call(
        attention_kernel,
        out_shape=jax.ShapeDtypeStruct((rows, local_width), jnp.bfloat16),
        grid_spec=pltpu.PrefetchScalarGridSpec(
            num_scalar_prefetch=2,
            grid=(heads,),
            in_specs=[
                spec,
                spec,
                spec,
                pl.BlockSpec(arrived.shape, lambda h, *_: (0, 0, 0, 0)),
            ],
            out_specs=spec,
            scratch_shapes=[
                pltpu.VMEM((block_len, HEAD_DIM), jnp.bfloat16),
                pltpu.VMEM((block_len, HEAD_DIM), jnp.bfloat16),
                pltpu.VMEM((rows, 1), jnp.float32),
                pltpu.VMEM((rows, 1), jnp.float32),
                pltpu.VMEM((rows, HEAD_DIM), jnp.float32),
            ],
        ),
        compiler_params=pltpu.CompilerParams(vmem_limit_bytes=48 * 1024 * 1024),
        cost_estimate=cost,
    )(slots, length, queries, new_keys, new_values, arrived)


def shards(
    hidden_in,
    cache_len,
    page_table,
    pool,
    attn_gain,
    w_qkv,
    w_out,
    moe_gain,
    w_gate,
    w_up,
    w_down,
    expert_ids,
    gate_weights,
):
    groups = lax.axis_size("group")
    expert_lanes = lax.axis_size(EXPERT)
    group_index = lax.axis_index("group")
    tok_rows = hidden_in.shape[0]
    model_width = hidden_in.shape[1]
    local_width = w_out.shape[0]
    head_size = HEAD_DIM
    local_heads = local_width // head_size
    new_count = tok_rows * expert_lanes
    block_len = CTX // NBLK
    length = cache_len[group_index]
    normed = norm_rows(hidden_in, attn_gain)
    projection = w_qkv.reshape(model_width, 3 * local_width)
    projected = jnp.dot(
        lax.all_gather(normed, EXPERT, axis=0, tiled=True),
        projection,
        preferred_element_type=jnp.float32,
    )
    projected = projected.reshape(new_count, 3, local_heads, head_size)
    positions = (length + jnp.arange(new_count, dtype=jnp.int32)).astype(jnp.float32)
    queries = rotate(projected[:, 0], positions).astype(jnp.bfloat16)
    new_keys = rotate(projected[:, 1], positions).astype(jnp.bfloat16)
    new_values = projected[:, 2].astype(jnp.bfloat16)
    pages_per = page_table.shape[1]
    page_most = max(1, pages_per // min(groups, 16))
    owner_group = page_table // pages_per
    local_slot = page_table % pages_per
    page_order = jnp.arange(pages_per, dtype=jnp.int32)
    mine = (owner_group == group_index).astype(jnp.int32)
    mine_rank = jnp.cumsum(mine, axis=1) - mine
    slot_ids = jnp.arange(page_most, dtype=jnp.int32)
    pick = (mine[:, None, :] > 0) & (mine_rank[:, None, :] == slot_ids[None, :, None])
    send_index = jnp.sum(jnp.where(pick, local_slot[:, None, :], 0), axis=-1)
    outgoing = pool[send_index]
    arrived = lax.all_to_all(outgoing, "group", split_axis=0, concat_axis=0, tiled=True)
    arrived = arrived.reshape((groups * page_most,) + pool.shape[1:])
    my_owner = owner_group[group_index]
    before = page_order[None, :] < page_order[:, None]
    my_rank = jnp.sum(jnp.logical_and(my_owner[:, None] == my_owner[None, :], before), axis=-1)
    slots = (my_owner * page_most + my_rank).astype(jnp.int32)
    attended = paged_attention(
        slots,
        jnp.reshape(length, (1,)).astype(jnp.int32),
        queries.reshape(new_count, local_width),
        new_keys.reshape(new_count, local_width),
        new_values.reshape(new_count, local_width),
        arrived,
        block_len,
    )
    head_weights = lax.all_gather(w_out, EXPERT, axis=0, tiled=True)
    head_weights = head_weights.reshape(expert_lanes, local_width, model_width)
    rows_piece = exchange(attended.reshape(expert_lanes, tok_rows, local_width), EXPERT, 2)
    head_parts = jnp.einsum(
        "gtc,gcd->gtd", rows_piece, head_weights, preferred_element_type=jnp.float32
    ).astype(jnp.bfloat16)
    head_sum = jnp.sum(head_parts.astype(jnp.float32), axis=0)
    residual = hidden_in.astype(jnp.float32) + head_sum
    moe_in = norm_rows(residual, moe_gain)
    route_count = expert_ids.shape[1]
    capacity = 2 * tok_rows * route_count // expert_lanes
    flat_expert = expert_ids.reshape(-1)
    assign_index = jnp.arange(flat_expert.shape[0], dtype=jnp.int32)
    earlier = assign_index[None, :] < assign_index[:, None]
    slot_index = jnp.sum(
        jnp.logical_and(flat_expert[:, None] == flat_expert[None, :], earlier), axis=-1
    )
    token_of = assign_index // route_count
    slot_of = flat_expert * capacity + slot_index
    dest_ids = jnp.arange(expert_lanes * capacity, dtype=jnp.int32)
    token_ids = jnp.arange(tok_rows, dtype=jnp.int32)
    hit = (slot_of[None, :] == dest_ids[:, None])
    source_token = jnp.sum(jnp.where(hit, token_of[None, :], 0), axis=-1)
    has_source = jnp.any(hit, axis=-1)
    select = ((source_token[:, None] == token_ids[None, :]) & has_source[:, None]).astype(jnp.bfloat16)
    outgoing_rows = (
        jnp.dot(select, moe_in, preferred_element_type=jnp.float32)
        .astype(jnp.bfloat16)
        .reshape(expert_lanes, capacity, model_width)
    )
    rows_piece = exchange(outgoing_rows, EXPERT, 0)
    flat_rows = rows_piece.reshape(-1, rows_piece.shape[-1])
    gate_part = jnp.dot(flat_rows, w_gate[0], preferred_element_type=jnp.float32)
    up_part = jnp.dot(flat_rows, w_up[0], preferred_element_type=jnp.float32)
    hidden = (jax.nn.silu(gate_part) * up_part).astype(jnp.bfloat16)
    result = (
        jnp.dot(hidden, w_down[0], preferred_element_type=jnp.float32)
        .astype(jnp.bfloat16)
        .reshape(rows_piece.shape)
    )
    returned = exchange(result, EXPERT, 1)
    picked = returned.reshape(expert_lanes * capacity, model_width)[
        flat_expert * capacity + slot_index
    ]
    weighted = jnp.sum(
        picked.reshape(tok_rows, route_count, model_width).astype(jnp.float32)
        * gate_weights[..., None],
        axis=1,
    )
    return residual + weighted


def solution(mesh):
    lanes = mesh.shape["expert"]
    cores = 2 if lanes % 2 == 0 else 1
    split = jax.sharding.Mesh(
        mesh.devices.reshape(mesh.shape["group"], lanes // cores, cores), ("group",) + EXPERT
    )
    rows = ("group",) + EXPERT
    placed = (
        P(rows, None),
        P(),
        P(),
        P("group", None, None, EXPERT),
        P(),
        P(None, None, EXPERT),
        P(EXPERT, None),
        P(),
        P(EXPERT, None, None),
        P(EXPERT, None, None),
        P(EXPERT, None, None),
        P(rows, None),
        P(rows, None),
    )
    return jax.shard_map(
        shards, mesh=split, in_specs=placed, out_specs=P(rows, None), check_vma=False
    )
```

```python
import functools

import jax
import jax.numpy as jnp
from jax import lax
from jax.experimental import pallas as pl
from jax.experimental.pallas import tpu as pltpu
from jax.sharding import PartitionSpec as P

HEAD_DIM = 128
EXPERT = ("ey", "ec")
MESH_AXES = ("group", "ey", "ec")
MESH_IDS = pl.DeviceIdType.MESH
NBLK = 4
CTX = 2048


def norm_rows(inputs, gain_vector):
    values = inputs.astype(jnp.float32)
    factor = lax.rsqrt(jnp.mean(values * values, axis=-1, keepdims=True) + 1e-05)
    return (values * factor * gain_vector).astype(jnp.bfloat16)


def rotate(vectors, positions):
    half_dim = vectors.shape[-1] // 2
    frequency = 10000.0 ** (-jnp.arange(half_dim).astype(jnp.float32) / half_dim)
    angles = positions[:, None] * frequency[None, :]
    cosine = jnp.cos(angles)[:, None, :]
    sine_part = jnp.sin(angles)[:, None, :]
    first_half = vectors[..., :half_dim]
    second_half = vectors[..., half_dim:]
    return jnp.concatenate(
        [
            first_half * cosine - second_half * sine_part,
            first_half * sine_part + second_half * cosine,
        ],
        axis=-1,
    )


def attend_block(softmax_state, queries, key_block, value_block, key_valid):
    old_peak, old_total, old_mixed = softmax_state
    score_scale = queries.shape[-1] ** (-0.5)
    scores = (
        jnp.einsum("qhd,khd->hqk", queries, key_block, preferred_element_type=jnp.float32)
        * score_scale
    )
    scores = jnp.where(key_valid[None], scores, -1e30)
    new_peak = jnp.maximum(old_peak, jnp.max(scores, axis=-1))
    weights = jnp.exp(scores - new_peak[..., None])
    factor = jnp.exp(old_peak - new_peak)
    new_total = old_total * factor + jnp.sum(weights, axis=-1)
    new_mixed = old_mixed * factor[..., None] + jnp.einsum(
        "hqk,khd->hqd",
        weights.astype(jnp.bfloat16),
        value_block,
        preferred_element_type=jnp.float32,
    )
    return (new_peak, new_total, new_mixed)


def cache_pass(
    softmax_state,
    queries,
    all_keys,
    all_values,
    length,
    turn_count,
    array_step,
    array_first,
    position_step,
    position_first,
    block_len,
):

    def step_once(turn_index, running):
        array_start = (array_first + array_step * turn_index) * block_len
        position_start = (position_first + position_step * turn_index) * block_len
        key_block = lax.dynamic_slice_in_dim(all_keys, array_start, block_len, 0)
        value_block = lax.dynamic_slice_in_dim(all_values, array_start, block_len, 0)
        key_valid = (position_start + jnp.arange(block_len, dtype=jnp.int32) < length)[None, :]
        return attend_block(running, queries, key_block, value_block, key_valid)

    return lax.fori_loop(0, turn_count, step_once, softmax_state)


def exchange_kernel(axes, split, x_ref, o_ref, send_sems, recv_sems, own_sem):
    sizes = [lax.axis_size(a) for a in axes]
    count = 1
    for size in sizes:
        count *= size
    me = 0
    for a, size in zip(axes, sizes):
        me = me * size + lax.axis_index(a)

    def device_of(peer):
        coords = {}
        rest = peer
        for a, size in reversed(list(zip(axes, sizes))):
            coords[a] = rest % size
            rest = rest // size
        return tuple(coords.get(a, lax.axis_index(a)) for a in MESH_AXES)

    barrier = pltpu.get_barrier_semaphore()
    for k in range(1, count):
        pl.semaphore_signal(
            barrier, inc=1, device_id=device_of((me + k) % count), device_id_type=MESH_IDS
        )
    pl.semaphore_wait(barrier, count - 1)
    def block(ref, index):
        return ref.at[index] if split == 0 else ref.at[:, index]

    own = pltpu.make_async_copy(block(x_ref, me), block(o_ref, me), own_sem)
    own.start()
    copies = []
    for k in range(1, count):
        peer = (me + k) % count
        copy = pltpu.make_async_remote_copy(
            src_ref=block(x_ref, peer),
            dst_ref=block(o_ref, me),
            send_sem=send_sems.at[k],
            recv_sem=recv_sems.at[k],
            device_id=device_of(peer),
            device_id_type=MESH_IDS,
        )
        copy.start()
        copies.append(copy)
    own.wait()
    for copy in copies:
        copy.wait()


def exchange(x, axes, ident, split=0):
    count = x.shape[split]
    return pl.pallas_call(
        functools.partial(exchange_kernel, axes, split),
        out_shape=jax.ShapeDtypeStruct(x.shape, x.dtype),
        in_specs=[pl.BlockSpec(memory_space=pl.ANY)],
        out_specs=pl.BlockSpec(memory_space=pl.ANY),
        scratch_shapes=[
            pltpu.SemaphoreType.DMA((count,)),
            pltpu.SemaphoreType.DMA((count,)),
            pltpu.SemaphoreType.DMA(()),
        ],
        compiler_params=pltpu.CompilerParams(collective_id=ident, has_side_effects=True),
    )(x)


def attention_kernel(
    slots_ref, len_ref, q_ref, nk_ref, nv_ref, arr_ref, o_ref, kbuf, vbuf, m_sc, l_sc, acc_sc
):
    head = pl.program_id(0)
    rows, width = q_ref.shape
    page = arr_ref.shape[2]
    block_len = kbuf.shape[0]
    pages_per_block = block_len // page
    score_scale = width ** (-0.5)
    lanes = pl.ds(pl.multiple_of(head * width, width), width)
    q = q_ref[...]
    dims = (((1,), (1,)), ((), ()))
    scores = lax.dot_general(q, nk_ref[...], dims, preferred_element_type=jnp.float32) * score_scale
    row_i = lax.broadcasted_iota(jnp.int32, (rows, rows), 0)
    col_i = lax.broadcasted_iota(jnp.int32, (rows, rows), 1)
    scores = jnp.where(col_i <= row_i, scores, -1e30)
    peak = jnp.max(scores, axis=-1, keepdims=True)
    weights = jnp.exp(scores - peak)
    m_sc[...] = peak
    l_sc[...] = jnp.sum(weights, axis=-1, keepdims=True)
    acc_sc[...] = jnp.dot(weights.astype(jnp.bfloat16), nv_ref[...], preferred_element_type=jnp.float32)
    length = len_ref[0]
    block_count = (length + block_len - 1) // block_len

    def one_block(b, carry):
        for i in range(pages_per_block):
            slot = slots_ref[b * pages_per_block + i]
            kbuf[pl.ds(i * page, page), :] = arr_ref[slot, 0, :, lanes]
            vbuf[pl.ds(i * page, page), :] = arr_ref[slot, 1, :, lanes]
        block_scores = (
            lax.dot_general(q, kbuf[...], dims, preferred_element_type=jnp.float32) * score_scale
        )
        position = b * block_len + lax.broadcasted_iota(jnp.int32, (rows, block_len), 1)
        block_scores = jnp.where(position < length, block_scores, -1e30)
        old_peak = m_sc[...]
        new_peak = jnp.maximum(old_peak, jnp.max(block_scores, axis=-1, keepdims=True))
        block_weights = jnp.exp(block_scores - new_peak)
        factor = jnp.exp(old_peak - new_peak)
        l_sc[...] = l_sc[...] * factor + jnp.sum(block_weights, axis=-1, keepdims=True)
        acc_sc[...] = acc_sc[...] * factor + jnp.dot(
            block_weights.astype(jnp.bfloat16), vbuf[...], preferred_element_type=jnp.float32
        )
        m_sc[...] = new_peak
        return carry

    lax.fori_loop(0, block_count, one_block, 0)
    o_ref[...] = (acc_sc[...] / l_sc[...]).astype(o_ref.dtype)


def paged_attention(slots, length, queries, new_keys, new_values, arrived, block_len):
    rows, local_width = queries.shape
    heads = local_width // HEAD_DIM
    slot_count, _, page, _ = arrived.shape
    column = lambda h, *_: (0, h)
    spec = pl.BlockSpec((rows, HEAD_DIM), column)
    cost = pl.CostEstimate(
        flops=4 * rows * (rows + CTX) * local_width,
        transcendentals=rows * (rows + CTX) * heads,
        bytes_accessed=arrived.size * 2 + 4 * rows * local_width * 2,
    )
    return pl.pallas_call(
        attention_kernel,
        out_shape=jax.ShapeDtypeStruct((rows, local_width), jnp.bfloat16),
        grid_spec=pltpu.PrefetchScalarGridSpec(
            num_scalar_prefetch=2,
            grid=(heads,),
            in_specs=[
                spec,
                spec,
                spec,
                pl.BlockSpec(arrived.shape, lambda h, *_: (0, 0, 0, 0)),
            ],
            out_specs=spec,
            scratch_shapes=[
                pltpu.VMEM((block_len, HEAD_DIM), jnp.bfloat16),
                pltpu.VMEM((block_len, HEAD_DIM), jnp.bfloat16),
                pltpu.VMEM((rows, 1), jnp.float32),
                pltpu.VMEM((rows, 1), jnp.float32),
                pltpu.VMEM((rows, HEAD_DIM), jnp.float32),
            ],
        ),
        compiler_params=pltpu.CompilerParams(vmem_limit_bytes=48 * 1024 * 1024),
        cost_estimate=cost,
    )(slots, length, queries, new_keys, new_values, arrived)


def shards(
    hidden_in,
    cache_len,
    page_table,
    pool,
    attn_gain,
    w_qkv,
    w_out,
    moe_gain,
    w_gate,
    w_up,
    w_down,
    expert_ids,
    gate_weights,
):
    groups = lax.axis_size("group")
    expert_lanes = lax.axis_size(EXPERT)
    group_index = lax.axis_index("group")
    tok_rows = hidden_in.shape[0]
    model_width = hidden_in.shape[1]
    local_width = w_out.shape[0]
    head_size = HEAD_DIM
    local_heads = local_width // head_size
    new_count = tok_rows * expert_lanes
    block_len = CTX // NBLK
    length = cache_len[group_index]
    normed = norm_rows(hidden_in, attn_gain)
    projection = w_qkv.reshape(model_width, 3 * local_width)
    projected = jnp.dot(
        lax.all_gather(normed, EXPERT, axis=0, tiled=True),
        projection,
        preferred_element_type=jnp.float32,
    )
    projected = projected.reshape(new_count, 3, local_heads, head_size)
    positions = (length + jnp.arange(new_count, dtype=jnp.int32)).astype(jnp.float32)
    queries = rotate(projected[:, 0], positions).astype(jnp.bfloat16)
    new_keys = rotate(projected[:, 1], positions).astype(jnp.bfloat16)
    new_values = projected[:, 2].astype(jnp.bfloat16)
    pages_per = page_table.shape[1]
    page_most = max(1, pages_per // min(groups, 16))
    owner_group = page_table // pages_per
    local_slot = page_table % pages_per
    page_order = jnp.arange(pages_per, dtype=jnp.int32)
    mine = (owner_group == group_index).astype(jnp.int32)
    mine_rank = jnp.cumsum(mine, axis=1) - mine
    slot_ids = jnp.arange(page_most, dtype=jnp.int32)
    pick = (mine[:, None, :] > 0) & (mine_rank[:, None, :] == slot_ids[None, :, None])
    send_index = jnp.sum(jnp.where(pick, local_slot[:, None, :], 0), axis=-1)
    outgoing = pool[send_index]
    arrived = lax.all_to_all(outgoing, "group", split_axis=0, concat_axis=0, tiled=True)
    arrived = arrived.reshape((groups * page_most,) + pool.shape[1:])
    my_owner = owner_group[group_index]
    before = page_order[None, :] < page_order[:, None]
    my_rank = jnp.sum(jnp.logical_and(my_owner[:, None] == my_owner[None, :], before), axis=-1)
    slots = (my_owner * page_most + my_rank).astype(jnp.int32)
    attended = paged_attention(
        slots,
        jnp.reshape(length, (1,)).astype(jnp.int32),
        queries.reshape(new_count, local_width),
        new_keys.reshape(new_count, local_width),
        new_values.reshape(new_count, local_width),
        arrived,
        block_len,
    )
    head_weights = lax.all_gather(w_out, EXPERT, axis=0, tiled=True)
    head_weights = head_weights.reshape(expert_lanes, local_width, model_width)
    rows_piece = lax.all_to_all(
        attended.reshape(expert_lanes, tok_rows, local_width), EXPERT, 0, 0, tiled=True
    )
    head_parts = jnp.einsum(
        "gtc,gcd->gtd", rows_piece, head_weights, preferred_element_type=jnp.float32
    ).astype(jnp.bfloat16)
    head_sum = jnp.sum(head_parts.astype(jnp.float32), axis=0)
    residual = hidden_in.astype(jnp.float32) + head_sum
    moe_in = norm_rows(residual, moe_gain)
    route_count = expert_ids.shape[1]
    capacity = 2 * tok_rows * route_count // expert_lanes
    flat_expert = expert_ids.reshape(-1)
    assign_index = jnp.arange(flat_expert.shape[0], dtype=jnp.int32)
    earlier = assign_index[None, :] < assign_index[:, None]
    slot_index = jnp.sum(
        jnp.logical_and(flat_expert[:, None] == flat_expert[None, :], earlier), axis=-1
    )
    token_of = assign_index // route_count
    slot_of = flat_expert * capacity + slot_index
    dest_ids = jnp.arange(expert_lanes * capacity, dtype=jnp.int32)
    token_ids = jnp.arange(tok_rows, dtype=jnp.int32)
    hit = (slot_of[None, :] == dest_ids[:, None])
    source_token = jnp.sum(jnp.where(hit, token_of[None, :], 0), axis=-1)
    has_source = jnp.any(hit, axis=-1)
    select = ((source_token[:, None] == token_ids[None, :]) & has_source[:, None]).astype(jnp.bfloat16)
    outgoing_rows = (
        jnp.dot(select, moe_in, preferred_element_type=jnp.float32)
        .astype(jnp.bfloat16)
        .reshape(expert_lanes, capacity, model_width)
    )
    rows_piece = exchange(outgoing_rows, EXPERT, 0)
    flat_rows = rows_piece.reshape(-1, rows_piece.shape[-1])
    gate_part = jnp.dot(flat_rows, w_gate[0], preferred_element_type=jnp.float32)
    up_part = jnp.dot(flat_rows, w_up[0], preferred_element_type=jnp.float32)
    hidden = (jax.nn.silu(gate_part) * up_part).astype(jnp.bfloat16)
    result = (
        jnp.dot(hidden, w_down[0], preferred_element_type=jnp.float32)
        .astype(jnp.bfloat16)
        .reshape(rows_piece.shape)
    )
    returned = exchange(result, EXPERT, 1)
    picked = returned.reshape(expert_lanes * capacity, model_width)[
        flat_expert * capacity + slot_index
    ]
    weighted = jnp.sum(
        picked.reshape(tok_rows, route_count, model_width).astype(jnp.float32)
        * gate_weights[..., None],
        axis=1,
    )
    return residual + weighted


def solution(mesh):
    lanes = mesh.shape["expert"]
    cores = 2 if lanes % 2 == 0 else 1
    split = jax.sharding.Mesh(
        mesh.devices.reshape(mesh.shape["group"], lanes // cores, cores), ("group",) + EXPERT
    )
    rows = ("group",) + EXPERT
    placed = (
        P(rows, None),
        P(),
        P(),
        P("group", None, None, EXPERT),
        P(),
        P(None, None, EXPERT),
        P(EXPERT, None),
        P(),
        P(EXPERT, None, None),
        P(EXPERT, None, None),
        P(EXPERT, None, None),
        P(rows, None),
        P(rows, None),
    )
    return jax.shard_map(
        shards, mesh=split, in_specs=placed, out_specs=P(rows, None), check_vma=False
    )
```

```python
import functools

import jax
import jax.numpy as jnp
from jax import lax
from jax.experimental import pallas as pl
from jax.experimental.pallas import tpu as pltpu
from jax.sharding import PartitionSpec as P

HEAD_DIM = 128
EXPERT = ("ey", "ec")
MESH_AXES = ("group", "ey", "ec")
MESH_IDS = pl.DeviceIdType.MESH
NBLK = 2
CTX = 2048


def norm_rows(inputs, gain_vector):
    values = inputs.astype(jnp.float32)
    factor = lax.rsqrt(jnp.mean(values * values, axis=-1, keepdims=True) + 1e-05)
    return (values * factor * gain_vector).astype(jnp.bfloat16)


def rotate(vectors, positions):
    half_dim = vectors.shape[-1] // 2
    frequency = 10000.0 ** (-jnp.arange(half_dim).astype(jnp.float32) / half_dim)
    angles = positions[:, None] * frequency[None, :]
    cosine = jnp.cos(angles)[:, None, :]
    sine_part = jnp.sin(angles)[:, None, :]
    first_half = vectors[..., :half_dim]
    second_half = vectors[..., half_dim:]
    return jnp.concatenate(
        [
            first_half * cosine - second_half * sine_part,
            first_half * sine_part + second_half * cosine,
        ],
        axis=-1,
    )


def attend_block(softmax_state, queries, key_block, value_block, key_valid):
    old_peak, old_total, old_mixed = softmax_state
    score_scale = queries.shape[-1] ** (-0.5)
    scores = (
        jnp.einsum("qhd,khd->hqk", queries, key_block, preferred_element_type=jnp.float32)
        * score_scale
    )
    scores = jnp.where(key_valid[None], scores, -1e30)
    new_peak = jnp.maximum(old_peak, jnp.max(scores, axis=-1))
    weights = jnp.exp(scores - new_peak[..., None])
    factor = jnp.exp(old_peak - new_peak)
    new_total = old_total * factor + jnp.sum(weights, axis=-1)
    new_mixed = old_mixed * factor[..., None] + jnp.einsum(
        "hqk,khd->hqd",
        weights.astype(jnp.bfloat16),
        value_block,
        preferred_element_type=jnp.float32,
    )
    return (new_peak, new_total, new_mixed)


def cache_pass(
    softmax_state,
    queries,
    all_keys,
    all_values,
    length,
    turn_count,
    array_step,
    array_first,
    position_step,
    position_first,
    block_len,
):

    def step_once(turn_index, running):
        array_start = (array_first + array_step * turn_index) * block_len
        position_start = (position_first + position_step * turn_index) * block_len
        key_block = lax.dynamic_slice_in_dim(all_keys, array_start, block_len, 0)
        value_block = lax.dynamic_slice_in_dim(all_values, array_start, block_len, 0)
        key_valid = (position_start + jnp.arange(block_len, dtype=jnp.int32) < length)[None, :]
        return attend_block(running, queries, key_block, value_block, key_valid)

    return lax.fori_loop(0, turn_count, step_once, softmax_state)


def exchange_kernel(axes, split, x_ref, o_ref, send_sems, recv_sems, own_sem):
    sizes = [lax.axis_size(a) for a in axes]
    count = 1
    for size in sizes:
        count *= size
    me = 0
    for a, size in zip(axes, sizes):
        me = me * size + lax.axis_index(a)

    def device_of(peer):
        coords = {}
        rest = peer
        for a, size in reversed(list(zip(axes, sizes))):
            coords[a] = rest % size
            rest = rest // size
        return tuple(coords.get(a, lax.axis_index(a)) for a in MESH_AXES)

    barrier = pltpu.get_barrier_semaphore()
    for k in range(1, count):
        pl.semaphore_signal(
            barrier, inc=1, device_id=device_of((me + k) % count), device_id_type=MESH_IDS
        )
    pl.semaphore_wait(barrier, count - 1)
    def block(ref, index):
        return ref.at[index] if split == 0 else ref.at[:, index]

    own = pltpu.make_async_copy(block(x_ref, me), block(o_ref, me), own_sem)
    own.start()
    copies = []
    for k in range(1, count):
        peer = (me + k) % count
        copy = pltpu.make_async_remote_copy(
            src_ref=block(x_ref, peer),
            dst_ref=block(o_ref, me),
            send_sem=send_sems.at[k],
            recv_sem=recv_sems.at[k],
            device_id=device_of(peer),
            device_id_type=MESH_IDS,
        )
        copy.start()
        copies.append(copy)
    own.wait()
    for copy in copies:
        copy.wait()


def exchange(x, axes, ident, split=0):
    count = x.shape[split]
    return pl.pallas_call(
        functools.partial(exchange_kernel, axes, split),
        out_shape=jax.ShapeDtypeStruct(x.shape, x.dtype),
        in_specs=[pl.BlockSpec(memory_space=pl.ANY)],
        out_specs=pl.BlockSpec(memory_space=pl.ANY),
        scratch_shapes=[
            pltpu.SemaphoreType.DMA((count,)),
            pltpu.SemaphoreType.DMA((count,)),
            pltpu.SemaphoreType.DMA(()),
        ],
        compiler_params=pltpu.CompilerParams(collective_id=ident, has_side_effects=True),
    )(x)


def attention_kernel(
    slots_ref, len_ref, q_ref, nk_ref, nv_ref, arr_ref, o_ref, kbuf, vbuf, m_sc, l_sc, acc_sc
):
    head = pl.program_id(0)
    rows, width = q_ref.shape
    page = arr_ref.shape[2]
    block_len = kbuf.shape[0]
    pages_per_block = block_len // page
    score_scale = width ** (-0.5)
    lanes = pl.ds(pl.multiple_of(head * width, width), width)
    q = q_ref[...]
    dims = (((1,), (1,)), ((), ()))
    scores = lax.dot_general(q, nk_ref[...], dims, preferred_element_type=jnp.float32) * score_scale
    row_i = lax.broadcasted_iota(jnp.int32, (rows, rows), 0)
    col_i = lax.broadcasted_iota(jnp.int32, (rows, rows), 1)
    scores = jnp.where(col_i <= row_i, scores, -1e30)
    peak = jnp.max(scores, axis=-1, keepdims=True)
    weights = jnp.exp(scores - peak)
    m_sc[...] = peak
    l_sc[...] = jnp.sum(weights, axis=-1, keepdims=True)
    acc_sc[...] = jnp.dot(weights.astype(jnp.bfloat16), nv_ref[...], preferred_element_type=jnp.float32)
    length = len_ref[0]
    block_count = (length + block_len - 1) // block_len

    def one_block(b, carry):
        for i in range(pages_per_block):
            slot = slots_ref[b * pages_per_block + i]
            kbuf[pl.ds(i * page, page), :] = arr_ref[slot, 0, :, lanes]
            vbuf[pl.ds(i * page, page), :] = arr_ref[slot, 1, :, lanes]
        block_scores = (
            lax.dot_general(q, kbuf[...], dims, preferred_element_type=jnp.float32) * score_scale
        )
        position = b * block_len + lax.broadcasted_iota(jnp.int32, (rows, block_len), 1)
        block_scores = jnp.where(position < length, block_scores, -1e30)
        old_peak = m_sc[...]
        new_peak = jnp.maximum(old_peak, jnp.max(block_scores, axis=-1, keepdims=True))
        block_weights = jnp.exp(block_scores - new_peak)
        factor = jnp.exp(old_peak - new_peak)
        l_sc[...] = l_sc[...] * factor + jnp.sum(block_weights, axis=-1, keepdims=True)
        acc_sc[...] = acc_sc[...] * factor + jnp.dot(
            block_weights.astype(jnp.bfloat16), vbuf[...], preferred_element_type=jnp.float32
        )
        m_sc[...] = new_peak
        return carry

    lax.fori_loop(0, block_count, one_block, 0)
    o_ref[...] = (acc_sc[...] / l_sc[...]).astype(o_ref.dtype)


def paged_attention(slots, length, queries, new_keys, new_values, arrived, block_len):
    rows, local_width = queries.shape
    heads = local_width // HEAD_DIM
    slot_count, _, page, _ = arrived.shape
    column = lambda h, *_: (0, h)
    spec = pl.BlockSpec((rows, HEAD_DIM), column)
    cost = pl.CostEstimate(
        flops=4 * rows * (rows + CTX) * local_width,
        transcendentals=rows * (rows + CTX) * heads,
        bytes_accessed=arrived.size * 2 + 4 * rows * local_width * 2,
    )
    return pl.pallas_call(
        attention_kernel,
        out_shape=jax.ShapeDtypeStruct((rows, local_width), jnp.bfloat16),
        grid_spec=pltpu.PrefetchScalarGridSpec(
            num_scalar_prefetch=2,
            grid=(heads,),
            in_specs=[
                spec,
                spec,
                spec,
                pl.BlockSpec(arrived.shape, lambda h, *_: (0, 0, 0, 0)),
            ],
            out_specs=spec,
            scratch_shapes=[
                pltpu.VMEM((block_len, HEAD_DIM), jnp.bfloat16),
                pltpu.VMEM((block_len, HEAD_DIM), jnp.bfloat16),
                pltpu.VMEM((rows, 1), jnp.float32),
                pltpu.VMEM((rows, 1), jnp.float32),
                pltpu.VMEM((rows, HEAD_DIM), jnp.float32),
            ],
        ),
        compiler_params=pltpu.CompilerParams(vmem_limit_bytes=48 * 1024 * 1024),
        cost_estimate=cost,
    )(slots, length, queries, new_keys, new_values, arrived)


def shards(
    hidden_in,
    cache_len,
    page_table,
    pool,
    attn_gain,
    w_qkv,
    w_out,
    moe_gain,
    w_gate,
    w_up,
    w_down,
    expert_ids,
    gate_weights,
):
    groups = lax.axis_size("group")
    expert_lanes = lax.axis_size(EXPERT)
    group_index = lax.axis_index("group")
    tok_rows = hidden_in.shape[0]
    model_width = hidden_in.shape[1]
    local_width = w_out.shape[0]
    head_size = HEAD_DIM
    local_heads = local_width // head_size
    new_count = tok_rows * expert_lanes
    block_len = CTX // NBLK
    length = cache_len[group_index]
    normed = norm_rows(hidden_in, attn_gain)
    projection = w_qkv.reshape(model_width, 3 * local_width)
    projected = jnp.dot(
        lax.all_gather(normed, EXPERT, axis=0, tiled=True),
        projection,
        preferred_element_type=jnp.float32,
    )
    projected = projected.reshape(new_count, 3, local_heads, head_size)
    positions = (length + jnp.arange(new_count, dtype=jnp.int32)).astype(jnp.float32)
    queries = rotate(projected[:, 0], positions).astype(jnp.bfloat16)
    new_keys = rotate(projected[:, 1], positions).astype(jnp.bfloat16)
    new_values = projected[:, 2].astype(jnp.bfloat16)
    pages_per = page_table.shape[1]
    page_most = max(1, pages_per // min(groups, 16))
    owner_group = page_table // pages_per
    local_slot = page_table % pages_per
    page_order = jnp.arange(pages_per, dtype=jnp.int32)
    mine = (owner_group == group_index).astype(jnp.int32)
    mine_rank = jnp.cumsum(mine, axis=1) - mine
    slot_ids = jnp.arange(page_most, dtype=jnp.int32)
    pick = (mine[:, None, :] > 0) & (mine_rank[:, None, :] == slot_ids[None, :, None])
    send_index = jnp.sum(jnp.where(pick, local_slot[:, None, :], 0), axis=-1)
    outgoing = pool[send_index]
    arrived = lax.all_to_all(outgoing, "group", split_axis=0, concat_axis=0, tiled=True)
    arrived = arrived.reshape((groups * page_most,) + pool.shape[1:])
    my_owner = owner_group[group_index]
    before = page_order[None, :] < page_order[:, None]
    my_rank = jnp.sum(jnp.logical_and(my_owner[:, None] == my_owner[None, :], before), axis=-1)
    slots = (my_owner * page_most + my_rank).astype(jnp.int32)
    attended = paged_attention(
        slots,
        jnp.reshape(length, (1,)).astype(jnp.int32),
        queries.reshape(new_count, local_width),
        new_keys.reshape(new_count, local_width),
        new_values.reshape(new_count, local_width),
        arrived,
        block_len,
    )
    head_weights = lax.all_gather(w_out, EXPERT, axis=0, tiled=True)
    head_weights = head_weights.reshape(expert_lanes, local_width, model_width)
    rows_piece = lax.all_to_all(
        attended.reshape(expert_lanes, tok_rows, local_width), EXPERT, 0, 0, tiled=True
    )
    head_parts = jnp.einsum(
        "gtc,gcd->gtd", rows_piece, head_weights, preferred_element_type=jnp.float32
    ).astype(jnp.bfloat16)
    head_sum = jnp.sum(head_parts.astype(jnp.float32), axis=0)
    residual = hidden_in.astype(jnp.float32) + head_sum
    moe_in = norm_rows(residual, moe_gain)
    route_count = expert_ids.shape[1]
    capacity = 2 * tok_rows * route_count // expert_lanes
    flat_expert = expert_ids.reshape(-1)
    assign_index = jnp.arange(flat_expert.shape[0], dtype=jnp.int32)
    earlier = assign_index[None, :] < assign_index[:, None]
    slot_index = jnp.sum(
        jnp.logical_and(flat_expert[:, None] == flat_expert[None, :], earlier), axis=-1
    )
    token_of = assign_index // route_count
    slot_of = flat_expert * capacity + slot_index
    dest_ids = jnp.arange(expert_lanes * capacity, dtype=jnp.int32)
    token_ids = jnp.arange(tok_rows, dtype=jnp.int32)
    hit = (slot_of[None, :] == dest_ids[:, None])
    source_token = jnp.sum(jnp.where(hit, token_of[None, :], 0), axis=-1)
    has_source = jnp.any(hit, axis=-1)
    select = ((source_token[:, None] == token_ids[None, :]) & has_source[:, None]).astype(jnp.bfloat16)
    outgoing_rows = (
        jnp.dot(select, moe_in, preferred_element_type=jnp.float32)
        .astype(jnp.bfloat16)
        .reshape(expert_lanes, capacity, model_width)
    )
    rows_piece = exchange(outgoing_rows, EXPERT, 0)
    flat_rows = rows_piece.reshape(-1, rows_piece.shape[-1])
    gate_part = jnp.dot(flat_rows, w_gate[0], preferred_element_type=jnp.float32)
    up_part = jnp.dot(flat_rows, w_up[0], preferred_element_type=jnp.float32)
    hidden = (jax.nn.silu(gate_part) * up_part).astype(jnp.bfloat16)
    result = (
        jnp.dot(hidden, w_down[0], preferred_element_type=jnp.float32)
        .astype(jnp.bfloat16)
        .reshape(rows_piece.shape)
    )
    returned = exchange(result, EXPERT, 1)
    picked = returned.reshape(expert_lanes * capacity, model_width)[
        flat_expert * capacity + slot_index
    ]
    weighted = jnp.sum(
        picked.reshape(tok_rows, route_count, model_width).astype(jnp.float32)
        * gate_weights[..., None],
        axis=1,
    )
    return residual + weighted


def solution(mesh):
    lanes = mesh.shape["expert"]
    cores = 2 if lanes % 2 == 0 else 1
    split = jax.sharding.Mesh(
        mesh.devices.reshape(mesh.shape["group"], lanes // cores, cores), ("group",) + EXPERT
    )
    rows = ("group",) + EXPERT
    placed = (
        P(rows, None),
        P(),
        P(),
        P("group", None, None, EXPERT),
        P(),
        P(None, None, EXPERT),
        P(EXPERT, None),
        P(),
        P(EXPERT, None, None),
        P(EXPERT, None, None),
        P(EXPERT, None, None),
        P(rows, None),
        P(rows, None),
    )
    return jax.shard_map(
        shards, mesh=split, in_specs=placed, out_specs=P(rows, None), check_vma=False
    )
```

```python
import functools

import jax
import jax.numpy as jnp
from jax import lax
from jax.experimental import pallas as pl
from jax.experimental.pallas import tpu as pltpu
from jax.sharding import PartitionSpec as P

HEAD_DIM = 128
EXPERT = ("ey", "ec")
MESH_AXES = ("group", "ey", "ec")
MESH_IDS = pl.DeviceIdType.MESH
NBLK = 1
CTX = 2048


def norm_rows(inputs, gain_vector):
    values = inputs.astype(jnp.float32)
    factor = lax.rsqrt(jnp.mean(values * values, axis=-1, keepdims=True) + 1e-05)
    return (values * factor * gain_vector).astype(jnp.bfloat16)


def rotate(vectors, positions):
    half_dim = vectors.shape[-1] // 2
    frequency = 10000.0 ** (-jnp.arange(half_dim).astype(jnp.float32) / half_dim)
    angles = positions[:, None] * frequency[None, :]
    cosine = jnp.cos(angles)[:, None, :]
    sine_part = jnp.sin(angles)[:, None, :]
    first_half = vectors[..., :half_dim]
    second_half = vectors[..., half_dim:]
    return jnp.concatenate(
        [
            first_half * cosine - second_half * sine_part,
            first_half * sine_part + second_half * cosine,
        ],
        axis=-1,
    )


def attend_block(softmax_state, queries, key_block, value_block, key_valid):
    old_peak, old_total, old_mixed = softmax_state
    score_scale = queries.shape[-1] ** (-0.5)
    scores = (
        jnp.einsum("qhd,khd->hqk", queries, key_block, preferred_element_type=jnp.float32)
        * score_scale
    )
    scores = jnp.where(key_valid[None], scores, -1e30)
    new_peak = jnp.maximum(old_peak, jnp.max(scores, axis=-1))
    weights = jnp.exp(scores - new_peak[..., None])
    factor = jnp.exp(old_peak - new_peak)
    new_total = old_total * factor + jnp.sum(weights, axis=-1)
    new_mixed = old_mixed * factor[..., None] + jnp.einsum(
        "hqk,khd->hqd",
        weights.astype(jnp.bfloat16),
        value_block,
        preferred_element_type=jnp.float32,
    )
    return (new_peak, new_total, new_mixed)


def cache_pass(
    softmax_state,
    queries,
    all_keys,
    all_values,
    length,
    turn_count,
    array_step,
    array_first,
    position_step,
    position_first,
    block_len,
):

    def step_once(turn_index, running):
        array_start = (array_first + array_step * turn_index) * block_len
        position_start = (position_first + position_step * turn_index) * block_len
        key_block = lax.dynamic_slice_in_dim(all_keys, array_start, block_len, 0)
        value_block = lax.dynamic_slice_in_dim(all_values, array_start, block_len, 0)
        key_valid = (position_start + jnp.arange(block_len, dtype=jnp.int32) < length)[None, :]
        return attend_block(running, queries, key_block, value_block, key_valid)

    return lax.fori_loop(0, turn_count, step_once, softmax_state)


def exchange_kernel(axes, split, x_ref, o_ref, send_sems, recv_sems, own_sem):
    sizes = [lax.axis_size(a) for a in axes]
    count = 1
    for size in sizes:
        count *= size
    me = 0
    for a, size in zip(axes, sizes):
        me = me * size + lax.axis_index(a)

    def device_of(peer):
        coords = {}
        rest = peer
        for a, size in reversed(list(zip(axes, sizes))):
            coords[a] = rest % size
            rest = rest // size
        return tuple(coords.get(a, lax.axis_index(a)) for a in MESH_AXES)

    barrier = pltpu.get_barrier_semaphore()
    for k in range(1, count):
        pl.semaphore_signal(
            barrier, inc=1, device_id=device_of((me + k) % count), device_id_type=MESH_IDS
        )
    pl.semaphore_wait(barrier, count - 1)
    def block(ref, index):
        return ref.at[index] if split == 0 else ref.at[:, index]

    own = pltpu.make_async_copy(block(x_ref, me), block(o_ref, me), own_sem)
    own.start()
    copies = []
    for k in range(1, count):
        peer = (me + k) % count
        copy = pltpu.make_async_remote_copy(
            src_ref=block(x_ref, peer),
            dst_ref=block(o_ref, me),
            send_sem=send_sems.at[k],
            recv_sem=recv_sems.at[k],
            device_id=device_of(peer),
            device_id_type=MESH_IDS,
        )
        copy.start()
        copies.append(copy)
    own.wait()
    for copy in copies:
        copy.wait()


def exchange(x, axes, ident, split=0):
    count = x.shape[split]
    return pl.pallas_call(
        functools.partial(exchange_kernel, axes, split),
        out_shape=jax.ShapeDtypeStruct(x.shape, x.dtype),
        in_specs=[pl.BlockSpec(memory_space=pl.ANY)],
        out_specs=pl.BlockSpec(memory_space=pl.ANY),
        scratch_shapes=[
            pltpu.SemaphoreType.DMA((count,)),
            pltpu.SemaphoreType.DMA((count,)),
            pltpu.SemaphoreType.DMA(()),
        ],
        compiler_params=pltpu.CompilerParams(collective_id=ident, has_side_effects=True),
    )(x)


def attention_kernel(
    slots_ref, len_ref, q_ref, nk_ref, nv_ref, arr_ref, o_ref, kbuf, vbuf, m_sc, l_sc, acc_sc
):
    head = pl.program_id(0)
    rows, width = q_ref.shape
    page = arr_ref.shape[2]
    block_len = kbuf.shape[0]
    pages_per_block = block_len // page
    score_scale = width ** (-0.5)
    lanes = pl.ds(pl.multiple_of(head * width, width), width)
    q = q_ref[...]
    dims = (((1,), (1,)), ((), ()))
    scores = lax.dot_general(q, nk_ref[...], dims, preferred_element_type=jnp.float32) * score_scale
    row_i = lax.broadcasted_iota(jnp.int32, (rows, rows), 0)
    col_i = lax.broadcasted_iota(jnp.int32, (rows, rows), 1)
    scores = jnp.where(col_i <= row_i, scores, -1e30)
    peak = jnp.max(scores, axis=-1, keepdims=True)
    weights = jnp.exp(scores - peak)
    m_sc[...] = peak
    l_sc[...] = jnp.sum(weights, axis=-1, keepdims=True)
    acc_sc[...] = jnp.dot(weights.astype(jnp.bfloat16), nv_ref[...], preferred_element_type=jnp.float32)
    length = len_ref[0]
    block_count = (length + block_len - 1) // block_len

    def one_block(b, carry):
        for i in range(pages_per_block):
            slot = slots_ref[b * pages_per_block + i]
            kbuf[pl.ds(i * page, page), :] = arr_ref[slot, 0, :, lanes]
            vbuf[pl.ds(i * page, page), :] = arr_ref[slot, 1, :, lanes]
        block_scores = (
            lax.dot_general(q, kbuf[...], dims, preferred_element_type=jnp.float32) * score_scale
        )
        position = b * block_len + lax.broadcasted_iota(jnp.int32, (rows, block_len), 1)
        block_scores = jnp.where(position < length, block_scores, -1e30)
        old_peak = m_sc[...]
        new_peak = jnp.maximum(old_peak, jnp.max(block_scores, axis=-1, keepdims=True))
        block_weights = jnp.exp(block_scores - new_peak)
        factor = jnp.exp(old_peak - new_peak)
        l_sc[...] = l_sc[...] * factor + jnp.sum(block_weights, axis=-1, keepdims=True)
        acc_sc[...] = acc_sc[...] * factor + jnp.dot(
            block_weights.astype(jnp.bfloat16), vbuf[...], preferred_element_type=jnp.float32
        )
        m_sc[...] = new_peak
        return carry

    lax.fori_loop(0, block_count, one_block, 0)
    o_ref[...] = (acc_sc[...] / l_sc[...]).astype(o_ref.dtype)


def paged_attention(slots, length, queries, new_keys, new_values, arrived, block_len):
    rows, local_width = queries.shape
    heads = local_width // HEAD_DIM
    slot_count, _, page, _ = arrived.shape
    column = lambda h, *_: (0, h)
    spec = pl.BlockSpec((rows, HEAD_DIM), column)
    cost = pl.CostEstimate(
        flops=4 * rows * (rows + CTX) * local_width,
        transcendentals=rows * (rows + CTX) * heads,
        bytes_accessed=arrived.size * 2 + 4 * rows * local_width * 2,
    )
    return pl.pallas_call(
        attention_kernel,
        out_shape=jax.ShapeDtypeStruct((rows, local_width), jnp.bfloat16),
        grid_spec=pltpu.PrefetchScalarGridSpec(
            num_scalar_prefetch=2,
            grid=(heads,),
            in_specs=[
                spec,
                spec,
                spec,
                pl.BlockSpec(arrived.shape, lambda h, *_: (0, 0, 0, 0)),
            ],
            out_specs=spec,
            scratch_shapes=[
                pltpu.VMEM((block_len, HEAD_DIM), jnp.bfloat16),
                pltpu.VMEM((block_len, HEAD_DIM), jnp.bfloat16),
                pltpu.VMEM((rows, 1), jnp.float32),
                pltpu.VMEM((rows, 1), jnp.float32),
                pltpu.VMEM((rows, HEAD_DIM), jnp.float32),
            ],
        ),
        compiler_params=pltpu.CompilerParams(vmem_limit_bytes=48 * 1024 * 1024),
        cost_estimate=cost,
    )(slots, length, queries, new_keys, new_values, arrived)


def shards(
    hidden_in,
    cache_len,
    page_table,
    pool,
    attn_gain,
    w_qkv,
    w_out,
    moe_gain,
    w_gate,
    w_up,
    w_down,
    expert_ids,
    gate_weights,
):
    groups = lax.axis_size("group")
    expert_lanes = lax.axis_size(EXPERT)
    group_index = lax.axis_index("group")
    tok_rows = hidden_in.shape[0]
    model_width = hidden_in.shape[1]
    local_width = w_out.shape[0]
    head_size = HEAD_DIM
    local_heads = local_width // head_size
    new_count = tok_rows * expert_lanes
    block_len = CTX // NBLK
    length = cache_len[group_index]
    normed = norm_rows(hidden_in, attn_gain)
    projection = w_qkv.reshape(model_width, 3 * local_width)
    projected = jnp.dot(
        lax.all_gather(normed, EXPERT, axis=0, tiled=True),
        projection,
        preferred_element_type=jnp.float32,
    )
    projected = projected.reshape(new_count, 3, local_heads, head_size)
    positions = (length + jnp.arange(new_count, dtype=jnp.int32)).astype(jnp.float32)
    queries = rotate(projected[:, 0], positions).astype(jnp.bfloat16)
    new_keys = rotate(projected[:, 1], positions).astype(jnp.bfloat16)
    new_values = projected[:, 2].astype(jnp.bfloat16)
    pages_per = page_table.shape[1]
    page_most = max(1, pages_per // min(groups, 16))
    owner_group = page_table // pages_per
    local_slot = page_table % pages_per
    page_order = jnp.arange(pages_per, dtype=jnp.int32)
    mine = (owner_group == group_index).astype(jnp.int32)
    mine_rank = jnp.cumsum(mine, axis=1) - mine
    slot_ids = jnp.arange(page_most, dtype=jnp.int32)
    pick = (mine[:, None, :] > 0) & (mine_rank[:, None, :] == slot_ids[None, :, None])
    send_index = jnp.sum(jnp.where(pick, local_slot[:, None, :], 0), axis=-1)
    outgoing = pool[send_index]
    arrived = lax.all_to_all(outgoing, "group", split_axis=0, concat_axis=0, tiled=True)
    arrived = arrived.reshape((groups * page_most,) + pool.shape[1:])
    my_owner = owner_group[group_index]
    before = page_order[None, :] < page_order[:, None]
    my_rank = jnp.sum(jnp.logical_and(my_owner[:, None] == my_owner[None, :], before), axis=-1)
    slots = (my_owner * page_most + my_rank).astype(jnp.int32)
    attended = paged_attention(
        slots,
        jnp.reshape(length, (1,)).astype(jnp.int32),
        queries.reshape(new_count, local_width),
        new_keys.reshape(new_count, local_width),
        new_values.reshape(new_count, local_width),
        arrived,
        block_len,
    )
    head_weights = lax.all_gather(w_out, EXPERT, axis=0, tiled=True)
    head_weights = head_weights.reshape(expert_lanes, local_width, model_width)
    rows_piece = lax.all_to_all(
        attended.reshape(expert_lanes, tok_rows, local_width), EXPERT, 0, 0, tiled=True
    )
    head_parts = jnp.einsum(
        "gtc,gcd->gtd", rows_piece, head_weights, preferred_element_type=jnp.float32
    ).astype(jnp.bfloat16)
    head_sum = jnp.sum(head_parts.astype(jnp.float32), axis=0)
    residual = hidden_in.astype(jnp.float32) + head_sum
    moe_in = norm_rows(residual, moe_gain)
    route_count = expert_ids.shape[1]
    capacity = 2 * tok_rows * route_count // expert_lanes
    flat_expert = expert_ids.reshape(-1)
    assign_index = jnp.arange(flat_expert.shape[0], dtype=jnp.int32)
    earlier = assign_index[None, :] < assign_index[:, None]
    slot_index = jnp.sum(
        jnp.logical_and(flat_expert[:, None] == flat_expert[None, :], earlier), axis=-1
    )
    token_of = assign_index // route_count
    slot_of = flat_expert * capacity + slot_index
    dest_ids = jnp.arange(expert_lanes * capacity, dtype=jnp.int32)
    token_ids = jnp.arange(tok_rows, dtype=jnp.int32)
    hit = (slot_of[None, :] == dest_ids[:, None])
    source_token = jnp.sum(jnp.where(hit, token_of[None, :], 0), axis=-1)
    has_source = jnp.any(hit, axis=-1)
    select = ((source_token[:, None] == token_ids[None, :]) & has_source[:, None]).astype(jnp.bfloat16)
    outgoing_rows = (
        jnp.dot(select, moe_in, preferred_element_type=jnp.float32)
        .astype(jnp.bfloat16)
        .reshape(expert_lanes, capacity, model_width)
    )
    rows_piece = exchange(outgoing_rows, EXPERT, 0)
    flat_rows = rows_piece.reshape(-1, rows_piece.shape[-1])
    gate_part = jnp.dot(flat_rows, w_gate[0], preferred_element_type=jnp.float32)
    up_part = jnp.dot(flat_rows, w_up[0], preferred_element_type=jnp.float32)
    hidden = (jax.nn.silu(gate_part) * up_part).astype(jnp.bfloat16)
    result = (
        jnp.dot(hidden, w_down[0], preferred_element_type=jnp.float32)
        .astype(jnp.bfloat16)
        .reshape(rows_piece.shape)
    )
    returned = exchange(result, EXPERT, 1)
    picked = returned.reshape(expert_lanes * capacity, model_width)[
        flat_expert * capacity + slot_index
    ]
    weighted = jnp.sum(
        picked.reshape(tok_rows, route_count, model_width).astype(jnp.float32)
        * gate_weights[..., None],
        axis=1,
    )
    return residual + weighted


def solution(mesh):
    lanes = mesh.shape["expert"]
    cores = 2 if lanes % 2 == 0 else 1
    split = jax.sharding.Mesh(
        mesh.devices.reshape(mesh.shape["group"], lanes // cores, cores), ("group",) + EXPERT
    )
    rows = ("group",) + EXPERT
    placed = (
        P(rows, None),
        P(),
        P(),
        P("group", None, None, EXPERT),
        P(),
        P(None, None, EXPERT),
        P(EXPERT, None),
        P(),
        P(EXPERT, None, None),
        P(EXPERT, None, None),
        P(EXPERT, None, None),
        P(rows, None),
        P(rows, None),
    )
    return jax.shard_map(
        shards, mesh=split, in_specs=placed, out_specs=P(rows, None), check_vma=False
    )
```

```python
import functools

import jax
import jax.numpy as jnp
from jax import lax
from jax.experimental import pallas as pl
from jax.experimental.pallas import tpu as pltpu
from jax.sharding import PartitionSpec as P

HEAD_DIM = 128
EXPERT = ("ey", "ec")
MESH_AXES = ("group", "ey", "ec")
MESH_IDS = pl.DeviceIdType.MESH
NBLK = 1
CTX = 2048


def norm_rows(inputs, gain_vector):
    values = inputs.astype(jnp.float32)
    factor = lax.rsqrt(jnp.mean(values * values, axis=-1, keepdims=True) + 1e-05)
    return (values * factor * gain_vector).astype(jnp.bfloat16)


def rotate(vectors, positions):
    half_dim = vectors.shape[-1] // 2
    frequency = 10000.0 ** (-jnp.arange(half_dim).astype(jnp.float32) / half_dim)
    angles = positions[:, None] * frequency[None, :]
    cosine = jnp.cos(angles)[:, None, :]
    sine_part = jnp.sin(angles)[:, None, :]
    first_half = vectors[..., :half_dim]
    second_half = vectors[..., half_dim:]
    return jnp.concatenate(
        [
            first_half * cosine - second_half * sine_part,
            first_half * sine_part + second_half * cosine,
        ],
        axis=-1,
    )


def attend_block(softmax_state, queries, key_block, value_block, key_valid):
    old_peak, old_total, old_mixed = softmax_state
    score_scale = queries.shape[-1] ** (-0.5)
    scores = (
        jnp.einsum("qhd,khd->hqk", queries, key_block, preferred_element_type=jnp.float32)
        * score_scale
    )
    scores = jnp.where(key_valid[None], scores, -1e30)
    new_peak = jnp.maximum(old_peak, jnp.max(scores, axis=-1))
    weights = jnp.exp(scores - new_peak[..., None])
    factor = jnp.exp(old_peak - new_peak)
    new_total = old_total * factor + jnp.sum(weights, axis=-1)
    new_mixed = old_mixed * factor[..., None] + jnp.einsum(
        "hqk,khd->hqd",
        weights.astype(jnp.bfloat16),
        value_block,
        preferred_element_type=jnp.float32,
    )
    return (new_peak, new_total, new_mixed)


def cache_pass(
    softmax_state,
    queries,
    all_keys,
    all_values,
    length,
    turn_count,
    array_step,
    array_first,
    position_step,
    position_first,
    block_len,
):

    def step_once(turn_index, running):
        array_start = (array_first + array_step * turn_index) * block_len
        position_start = (position_first + position_step * turn_index) * block_len
        key_block = lax.dynamic_slice_in_dim(all_keys, array_start, block_len, 0)
        value_block = lax.dynamic_slice_in_dim(all_values, array_start, block_len, 0)
        key_valid = (position_start + jnp.arange(block_len, dtype=jnp.int32) < length)[None, :]
        return attend_block(running, queries, key_block, value_block, key_valid)

    return lax.fori_loop(0, turn_count, step_once, softmax_state)


def exchange_kernel(axes, split, x_ref, o_ref, send_sems, recv_sems, own_sem):
    sizes = [lax.axis_size(a) for a in axes]
    count = 1
    for size in sizes:
        count *= size
    me = 0
    for a, size in zip(axes, sizes):
        me = me * size + lax.axis_index(a)

    def device_of(peer):
        coords = {}
        rest = peer
        for a, size in reversed(list(zip(axes, sizes))):
            coords[a] = rest % size
            rest = rest // size
        return tuple(coords.get(a, lax.axis_index(a)) for a in MESH_AXES)

    barrier = pltpu.get_barrier_semaphore()
    for k in range(1, count):
        pl.semaphore_signal(
            barrier, inc=1, device_id=device_of((me + k) % count), device_id_type=MESH_IDS
        )
    pl.semaphore_wait(barrier, count - 1)
    def block(ref, index):
        return ref.at[index] if split == 0 else ref.at[:, index]

    own = pltpu.make_async_copy(block(x_ref, me), block(o_ref, me), own_sem)
    own.start()
    copies = []
    for k in range(1, count):
        peer = (me + k) % count
        copy = pltpu.make_async_remote_copy(
            src_ref=block(x_ref, peer),
            dst_ref=block(o_ref, me),
            send_sem=send_sems.at[k],
            recv_sem=recv_sems.at[k],
            device_id=device_of(peer),
            device_id_type=MESH_IDS,
        )
        copy.start()
        copies.append(copy)
    own.wait()
    for copy in copies:
        copy.wait()


def exchange(x, axes, ident, split=0):
    count = x.shape[split]
    return pl.pallas_call(
        functools.partial(exchange_kernel, axes, split),
        out_shape=jax.ShapeDtypeStruct(x.shape, x.dtype),
        in_specs=[pl.BlockSpec(memory_space=pl.ANY)],
        out_specs=pl.BlockSpec(memory_space=pl.ANY),
        scratch_shapes=[
            pltpu.SemaphoreType.DMA((count,)),
            pltpu.SemaphoreType.DMA((count,)),
            pltpu.SemaphoreType.DMA(()),
        ],
        compiler_params=pltpu.CompilerParams(collective_id=ident, has_side_effects=True),
    )(x)


def attention_kernel(
    slots_ref, len_ref, q_ref, nk_ref, nv_ref, arr_ref, o_ref, kbuf, vbuf, m_sc, l_sc, acc_sc
):
    head = pl.program_id(0)
    rows, width = q_ref.shape
    page = arr_ref.shape[2]
    block_len = kbuf.shape[0]
    pages_per_block = block_len // page
    score_scale = width ** (-0.5)
    lanes = pl.ds(pl.multiple_of(head * width, width), width)
    q = q_ref[...]
    dims = (((1,), (1,)), ((), ()))
    scores = lax.dot_general(q, nk_ref[...], dims, preferred_element_type=jnp.float32) * score_scale
    row_i = lax.broadcasted_iota(jnp.int32, (rows, rows), 0)
    col_i = lax.broadcasted_iota(jnp.int32, (rows, rows), 1)
    scores = jnp.where(col_i <= row_i, scores, -1e30)
    peak = jnp.max(scores, axis=-1, keepdims=True)
    weights = jnp.exp(scores - peak)
    m_sc[...] = peak
    l_sc[...] = jnp.sum(weights, axis=-1, keepdims=True)
    acc_sc[...] = jnp.dot(weights.astype(jnp.bfloat16), nv_ref[...], preferred_element_type=jnp.float32)
    length = len_ref[0]
    block_count = (length + block_len - 1) // block_len

    def one_block(b, carry):
        for i in range(pages_per_block):
            slot = slots_ref[b * pages_per_block + i]
            kbuf[pl.ds(i * page, page), :] = arr_ref[slot, 0, :, lanes]
            vbuf[pl.ds(i * page, page), :] = arr_ref[slot, 1, :, lanes]
        block_scores = (
            lax.dot_general(q, kbuf[...], dims, preferred_element_type=jnp.float32) * score_scale
        )
        position = b * block_len + lax.broadcasted_iota(jnp.int32, (rows, block_len), 1)
        block_scores = jnp.where(position < length, block_scores, -1e30)
        old_peak = m_sc[...]
        new_peak = jnp.maximum(old_peak, jnp.max(block_scores, axis=-1, keepdims=True))
        block_weights = jnp.exp(block_scores - new_peak)
        factor = jnp.exp(old_peak - new_peak)
        l_sc[...] = l_sc[...] * factor + jnp.sum(block_weights, axis=-1, keepdims=True)
        acc_sc[...] = acc_sc[...] * factor + jnp.dot(
            block_weights.astype(jnp.bfloat16), vbuf[...], preferred_element_type=jnp.float32
        )
        m_sc[...] = new_peak
        return carry

    lax.fori_loop(0, block_count, one_block, 0)
    o_ref[...] = (acc_sc[...] / l_sc[...]).astype(o_ref.dtype)


def paged_attention(slots, length, queries, new_keys, new_values, arrived, block_len):
    rows, local_width = queries.shape
    heads = local_width // HEAD_DIM
    slot_count, _, page, _ = arrived.shape
    column = lambda h, *_: (0, h)
    spec = pl.BlockSpec((rows, HEAD_DIM), column)
    cost = pl.CostEstimate(
        flops=4 * rows * (rows + CTX) * local_width,
        transcendentals=rows * (rows + CTX) * heads,
        bytes_accessed=arrived.size * 2 + 4 * rows * local_width * 2,
    )
    return pl.pallas_call(
        attention_kernel,
        out_shape=jax.ShapeDtypeStruct((rows, local_width), jnp.bfloat16),
        grid_spec=pltpu.PrefetchScalarGridSpec(
            num_scalar_prefetch=2,
            grid=(heads,),
            in_specs=[
                spec,
                spec,
                spec,
                pl.BlockSpec(arrived.shape, lambda h, *_: (0, 0, 0, 0)),
            ],
            out_specs=spec,
            scratch_shapes=[
                pltpu.VMEM((block_len, HEAD_DIM), jnp.bfloat16),
                pltpu.VMEM((block_len, HEAD_DIM), jnp.bfloat16),
                pltpu.VMEM((rows, 1), jnp.float32),
                pltpu.VMEM((rows, 1), jnp.float32),
                pltpu.VMEM((rows, HEAD_DIM), jnp.float32),
            ],
        ),
        compiler_params=pltpu.CompilerParams(vmem_limit_bytes=48 * 1024 * 1024),
        cost_estimate=cost,
    )(slots, length, queries, new_keys, new_values, arrived)


def shards(
    hidden_in,
    cache_len,
    page_table,
    pool,
    attn_gain,
    w_qkv,
    w_out,
    moe_gain,
    w_gate,
    w_up,
    w_down,
    expert_ids,
    gate_weights,
):
    groups = lax.axis_size("group")
    expert_lanes = lax.axis_size(EXPERT)
    group_index = lax.axis_index("group")
    tok_rows = hidden_in.shape[0]
    model_width = hidden_in.shape[1]
    local_width = w_out.shape[0]
    head_size = HEAD_DIM
    local_heads = local_width // head_size
    new_count = tok_rows * expert_lanes
    block_len = CTX // NBLK
    length = cache_len[group_index]
    normed = norm_rows(hidden_in, attn_gain)
    projection = w_qkv.reshape(model_width, 3 * local_width)
    projected = jnp.dot(
        lax.all_gather(normed, EXPERT, axis=0, tiled=True),
        projection,
        preferred_element_type=jnp.float32,
    )
    projected = projected.reshape(new_count, 3, local_heads, head_size)
    positions = (length + jnp.arange(new_count, dtype=jnp.int32)).astype(jnp.float32)
    queries = rotate(projected[:, 0], positions).astype(jnp.bfloat16)
    new_keys = rotate(projected[:, 1], positions).astype(jnp.bfloat16)
    new_values = projected[:, 2].astype(jnp.bfloat16)
    pages_per = page_table.shape[1]
    page_most = max(1, pages_per // min(groups, 16))
    owner_group = page_table // pages_per
    local_slot = page_table % pages_per
    page_order = jnp.arange(pages_per, dtype=jnp.int32)
    mine = (owner_group == group_index).astype(jnp.int32)
    mine_rank = jnp.cumsum(mine, axis=1) - mine
    slot_ids = jnp.arange(page_most, dtype=jnp.int32)
    pick = (mine[:, None, :] > 0) & (mine_rank[:, None, :] == slot_ids[None, :, None])
    send_index = jnp.sum(jnp.where(pick, local_slot[:, None, :], 0), axis=-1)
    outgoing = pool[send_index]
    arrived = lax.all_to_all(outgoing, "group", split_axis=0, concat_axis=0, tiled=True)
    arrived = arrived.reshape((groups * page_most,) + pool.shape[1:])
    my_owner = owner_group[group_index]
    before = page_order[None, :] < page_order[:, None]
    my_rank = jnp.sum(jnp.logical_and(my_owner[:, None] == my_owner[None, :], before), axis=-1)
    slots = (my_owner * page_most + my_rank).astype(jnp.int32)
    attended = paged_attention(
        slots,
        jnp.reshape(length, (1,)).astype(jnp.int32),
        queries.reshape(new_count, local_width),
        new_keys.reshape(new_count, local_width),
        new_values.reshape(new_count, local_width),
        arrived,
        block_len,
    )
    head_weights = lax.all_gather(w_out, EXPERT, axis=0, tiled=True)
    head_weights = head_weights.reshape(expert_lanes, local_width, model_width)
    rows_piece = lax.all_to_all(
        attended.reshape(expert_lanes, tok_rows, local_width), EXPERT, 0, 0, tiled=True
    )
    head_parts = jnp.einsum(
        "gtc,gcd->gtd", rows_piece, head_weights, preferred_element_type=jnp.float32
    ).astype(jnp.bfloat16)
    head_sum = jnp.sum(head_parts.astype(jnp.float32), axis=0)
    residual = hidden_in.astype(jnp.float32) + head_sum
    moe_in = norm_rows(residual, moe_gain)
    route_count = expert_ids.shape[1]
    capacity = 2 * tok_rows * route_count // expert_lanes
    flat_expert = expert_ids.reshape(-1)
    assign_index = jnp.arange(flat_expert.shape[0], dtype=jnp.int32)
    earlier = assign_index[None, :] < assign_index[:, None]
    slot_index = jnp.sum(
        jnp.logical_and(flat_expert[:, None] == flat_expert[None, :], earlier), axis=-1
    )
    token_of = assign_index // route_count
    slot_of = flat_expert * capacity + slot_index
    dest_ids = jnp.arange(expert_lanes * capacity, dtype=jnp.int32)
    token_ids = jnp.arange(tok_rows, dtype=jnp.int32)
    hit = (slot_of[None, :] == dest_ids[:, None])
    source_token = jnp.sum(jnp.where(hit, token_of[None, :], 0), axis=-1)
    has_source = jnp.any(hit, axis=-1)
    select = ((source_token[:, None] == token_ids[None, :]) & has_source[:, None]).astype(jnp.bfloat16)
    outgoing_rows = (
        jnp.dot(select, moe_in, preferred_element_type=jnp.float32)
        .astype(jnp.bfloat16)
        .reshape(expert_lanes, capacity, model_width)
    )
    rows_piece = exchange(outgoing_rows, EXPERT, 0)
    flat_rows = rows_piece.reshape(-1, rows_piece.shape[-1])
    gate_part = jnp.dot(flat_rows, w_gate[0], preferred_element_type=jnp.float32)
    up_part = jnp.dot(flat_rows, w_up[0], preferred_element_type=jnp.float32)
    hidden = (jax.nn.silu(gate_part) * up_part).astype(jnp.bfloat16)
    result = (
        jnp.dot(hidden, w_down[0], preferred_element_type=jnp.float32)
        .astype(jnp.bfloat16)
        .reshape(rows_piece.shape)
    )
    returned = exchange(result, EXPERT, 1)
    flat_returned = returned.reshape(expert_lanes * capacity, model_width)
    slot_pair = (flat_expert * capacity + slot_index).reshape(tok_rows, route_count)
    weighted = flat_returned[slot_pair[:, 0]].astype(jnp.float32) * gate_weights[:, 0:1]
    for k in range(1, route_count):
        weighted = weighted + flat_returned[slot_pair[:, k]].astype(jnp.float32) * gate_weights[:, k : k + 1]
    return residual + weighted


def solution(mesh):
    lanes = mesh.shape["expert"]
    cores = 2 if lanes % 2 == 0 else 1
    split = jax.sharding.Mesh(
        mesh.devices.reshape(mesh.shape["group"], lanes // cores, cores), ("group",) + EXPERT
    )
    rows = ("group",) + EXPERT
    placed = (
        P(rows, None),
        P(),
        P(),
        P("group", None, None, EXPERT),
        P(),
        P(None, None, EXPERT),
        P(EXPERT, None),
        P(),
        P(EXPERT, None, None),
        P(EXPERT, None, None),
        P(EXPERT, None, None),
        P(rows, None),
        P(rows, None),
    )
    return jax.shard_map(
        shards, mesh=split, in_specs=placed, out_specs=P(rows, None), check_vma=False
    )
```

```python
import functools

import jax
import jax.numpy as jnp
from jax import lax
from jax.experimental import pallas as pl
from jax.experimental.pallas import tpu as pltpu
from jax.sharding import PartitionSpec as P

HEAD_DIM = 128
EXPERT = ("ey", "ec")
MESH_AXES = ("group", "ey", "ec")
MESH_IDS = pl.DeviceIdType.MESH
NBLK = 1
CTX = 2048


def norm_rows(inputs, gain_vector):
    values = inputs.astype(jnp.float32)
    factor = lax.rsqrt(jnp.mean(values * values, axis=-1, keepdims=True) + 1e-05)
    return (values * factor * gain_vector).astype(jnp.bfloat16)


def rotate(vectors, positions):
    half_dim = vectors.shape[-1] // 2
    frequency = 10000.0 ** (-jnp.arange(half_dim).astype(jnp.float32) / half_dim)
    angles = positions[:, None] * frequency[None, :]
    cosine = jnp.cos(angles)[:, None, :]
    sine_part = jnp.sin(angles)[:, None, :]
    first_half = vectors[..., :half_dim]
    second_half = vectors[..., half_dim:]
    return jnp.concatenate(
        [
            first_half * cosine - second_half * sine_part,
            first_half * sine_part + second_half * cosine,
        ],
        axis=-1,
    )


def attend_block(softmax_state, queries, key_block, value_block, key_valid):
    old_peak, old_total, old_mixed = softmax_state
    score_scale = queries.shape[-1] ** (-0.5)
    scores = (
        jnp.einsum("qhd,khd->hqk", queries, key_block, preferred_element_type=jnp.float32)
        * score_scale
    )
    scores = jnp.where(key_valid[None], scores, -1e30)
    new_peak = jnp.maximum(old_peak, jnp.max(scores, axis=-1))
    weights = jnp.exp(scores - new_peak[..., None])
    factor = jnp.exp(old_peak - new_peak)
    new_total = old_total * factor + jnp.sum(weights, axis=-1)
    new_mixed = old_mixed * factor[..., None] + jnp.einsum(
        "hqk,khd->hqd",
        weights.astype(jnp.bfloat16),
        value_block,
        preferred_element_type=jnp.float32,
    )
    return (new_peak, new_total, new_mixed)


def cache_pass(
    softmax_state,
    queries,
    all_keys,
    all_values,
    length,
    turn_count,
    array_step,
    array_first,
    position_step,
    position_first,
    block_len,
):

    def step_once(turn_index, running):
        array_start = (array_first + array_step * turn_index) * block_len
        position_start = (position_first + position_step * turn_index) * block_len
        key_block = lax.dynamic_slice_in_dim(all_keys, array_start, block_len, 0)
        value_block = lax.dynamic_slice_in_dim(all_values, array_start, block_len, 0)
        key_valid = (position_start + jnp.arange(block_len, dtype=jnp.int32) < length)[None, :]
        return attend_block(running, queries, key_block, value_block, key_valid)

    return lax.fori_loop(0, turn_count, step_once, softmax_state)


def exchange_kernel(axes, split, x_ref, o_ref, send_sems, recv_sems, own_sem):
    sizes = [lax.axis_size(a) for a in axes]
    count = 1
    for size in sizes:
        count *= size
    me = 0
    for a, size in zip(axes, sizes):
        me = me * size + lax.axis_index(a)

    def device_of(peer):
        coords = {}
        rest = peer
        for a, size in reversed(list(zip(axes, sizes))):
            coords[a] = rest % size
            rest = rest // size
        return tuple(coords.get(a, lax.axis_index(a)) for a in MESH_AXES)

    barrier = pltpu.get_barrier_semaphore()
    for k in range(1, count):
        pl.semaphore_signal(
            barrier, inc=1, device_id=device_of((me + k) % count), device_id_type=MESH_IDS
        )
    pl.semaphore_wait(barrier, count - 1)
    def block(ref, index):
        return ref.at[index] if split == 0 else ref.at[:, index]

    own = pltpu.make_async_copy(block(x_ref, me), block(o_ref, me), own_sem)
    own.start()
    copies = []
    for k in range(1, count):
        peer = (me + k) % count
        copy = pltpu.make_async_remote_copy(
            src_ref=block(x_ref, peer),
            dst_ref=block(o_ref, me),
            send_sem=send_sems.at[k],
            recv_sem=recv_sems.at[k],
            device_id=device_of(peer),
            device_id_type=MESH_IDS,
        )
        copy.start()
        copies.append(copy)
    own.wait()
    for copy in copies:
        copy.wait()


def exchange(x, axes, ident, split=0):
    count = x.shape[split]
    return pl.pallas_call(
        functools.partial(exchange_kernel, axes, split),
        out_shape=jax.ShapeDtypeStruct(x.shape, x.dtype),
        in_specs=[pl.BlockSpec(memory_space=pl.ANY)],
        out_specs=pl.BlockSpec(memory_space=pl.ANY),
        scratch_shapes=[
            pltpu.SemaphoreType.DMA((count,)),
            pltpu.SemaphoreType.DMA((count,)),
            pltpu.SemaphoreType.DMA(()),
        ],
        compiler_params=pltpu.CompilerParams(collective_id=ident, has_side_effects=True),
    )(x)


def attention_kernel(
    slots_ref, len_ref, q_ref, nk_ref, nv_ref, arr_ref, o_ref, kbuf, vbuf, m_sc, l_sc, acc_sc
):
    head = pl.program_id(0)
    rows, width = q_ref.shape
    page = arr_ref.shape[2]
    block_len = kbuf.shape[0]
    pages_per_block = block_len // page
    score_scale = width ** (-0.5)
    lanes = pl.ds(pl.multiple_of(head * width, width), width)
    q = q_ref[...]
    dims = (((1,), (1,)), ((), ()))
    scores = lax.dot_general(q, nk_ref[...], dims, preferred_element_type=jnp.float32) * score_scale
    row_i = lax.broadcasted_iota(jnp.int32, (rows, rows), 0)
    col_i = lax.broadcasted_iota(jnp.int32, (rows, rows), 1)
    scores = jnp.where(col_i <= row_i, scores, -1e30)
    peak = jnp.max(scores, axis=-1, keepdims=True)
    weights = jnp.exp(scores - peak)
    m_sc[...] = peak
    l_sc[...] = jnp.sum(weights, axis=-1, keepdims=True)
    acc_sc[...] = jnp.dot(weights.astype(jnp.bfloat16), nv_ref[...], preferred_element_type=jnp.float32)
    length = len_ref[0]
    block_count = (length + block_len - 1) // block_len

    def one_block(b, carry):
        for i in range(pages_per_block):
            slot = slots_ref[b * pages_per_block + i]
            kbuf[pl.ds(i * page, page), :] = arr_ref[slot, 0, :, lanes]
            vbuf[pl.ds(i * page, page), :] = arr_ref[slot, 1, :, lanes]
        block_scores = (
            lax.dot_general(q, kbuf[...], dims, preferred_element_type=jnp.float32) * score_scale
        )
        position = b * block_len + lax.broadcasted_iota(jnp.int32, (rows, block_len), 1)
        block_scores = jnp.where(position < length, block_scores, -1e30)
        old_peak = m_sc[...]
        new_peak = jnp.maximum(old_peak, jnp.max(block_scores, axis=-1, keepdims=True))
        block_weights = jnp.exp(block_scores - new_peak)
        factor = jnp.exp(old_peak - new_peak)
        l_sc[...] = l_sc[...] * factor + jnp.sum(block_weights, axis=-1, keepdims=True)
        acc_sc[...] = acc_sc[...] * factor + jnp.dot(
            block_weights.astype(jnp.bfloat16), vbuf[...], preferred_element_type=jnp.float32
        )
        m_sc[...] = new_peak
        return carry

    lax.fori_loop(0, block_count, one_block, 0)
    o_ref[...] = (acc_sc[...] / l_sc[...]).astype(o_ref.dtype)


def paged_attention(slots, length, queries, new_keys, new_values, arrived, block_len):
    rows, local_width = queries.shape
    heads = local_width // HEAD_DIM
    slot_count, _, page, _ = arrived.shape
    column = lambda h, *_: (0, h)
    spec = pl.BlockSpec((rows, HEAD_DIM), column)
    cost = pl.CostEstimate(
        flops=4 * rows * (rows + CTX) * local_width,
        transcendentals=rows * (rows + CTX) * heads,
        bytes_accessed=arrived.size * 2 + 4 * rows * local_width * 2,
    )
    return pl.pallas_call(
        attention_kernel,
        out_shape=jax.ShapeDtypeStruct((rows, local_width), jnp.bfloat16),
        grid_spec=pltpu.PrefetchScalarGridSpec(
            num_scalar_prefetch=2,
            grid=(heads,),
            in_specs=[
                spec,
                spec,
                spec,
                pl.BlockSpec(arrived.shape, lambda h, *_: (0, 0, 0, 0)),
            ],
            out_specs=spec,
            scratch_shapes=[
                pltpu.VMEM((block_len, HEAD_DIM), jnp.bfloat16),
                pltpu.VMEM((block_len, HEAD_DIM), jnp.bfloat16),
                pltpu.VMEM((rows, 1), jnp.float32),
                pltpu.VMEM((rows, 1), jnp.float32),
                pltpu.VMEM((rows, HEAD_DIM), jnp.float32),
            ],
        ),
        compiler_params=pltpu.CompilerParams(vmem_limit_bytes=48 * 1024 * 1024),
        cost_estimate=cost,
    )(slots, length, queries, new_keys, new_values, arrived)


def shards(
    hidden_in,
    cache_len,
    page_table,
    pool,
    attn_gain,
    w_qkv,
    w_out,
    moe_gain,
    w_gate,
    w_up,
    w_down,
    expert_ids,
    gate_weights,
):
    groups = lax.axis_size("group")
    expert_lanes = lax.axis_size(EXPERT)
    group_index = lax.axis_index("group")
    tok_rows = hidden_in.shape[0]
    model_width = hidden_in.shape[1]
    local_width = w_out.shape[0]
    head_size = HEAD_DIM
    local_heads = local_width // head_size
    new_count = tok_rows * expert_lanes
    block_len = CTX // NBLK
    length = cache_len[group_index]
    normed = norm_rows(hidden_in, attn_gain)
    projection = w_qkv.reshape(model_width, 3 * local_width)
    projected = jnp.dot(
        lax.all_gather(normed, EXPERT, axis=0, tiled=True),
        projection,
        preferred_element_type=jnp.float32,
    )
    projected = projected.reshape(new_count, 3, local_heads, head_size)
    positions = (length + jnp.arange(new_count, dtype=jnp.int32)).astype(jnp.float32)
    queries = rotate(projected[:, 0], positions).astype(jnp.bfloat16)
    new_keys = rotate(projected[:, 1], positions).astype(jnp.bfloat16)
    new_values = projected[:, 2].astype(jnp.bfloat16)
    pages_per = page_table.shape[1]
    page_most = max(1, pages_per // min(groups, 16))
    owner_group = page_table // pages_per
    local_slot = page_table % pages_per
    page_order = jnp.arange(pages_per, dtype=jnp.int32)
    mine = (owner_group == group_index).astype(jnp.int32)
    mine_rank = jnp.cumsum(mine, axis=1) - mine
    slot_ids = jnp.arange(page_most, dtype=jnp.int32)
    pick = (mine[:, None, :] > 0) & (mine_rank[:, None, :] == slot_ids[None, :, None])
    send_index = jnp.sum(jnp.where(pick, local_slot[:, None, :], 0), axis=-1)
    outgoing = pool[send_index]
    arrived = lax.all_to_all(outgoing, "group", split_axis=0, concat_axis=0, tiled=True)
    arrived = arrived.reshape((groups * page_most,) + pool.shape[1:])
    my_owner = owner_group[group_index]
    before = page_order[None, :] < page_order[:, None]
    my_rank = jnp.sum(jnp.logical_and(my_owner[:, None] == my_owner[None, :], before), axis=-1)
    slots = (my_owner * page_most + my_rank).astype(jnp.int32)
    attended = paged_attention(
        slots,
        jnp.reshape(length, (1,)).astype(jnp.int32),
        queries.reshape(new_count, local_width),
        new_keys.reshape(new_count, local_width),
        new_values.reshape(new_count, local_width),
        arrived,
        block_len,
    )
    head_weights = lax.all_gather(w_out, EXPERT, axis=0, tiled=True)
    head_weights = head_weights.reshape(expert_lanes, local_width, model_width)
    rows_piece = exchange(attended.reshape(expert_lanes, tok_rows, local_width), EXPERT, 2)
    head_parts = jnp.einsum(
        "gtc,gcd->gtd", rows_piece, head_weights, preferred_element_type=jnp.float32
    ).astype(jnp.bfloat16)
    head_sum = jnp.sum(head_parts.astype(jnp.float32), axis=0)
    residual = hidden_in.astype(jnp.float32) + head_sum
    moe_in = norm_rows(residual, moe_gain)
    route_count = expert_ids.shape[1]
    capacity = 2 * tok_rows * route_count // expert_lanes
    flat_expert = expert_ids.reshape(-1)
    assign_index = jnp.arange(flat_expert.shape[0], dtype=jnp.int32)
    earlier = assign_index[None, :] < assign_index[:, None]
    slot_index = jnp.sum(
        jnp.logical_and(flat_expert[:, None] == flat_expert[None, :], earlier), axis=-1
    )
    token_of = assign_index // route_count
    slot_of = flat_expert * capacity + slot_index
    dest_ids = jnp.arange(expert_lanes * capacity, dtype=jnp.int32)
    token_ids = jnp.arange(tok_rows, dtype=jnp.int32)
    hit = (slot_of[None, :] == dest_ids[:, None])
    source_token = jnp.sum(jnp.where(hit, token_of[None, :], 0), axis=-1)
    has_source = jnp.any(hit, axis=-1)
    select = ((source_token[:, None] == token_ids[None, :]) & has_source[:, None]).astype(jnp.bfloat16)
    outgoing_rows = (
        jnp.dot(select, moe_in, preferred_element_type=jnp.float32)
        .astype(jnp.bfloat16)
        .reshape(expert_lanes, capacity, model_width)
    )
    rows_piece = exchange(outgoing_rows, EXPERT, 0)
    flat_rows = rows_piece.reshape(-1, rows_piece.shape[-1])
    gate_part = jnp.dot(flat_rows, w_gate[0], preferred_element_type=jnp.float32)
    up_part = jnp.dot(flat_rows, w_up[0], preferred_element_type=jnp.float32)
    hidden = (jax.nn.silu(gate_part) * up_part).astype(jnp.bfloat16)
    result = (
        jnp.dot(hidden, w_down[0], preferred_element_type=jnp.float32)
        .astype(jnp.bfloat16)
        .reshape(rows_piece.shape)
    )
    returned = exchange(result, EXPERT, 1)
    picked = returned.reshape(expert_lanes * capacity, model_width)[
        flat_expert * capacity + slot_index
    ]
    weighted = jnp.sum(
        picked.reshape(tok_rows, route_count, model_width).astype(jnp.float32)
        * gate_weights[..., None],
        axis=1,
    )
    return residual + weighted


def solution(mesh):
    lanes = mesh.shape["expert"]
    cores = 2 if lanes % 2 == 0 else 1
    split = jax.sharding.Mesh(
        mesh.devices.reshape(mesh.shape["group"], lanes // cores, cores), ("group",) + EXPERT
    )
    rows = ("group",) + EXPERT
    placed = (
        P(rows, None),
        P(),
        P(),
        P("group", None, None, EXPERT),
        P(),
        P(None, None, EXPERT),
        P(EXPERT, None),
        P(),
        P(EXPERT, None, None),
        P(EXPERT, None, None),
        P(EXPERT, None, None),
        P(rows, None),
        P(rows, None),
    )
    return jax.shard_map(
        shards, mesh=split, in_specs=placed, out_specs=P(rows, None), check_vma=False
    )
```

```python
import functools

import jax
import jax.numpy as jnp
from jax import lax
from jax.experimental import pallas as pl
from jax.experimental.pallas import tpu as pltpu
from jax.sharding import PartitionSpec as P

HEAD_DIM = 128
EXPERT = ("ey", "ec")
MESH_AXES = ("group", "ey", "ec")
MESH_IDS = pl.DeviceIdType.MESH
NBLK = 1
CTX = 2048


def norm_rows(inputs, gain_vector):
    values = inputs.astype(jnp.float32)
    factor = lax.rsqrt(jnp.mean(values * values, axis=-1, keepdims=True) + 1e-05)
    return (values * factor * gain_vector).astype(jnp.bfloat16)


def rotate(vectors, positions):
    half_dim = vectors.shape[-1] // 2
    frequency = 10000.0 ** (-jnp.arange(half_dim).astype(jnp.float32) / half_dim)
    angles = positions[:, None] * frequency[None, :]
    cosine = jnp.cos(angles)[:, None, :]
    sine_part = jnp.sin(angles)[:, None, :]
    first_half = vectors[..., :half_dim]
    second_half = vectors[..., half_dim:]
    return jnp.concatenate(
        [
            first_half * cosine - second_half * sine_part,
            first_half * sine_part + second_half * cosine,
        ],
        axis=-1,
    )


def attend_block(softmax_state, queries, key_block, value_block, key_valid):
    old_peak, old_total, old_mixed = softmax_state
    score_scale = queries.shape[-1] ** (-0.5)
    scores = (
        jnp.einsum("qhd,khd->hqk", queries, key_block, preferred_element_type=jnp.float32)
        * score_scale
    )
    scores = jnp.where(key_valid[None], scores, -1e30)
    new_peak = jnp.maximum(old_peak, jnp.max(scores, axis=-1))
    weights = jnp.exp(scores - new_peak[..., None])
    factor = jnp.exp(old_peak - new_peak)
    new_total = old_total * factor + jnp.sum(weights, axis=-1)
    new_mixed = old_mixed * factor[..., None] + jnp.einsum(
        "hqk,khd->hqd",
        weights.astype(jnp.bfloat16),
        value_block,
        preferred_element_type=jnp.float32,
    )
    return (new_peak, new_total, new_mixed)


def cache_pass(
    softmax_state,
    queries,
    all_keys,
    all_values,
    length,
    turn_count,
    array_step,
    array_first,
    position_step,
    position_first,
    block_len,
):

    def step_once(turn_index, running):
        array_start = (array_first + array_step * turn_index) * block_len
        position_start = (position_first + position_step * turn_index) * block_len
        key_block = lax.dynamic_slice_in_dim(all_keys, array_start, block_len, 0)
        value_block = lax.dynamic_slice_in_dim(all_values, array_start, block_len, 0)
        key_valid = (position_start + jnp.arange(block_len, dtype=jnp.int32) < length)[None, :]
        return attend_block(running, queries, key_block, value_block, key_valid)

    return lax.fori_loop(0, turn_count, step_once, softmax_state)


def exchange_kernel(axes, split, x_ref, o_ref, send_sems, recv_sems, own_sem):
    sizes = [lax.axis_size(a) for a in axes]
    count = 1
    for size in sizes:
        count *= size
    me = 0
    for a, size in zip(axes, sizes):
        me = me * size + lax.axis_index(a)

    def device_of(peer):
        coords = {}
        rest = peer
        for a, size in reversed(list(zip(axes, sizes))):
            coords[a] = rest % size
            rest = rest // size
        return tuple(coords.get(a, lax.axis_index(a)) for a in MESH_AXES)

    barrier = pltpu.get_barrier_semaphore()
    for k in range(1, count):
        pl.semaphore_signal(
            barrier, inc=1, device_id=device_of((me + k) % count), device_id_type=MESH_IDS
        )
    pl.semaphore_wait(barrier, count - 1)
    def block(ref, index):
        return ref.at[index] if split == 0 else ref.at[:, index]

    own = pltpu.make_async_copy(block(x_ref, me), block(o_ref, me), own_sem)
    own.start()
    copies = []
    for k in range(1, count):
        peer = (me + k) % count
        copy = pltpu.make_async_remote_copy(
            src_ref=block(x_ref, peer),
            dst_ref=block(o_ref, me),
            send_sem=send_sems.at[k],
            recv_sem=recv_sems.at[k],
            device_id=device_of(peer),
            device_id_type=MESH_IDS,
        )
        copy.start()
        copies.append(copy)
    own.wait()
    for copy in copies:
        copy.wait()


def exchange(x, axes, ident, split=0):
    count = x.shape[split]
    return pl.pallas_call(
        functools.partial(exchange_kernel, axes, split),
        out_shape=jax.ShapeDtypeStruct(x.shape, x.dtype),
        in_specs=[pl.BlockSpec(memory_space=pl.ANY)],
        out_specs=pl.BlockSpec(memory_space=pl.ANY),
        scratch_shapes=[
            pltpu.SemaphoreType.DMA((count,)),
            pltpu.SemaphoreType.DMA((count,)),
            pltpu.SemaphoreType.DMA(()),
        ],
        compiler_params=pltpu.CompilerParams(collective_id=ident, has_side_effects=True),
    )(x)


def attention_kernel(
    slots_ref, len_ref, q_ref, nk_ref, nv_ref, arr_ref, o_ref, kbuf, vbuf, m_sc, l_sc, acc_sc
):
    head = pl.program_id(0)
    rows, width = q_ref.shape
    page = arr_ref.shape[2]
    block_len = kbuf.shape[0]
    pages_per_block = block_len // page
    score_scale = width ** (-0.5)
    lanes = pl.ds(pl.multiple_of(head * width, width), width)
    q = q_ref[...]
    dims = (((1,), (1,)), ((), ()))
    scores = lax.dot_general(q, nk_ref[...], dims, preferred_element_type=jnp.float32) * score_scale
    row_i = lax.broadcasted_iota(jnp.int32, (rows, rows), 0)
    col_i = lax.broadcasted_iota(jnp.int32, (rows, rows), 1)
    scores = jnp.where(col_i <= row_i, scores, -1e30)
    peak = jnp.max(scores, axis=-1, keepdims=True)
    weights = jnp.exp(scores - peak)
    m_sc[...] = peak
    l_sc[...] = jnp.sum(weights, axis=-1, keepdims=True)
    acc_sc[...] = jnp.dot(weights.astype(jnp.bfloat16), nv_ref[...], preferred_element_type=jnp.float32)
    length = len_ref[0]
    block_count = (length + block_len - 1) // block_len

    def one_block(b, carry):
        for i in range(pages_per_block):
            slot = slots_ref[b * pages_per_block + i]
            kbuf[pl.ds(i * page, page), :] = arr_ref[slot, 0, :, lanes]
            vbuf[pl.ds(i * page, page), :] = arr_ref[slot, 1, :, lanes]
        block_scores = (
            lax.dot_general(q, kbuf[...], dims, preferred_element_type=jnp.float32) * score_scale
        )
        position = b * block_len + lax.broadcasted_iota(jnp.int32, (rows, block_len), 1)
        block_scores = jnp.where(position < length, block_scores, -1e30)
        old_peak = m_sc[...]
        new_peak = jnp.maximum(old_peak, jnp.max(block_scores, axis=-1, keepdims=True))
        block_weights = jnp.exp(block_scores - new_peak)
        factor = jnp.exp(old_peak - new_peak)
        l_sc[...] = l_sc[...] * factor + jnp.sum(block_weights, axis=-1, keepdims=True)
        acc_sc[...] = acc_sc[...] * factor + jnp.dot(
            block_weights.astype(jnp.bfloat16), vbuf[...], preferred_element_type=jnp.float32
        )
        m_sc[...] = new_peak
        return carry

    lax.fori_loop(0, block_count, one_block, 0)
    o_ref[...] = (acc_sc[...] / l_sc[...]).astype(o_ref.dtype)


def paged_attention(slots, length, queries, new_keys, new_values, arrived, block_len):
    rows, local_width = queries.shape
    heads = local_width // HEAD_DIM
    slot_count, _, page, _ = arrived.shape
    column = lambda h, *_: (0, h)
    spec = pl.BlockSpec((rows, HEAD_DIM), column)
    cost = pl.CostEstimate(
        flops=4 * rows * (rows + CTX) * local_width,
        transcendentals=rows * (rows + CTX) * heads,
        bytes_accessed=arrived.size * 2 + 4 * rows * local_width * 2,
    )
    return pl.pallas_call(
        attention_kernel,
        out_shape=jax.ShapeDtypeStruct((rows, local_width), jnp.bfloat16),
        grid_spec=pltpu.PrefetchScalarGridSpec(
            num_scalar_prefetch=2,
            grid=(heads,),
            in_specs=[
                spec,
                spec,
                spec,
                pl.BlockSpec(arrived.shape, lambda h, *_: (0, 0, 0, 0)),
            ],
            out_specs=spec,
            scratch_shapes=[
                pltpu.VMEM((block_len, HEAD_DIM), jnp.bfloat16),
                pltpu.VMEM((block_len, HEAD_DIM), jnp.bfloat16),
                pltpu.VMEM((rows, 1), jnp.float32),
                pltpu.VMEM((rows, 1), jnp.float32),
                pltpu.VMEM((rows, HEAD_DIM), jnp.float32),
            ],
        ),
        compiler_params=pltpu.CompilerParams(vmem_limit_bytes=48 * 1024 * 1024),
        cost_estimate=cost,
    )(slots, length, queries, new_keys, new_values, arrived)


def shards(
    hidden_in,
    cache_len,
    page_table,
    pool,
    attn_gain,
    w_qkv,
    w_out,
    moe_gain,
    w_gate,
    w_up,
    w_down,
    expert_ids,
    gate_weights,
):
    groups = lax.axis_size("group")
    expert_lanes = lax.axis_size(EXPERT)
    group_index = lax.axis_index("group")
    tok_rows = hidden_in.shape[0]
    model_width = hidden_in.shape[1]
    local_width = w_out.shape[0]
    head_size = HEAD_DIM
    local_heads = local_width // head_size
    new_count = tok_rows * expert_lanes
    block_len = CTX // NBLK
    length = cache_len[group_index]
    normed = norm_rows(hidden_in, attn_gain)
    projection = w_qkv.reshape(model_width, 3 * local_width)
    projected = jnp.dot(
        lax.all_gather(normed, EXPERT, axis=0, tiled=True),
        projection,
        preferred_element_type=jnp.float32,
    )
    projected = projected.reshape(new_count, 3, local_heads, head_size)
    positions = (length + jnp.arange(new_count, dtype=jnp.int32)).astype(jnp.float32)
    queries = rotate(projected[:, 0], positions).astype(jnp.bfloat16)
    new_keys = rotate(projected[:, 1], positions).astype(jnp.bfloat16)
    new_values = projected[:, 2].astype(jnp.bfloat16)
    pages_per = page_table.shape[1]
    page_most = max(1, pages_per // min(groups, 16))
    owner_group = page_table // pages_per
    local_slot = page_table % pages_per
    page_order = jnp.arange(pages_per, dtype=jnp.int32)
    mine = (owner_group == group_index).astype(jnp.int32)
    mine_rank = jnp.cumsum(mine, axis=1) - mine
    slot_ids = jnp.arange(page_most, dtype=jnp.int32)
    pick = (mine[:, None, :] > 0) & (mine_rank[:, None, :] == slot_ids[None, :, None])
    send_index = jnp.sum(jnp.where(pick, local_slot[:, None, :], 0), axis=-1)
    outgoing = pool[send_index]
    arrived = lax.all_to_all(outgoing, "group", split_axis=0, concat_axis=0, tiled=True)
    arrived = arrived.reshape((groups * page_most,) + pool.shape[1:])
    my_owner = owner_group[group_index]
    before = page_order[None, :] < page_order[:, None]
    my_rank = jnp.sum(jnp.logical_and(my_owner[:, None] == my_owner[None, :], before), axis=-1)
    slots = (my_owner * page_most + my_rank).astype(jnp.int32)
    attended = paged_attention(
        slots,
        jnp.reshape(length, (1,)).astype(jnp.int32),
        queries.reshape(new_count, local_width),
        new_keys.reshape(new_count, local_width),
        new_values.reshape(new_count, local_width),
        arrived,
        block_len,
    )
    head_weights = lax.all_gather(w_out, EXPERT, axis=0, tiled=True)
    head_weights = head_weights.reshape(expert_lanes, local_width, model_width)
    rows_piece = exchange(attended.reshape(expert_lanes, tok_rows, local_width), EXPERT, 2)
    head_parts = jnp.einsum(
        "gtc,gcd->gtd", rows_piece, head_weights, preferred_element_type=jnp.float32
    ).astype(jnp.bfloat16)
    head_sum = jnp.sum(head_parts.astype(jnp.float32), axis=0)
    residual = hidden_in.astype(jnp.float32) + head_sum
    moe_in = norm_rows(residual, moe_gain)
    route_count = expert_ids.shape[1]
    capacity = 2 * tok_rows * route_count // expert_lanes
    flat_expert = expert_ids.reshape(-1)
    assign_index = jnp.arange(flat_expert.shape[0], dtype=jnp.int32)
    earlier = assign_index[None, :] < assign_index[:, None]
    slot_index = jnp.sum(
        jnp.logical_and(flat_expert[:, None] == flat_expert[None, :], earlier), axis=-1
    )
    token_of = assign_index // route_count
    slot_of = flat_expert * capacity + slot_index
    dest_ids = jnp.arange(expert_lanes * capacity, dtype=jnp.int32)
    token_ids = jnp.arange(tok_rows, dtype=jnp.int32)
    hit = (slot_of[None, :] == dest_ids[:, None])
    source_token = jnp.sum(jnp.where(hit, token_of[None, :], 0), axis=-1)
    has_source = jnp.any(hit, axis=-1)
    select = ((source_token[:, None] == token_ids[None, :]) & has_source[:, None]).astype(jnp.bfloat16)
    outgoing_rows = (
        jnp.dot(select, moe_in, preferred_element_type=jnp.float32)
        .astype(jnp.bfloat16)
        .reshape(expert_lanes, capacity, model_width)
    )
    rows_piece = exchange(outgoing_rows, EXPERT, 0)
    flat_rows = rows_piece.reshape(-1, rows_piece.shape[-1])
    gate_part = jnp.dot(flat_rows, w_gate[0], preferred_element_type=jnp.float32)
    up_part = jnp.dot(flat_rows, w_up[0], preferred_element_type=jnp.float32)
    hidden = (jax.nn.silu(gate_part) * up_part).astype(jnp.bfloat16)
    result = (
        jnp.dot(hidden, w_down[0], preferred_element_type=jnp.float32)
        .astype(jnp.bfloat16)
        .reshape(rows_piece.shape)
    )
    returned = exchange(result, EXPERT, 1)
    flat_returned = returned.reshape(expert_lanes * capacity, model_width)
    slot_pair = (flat_expert * capacity + slot_index).reshape(tok_rows, route_count)
    weighted = flat_returned[slot_pair[:, 0]].astype(jnp.float32) * gate_weights[:, 0:1]
    for k in range(1, route_count):
        weighted = weighted + flat_returned[slot_pair[:, k]].astype(jnp.float32) * gate_weights[:, k : k + 1]
    return residual + weighted


def solution(mesh):
    lanes = mesh.shape["expert"]
    cores = 2 if lanes % 2 == 0 else 1
    split = jax.sharding.Mesh(
        mesh.devices.reshape(mesh.shape["group"], lanes // cores, cores), ("group",) + EXPERT
    )
    rows = ("group",) + EXPERT
    placed = (
        P(rows, None),
        P(),
        P(),
        P("group", None, None, EXPERT),
        P(),
        P(None, None, EXPERT),
        P(EXPERT, None),
        P(),
        P(EXPERT, None, None),
        P(EXPERT, None, None),
        P(EXPERT, None, None),
        P(rows, None),
        P(rows, None),
    )
    return jax.shard_map(
        shards, mesh=split, in_specs=placed, out_specs=P(rows, None), check_vma=False
    )
```
